32 devices in a mesh: shard: 2 (over x), ctx: 4 (over y, core), tp: 4 (over z).
Axes of the slice: x: 2, y: 2, z: 4, core: 2. Of those that a mesh axis runs over, the one named last changes fastest.
Arguments:
- tokens: bfloat16 [4, 2048, 1536], P('shard', 'ctx'), may hold values from -6 to 6
- segments: int32 [4, 2048], P('shard', 'ctx'), may hold values from 0 to 15, never falling along the last dimension, each value on 1 to 800 neighbouring positions
- norm_gain: bfloat16 [1536], P('shard'), may hold values from 0.5 to 1.5
- ffn_gain: bfloat16 [1536], P('shard'), may hold values from 0.5 to 1.5
- memory_gain: bfloat16 [16, 96], P('tp', 'shard'), may hold values from 0.5 to 1.5
- memory_rates: bfloat16 [2, 6144], P('shard'), may hold values from 0.19921875 to 0.9765625
- persistent: bfloat16 [64, 1536], P(None, 'shard'), may hold values from -6 to 6
- w_qkv: bfloat16 [3, 1536, 1536], P(None, 'shard', 'tp'), may hold values from -0.15625 to 0.15625
- w_out: bfloat16 [1536, 1536], P('tp', 'shard'), may hold values from -0.625 to 0.625
- w_value: bfloat16 [1536, 1536], P('shard', 'tp'), may hold values from -0.15625 to 0.15625
- w_feature: bfloat16 [1536, 6144], P('shard', 'tp'), may hold values from -0.15625 to 0.15625
- w_gate_up: bfloat16 [2, 1536, 4096], P(None, 'shard', 'tp'), may hold values from -0.15625 to 0.15625
- w_down: bfloat16 [4096, 1536], P('tp', 'shard'), may hold values from -0.09375 to 0.09375
- out_grad: bfloat16 [4, 2048, 1536], P('shard', 'ctx'), may hold values from -6 to 6
Outputs:
- output: bfloat16 [4, 2048, 1536], P('shard', 'ctx')
- input_grad: float32 [4, 2048, 1536], P('shard', 'ctx')
- grad_norm_gain: float32 [1536], P('shard')
- grad_ffn_gain: float32 [1536], P('shard')
- grad_memory_gain: float32 [16, 96], P('tp', 'shard')
- grad_memory_rates: float32 [2, 6144], P('shard', 'tp')
- grad_persistent: float32 [64, 1536], P(None, 'shard')
- grad_w_qkv: float32 [3, 1536, 1536], P(None, 'shard', 'tp')
- grad_w_out: float32 [1536, 1536], P('tp', 'shard')
- grad_w_value: float32 [1536, 1536], P('shard', 'tp')
- grad_w_feature: float32 [1536, 6144], P('shard', 'tp')
- grad_w_gate_up: float32 [2, 1536, 4096], P(None, 'shard', 'tp')
- grad_w_down: float32 [4096, 1536], P('tp', 'shard')
The draws below stay inside these ranges and needn't reach their ends.
Inputs may be any that keep to these rules, and one draw needn't show every extreme that they name: `segments`: along each sequence the document numbers never fall; a document holds 1 to 800 positions, one exactly that many.
All inputs are finite; a program needn't handle non-finite values.
Results may differ from the reference program's by a relative error of at most 0.02.
Values may be sent and summed in bfloat16 or wider, within the bound.
A program may use at most 512 MiB of HBM per device.

```python
import math
import jax
import jax.numpy as jnp
import numpy as np
from jax import lax

D = 1536
HEADS = 16
HD = 96
PERSIST = 64
FF = 6144
FFN = 4096
SPAN = 256
LENGTH = 2048
SEQS = 4


def steps_of(own_key, dims, cuts, least, largest):
    def one(dim, shards_of):
        steps = jax.random.uniform(jax.random.fold_in(jax.random.fold_in(own_key, 6), dim), (shards_of,), jnp.float32, least / len(cuts), largest / len(cuts))
        return jnp.repeat(jnp.exp(steps), dims[dim] // shards_of).reshape((-1,) + (1,) * (len(dims) - dim - 1))

    factor_of = one(*cuts[0])
    for cut in cuts[1:]:
        factor_of = factor_of * one(*cut)
    return factor_of


def split_up(amount, total, limit, skew):
    weights = [(1 << 20) // math.isqrt(standing ** skew) + 1 for standing in range(2, amount + 1)]
    spare, counts = total - limit - (amount - 1), [1] * (amount - 1)
    while spare > 0:
        candidates = [i for i in range(amount - 1) if counts[i] < limit]
        whole, left = sum([weights[i] for i in candidates]), spare
        for i in candidates:
            extra = min(limit - counts[i], max(1, left * weights[i] // whole), spare)
            counts[i] = counts[i] + extra
            spare = spare - extra
    return np.array([limit] + counts)


def uneven_parts(key, number_of, total, reach, lean):
    if number_of == 2:
        one = jax.random.randint(key, (), max(1, total - reach), min(reach, total - 1) + 1)
        return jnp.stack([one, total - one])
    sizes = jnp.asarray(split_up(number_of, total, reach, lean), jnp.int32)
    couples = (number_of - 1) // 2
    giver, sink = sizes[1:1 + 2 * couples:2], sizes[2:2 + 2 * couples:2]
    slack = jnp.minimum(giver - 1, reach - sink)
    moved = jax.random.randint(jax.random.fold_in(key, 1), (couples,), 0, 1 << 20) % (slack + 1)
    sizes = sizes.at[1:1 + 2 * couples:2].set(giver - moved).at[2:2 + 2 * couples:2].set(sink + moved)
    return sizes[jax.random.permutation(jax.random.fold_in(key, 2), number_of)]


def noise(own_key, extent, scale, limit, cuts=(), kind=jnp.bfloat16):
    array = jax.random.normal(own_key, extent, jnp.float32) * scale
    if len(cuts) > 0:
        array = steps_of(own_key, extent, cuts, -0.22, 0.18) * array
    return jnp.clip(array, min=-limit, max=limit).astype(kind)


def setup_inputs(seed: int = 0) -> dict:
    key_of = jax.random.split(jax.random.key(seed), 15)
    return {
        "tokens": noise(key_of[0], (SEQS, LENGTH, D), 1.0, 6.0, ((0, 2), (1, 4))),
        "segments": jax.vmap(lambda own: jnp.searchsorted(jnp.cumsum(uneven_parts(own, max(4, LENGTH // 128), LENGTH, LENGTH * 25 // 64, 1)), jnp.arange(LENGTH), side="right"))(jax.random.split(key_of[1], SEQS)).reshape((SEQS, LENGTH)).astype(jnp.int32),
        "norm_gain": jnp.clip(1.0 + 0.1 * jax.random.normal(key_of[2], (D,), jnp.float32), 0.5, 1.5).astype(jnp.bfloat16),
        "ffn_gain": jnp.clip(1.0 + 0.1 * jax.random.normal(key_of[3], (D,), jnp.float32), 0.5, 1.5).astype(jnp.bfloat16),
        "memory_gain": jnp.clip(1.0 + 0.1 * jax.random.normal(key_of[4], (HEADS, HD), jnp.float32), 0.5, 1.5).astype(jnp.bfloat16),
        "memory_rates": jnp.clip(jnp.exp(math.log(0.9765625) - 1.5896353 * jax.random.uniform(key_of[5], (2, FF), jnp.float32) ** steps_of(key_of[5], (2, FF), ((0, 2),), -0.2, 0.2)), 0.19921875, 0.9765625).astype(jnp.bfloat16),
        "persistent": noise(key_of[6], (PERSIST, D), 1.0, 6.0, ((1, 2),)),
        "w_qkv": noise(key_of[7], (3, D, D), D ** -0.5, 0.15625, ((1, 2), (2, 4))),
        "w_out": noise(key_of[8], (D, D), HD ** -0.5, 0.625, ((0, 4), (1, 2))),
        "w_value": noise(key_of[9], (D, D), D ** -0.5, 0.15625, ((0, 2), (1, 4))),
        "w_feature": noise(key_of[10], (D, FF), D ** -0.5, 0.15625, ((0, 2), (1, 4))),
        "w_gate_up": noise(key_of[11], (2, D, FFN), D ** -0.5, 0.15625, ((1, 2), (2, 4))),
        "w_down": noise(key_of[12], (FFN, D), FFN ** -0.5, 0.09375, ((0, 4), (1, 2))),
        "out_grad": noise(key_of[13], (SEQS, LENGTH, D), 1.0, 6.0, ((0, 2), (1, 4))),
    }


EPSILON = 1e-06
MASKED = -1e+30
HIGHEST = lax.Precision.HIGHEST

@jax.custom_vjp
def low(v):
    return lax.optimization_barrier(v.astype(jnp.bfloat16)).astype(jnp.float32)

@jax.custom_vjp
def low_back(v):
    return v

def low_keep(v):
    return (low(v), None)

def low_pass(kept, grad):
    return (grad,)

def back_keep(v):
    return (v, None)

def back_low(kept, grad):
    return (low(grad),)
low.defvjp(low_keep, low_pass)
low_back.defvjp(back_keep, back_low)

def both_ways(values):
    return low(low_back(values))

def matmul(left, right):
    return jnp.dot(left, right, precision=HIGHEST, preferred_element_type=jnp.float32)

def norm_rows(values, gain):
    return values * lax.rsqrt(lax.optimization_barrier(jnp.mean(values * values, axis=-1, keepdims=True)) + EPSILON) * gain

def sequence_pass(weights, tokens, segments):
    gain_in, gain_ffn, gain_memory, rates, persist, qkv, w_out, w_value, w_feature, gate_up, w_down = weights
    length = tokens.shape[0]
    count = length // SPAN
    step = 6.0 / (SPAN + 8)
    scale = HD ** (-0.5)
    input_low = low(norm_rows(tokens, gain_in))
    preact = low_back(matmul(input_low, w_feature))
    features = low(jax.nn.silu(preact))
    key_scale = lax.rsqrt(lax.optimization_barrier(jnp.sum(features * features, axis=-1)) + EPSILON)
    targets = low_back(matmul(input_low, w_value))
    labels = segments.astype(jnp.float32).reshape(count, SPAN) + 1.0
    lasts = labels[:, -1]
    before = jnp.concatenate([jnp.zeros((1,), jnp.float32), lasts[:-1]])
    keeping = (lasts == before).astype(jnp.float32)
    writing = (labels == lasts[:, None]).astype(jnp.float32)
    reading = (labels == before[:, None]).astype(jnp.float32)
    retain = rates[0]
    moment = rates[1]

    def advance(carry, inputs):
        memory, velocity = carry
        span_feat, span_scale, span_target, span_write, span_keep = inputs
        recall = span_scale[:, None] * low_back(matmul(span_feat, low(memory)))
        error = span_write[:, None] * (span_keep * recall - span_target)
        update = low_back(matmul(span_feat.T, low(span_scale[:, None] * error)))
        velocity = span_keep * moment[:, None] * velocity - step * update
        memory = span_keep * retain[:, None] * memory + velocity
        return ((memory, velocity), recall)
    empty = jnp.zeros((FF, D), jnp.float32)
    _, recalls = lax.scan(advance, (empty, empty), (features.reshape(count, SPAN, FF), key_scale.reshape(count, SPAN), targets.reshape(count, SPAN, D), writing, keeping))
    masked = (recalls * reading[:, :, None]).reshape(length, HEADS, HD)
    normed = masked * lax.rsqrt(lax.optimization_barrier(jnp.mean(masked * masked, axis=-1, keepdims=True)) + EPSILON) * gain_memory
    retrieved = low(normed.reshape(length, D))

    def heads(values):
        return values.reshape(count, SPAN, HEADS, HD)
    queries = heads(both_ways(matmul(input_low, qkv[0])))
    fixed_keys = low(matmul(persist, qkv[1])).reshape(1, PERSIST, HEADS, HD)
    fixed_values = low(matmul(persist, qkv[2])).reshape(1, PERSIST, HEADS, HD)
    keys = jnp.concatenate([jnp.broadcast_to(fixed_keys, (count, PERSIST, HEADS, HD)), heads(both_ways(matmul(retrieved, qkv[1]))), heads(both_ways(matmul(input_low, qkv[1])))], axis=1)
    values = jnp.concatenate([jnp.broadcast_to(fixed_values, (count, PERSIST, HEADS, HD)), heads(both_ways(matmul(retrieved, qkv[2]))), heads(both_ways(matmul(input_low, qkv[2])))], axis=1)
    position = jnp.arange(SPAN)
    causal = position[:, None] >= position[None, :]
    same_doc = labels[:, :, None] == labels[:, None, :]
    visible_own = causal[None] & same_doc
    visible_memory = visible_own & (reading[:, None, :] > 0.5)
    visible = jnp.concatenate([jnp.ones((count, SPAN, PERSIST), jnp.bool_), visible_memory, visible_own], axis=2)
    raw = jnp.einsum('bthd,bkhd->bhtk', queries, keys, precision=HIGHEST)
    scores = jnp.where(visible[:, None], low_back(raw * scale), MASKED)
    probs = jax.nn.softmax(scores, axis=-1)
    attended = both_ways(jnp.einsum('bhtk,bkhd->bthd', low(probs), values, precision=HIGHEST)).reshape(length, D)
    hidden = tokens + low_back(matmul(attended, w_out))
    mid_low = low(norm_rows(hidden, gain_ffn))
    gate = low_back(matmul(mid_low, gate_up[0]))
    upper = low_back(matmul(mid_low, gate_up[1]))
    activ = low(jax.nn.silu(gate) * upper)
    return hidden + matmul(activ, w_down)

def reference(tokens, segments, norm_gain, ffn_gain, memory_gain, memory_rates, persistent, w_qkv, w_out, w_value, w_feature, w_gate_up, w_down, out_grad):
    weights = (norm_gain, ffn_gain, memory_gain, memory_rates, persistent, w_qkv, w_out, w_value, w_feature, w_gate_up, w_down)
    weights = tuple((item.astype(jnp.float32) for item in weights))
    inputs = tokens.astype(jnp.float32)

    def forward(values, *params):

        def each(carry, pieces):
            return (carry, jax.checkpoint(sequence_pass)(params, pieces[0], pieces[1]))
        return lax.scan(each, jnp.zeros((), jnp.float32), (values, segments))[1]
    result, pullback = jax.vjp(forward, inputs, *weights)
    grads = pullback(out_grad.astype(jnp.float32))
    return (result.astype(jnp.bfloat16), grads[0], grads[1], grads[2], grads[3], grads[4], grads[5], grads[6], grads[7], grads[8], grads[9], grads[10], grads[11])
```

```python
import jax
import jax.numpy as jnp
from jax import lax
from jax.sharding import PartitionSpec as P

HD = 96
SPAN = 256
LIMIT = 800
LAGS = (LIMIT + SPAN - 2) // SPAN


EPSILON = 1e-06
MASKED = -1e30
WIDE = jnp.float32
NARROW = jnp.bfloat16


def passed_along(value, axis, steps):
    count = lax.axis_size(axis)
    initial, last = (max(0, -steps), min(count, count - steps))
    return lax.ppermute(value, axis, [(source, source + steps) for source in range(initial, last)])


def norm_rows(values, gain):
    factor = lax.rsqrt(jnp.mean(values * values, axis=-1, keepdims=True) + EPSILON)
    normed = values * factor
    return (normed * gain, normed, factor)


def norm_back(upstream, normed, factor, gain):
    inner = upstream * gain
    return factor * (inner - normed * jnp.mean(inner * normed, axis=-1, keepdims=True))


def silu_slope(values):
    sigmoid = jax.nn.sigmoid(values)
    return sigmoid * (1.0 + values * (1.0 - sigmoid))


def matmul(left, right):
    return jnp.dot(left, right, preferred_element_type=WIDE)


def over_rows(left, right):
    return lax.dot_general(left, right, (((0,), (0,)), ((), ())), preferred_element_type=WIDE)


def by_rows(left, right):
    return lax.dot_general(left, right, (((1,), (1,)), ((), ())), preferred_element_type=WIDE)


def exact_product(left, right):
    return jnp.dot(left, right, precision=lax.Precision.HIGHEST, preferred_element_type=WIDE)


def batched(spec, left, right):
    return jnp.einsum(spec, left, right, preferred_element_type=WIDE)


def on_device(
    tokens,
    segments,
    norm_gain,
    ffn_gain,
    memory_gain,
    memory_rates,
    persistent,
    w_qkv,
    w_out,
    w_value,
    w_feature,
    w_gate_up,
    w_down,
    out_grad,
):
    def whole(array, axis):
        return lax.all_gather(array, "shard", axis=axis, tiled=True)

    feature_cols = whole(w_feature, 0)
    value_cols = whole(w_value, 0)
    qkv_cols = whole(w_qkv, 1)
    out_rows = whole(w_out, 1)
    gate_up_cols = whole(w_gate_up, 1)
    down_rows = whole(w_down, 1)
    persist = whole(persistent, 1)
    gain_in_wide = whole(norm_gain, 0).astype(WIDE)
    gain_ffn_wide = whole(ffn_gain, 0).astype(WIDE)
    gain_mem = whole(memory_gain, 1).astype(WIDE)
    rates = whole(memory_rates, 0)

    groups, local_len, width = tokens.shape
    rows = groups * local_len
    blocks_each = local_len // SPAN
    blocks = groups * blocks_each
    local_width = qkv_cols.shape[2]
    local_units = feature_cols.shape[1]
    local_heads = local_width // HD
    persist_count = persist.shape[0]
    parts, ranks = (lax.axis_size("ctx"), lax.axis_size("tp"))
    part, rank = (lax.axis_index("ctx"), lax.axis_index("tp"))
    total_blocks = parts * blocks_each
    reach = -(-LAGS // blocks_each)
    step = 6.0 / (SPAN + 8)
    scale = HD ** (-0.5)
    sub = rows // ranks

    def own_rows(array):
        return lax.dynamic_slice_in_dim(array, rank * sub, sub, 0)

    def scattered(array):
        return lax.psum_scatter(
            array.astype(NARROW), "tp", scatter_dimension=0, tiled=True
        ).astype(WIDE)

    def collected(array):
        return lax.all_gather(array.astype(NARROW), "tp", axis=0, tiled=True)

    flat_tokens = tokens.reshape(rows, width)
    all_tokens = lax.all_gather(tokens, "ctx", axis=1, tiled=True)
    all_labels = lax.all_gather(segments, "ctx", axis=1, tiled=True).astype(WIDE) + 1.0
    block_lasts = all_labels.reshape(groups, total_blocks, SPAN)[:, :, -1]
    own_units = lax.dynamic_slice_in_dim(rates.astype(WIDE), rank * local_units, local_units, 1)
    retain, moment = (own_units[0], own_units[1])
    decays = [jnp.ones_like(retain)]
    for lag in range(1, LAGS):
        decays.append(retain * decays[-1] + moment**lag)

    input_low = norm_rows(flat_tokens.astype(WIDE), gain_in_wide)[0].astype(NARROW)
    preact = matmul(input_low, feature_cols)
    features = jax.nn.silu(preact).astype(NARROW)
    all_low = norm_rows(
        all_tokens.reshape(groups * parts * local_len, width).astype(WIDE), gain_in_wide
    )[0].astype(NARROW)
    all_features = (
        jax.nn.silu(matmul(all_low, feature_cols))
        .astype(NARROW)
        .reshape(groups, total_blocks, SPAN, local_units)
    )
    squares = jnp.sum(jnp.square(features.astype(WIDE)), axis=1)
    key_scale = lax.rsqrt(lax.psum(squares, "tp") + EPSILON)
    scales = key_scale.reshape(groups, blocks_each, SPAN, 1)
    targets = matmul(input_low, value_cols).reshape(groups, blocks_each, SPAN, local_width)
    first = part * blocks_each

    def block_of(index):
        return lax.dynamic_index_in_dim(
            all_features, jnp.clip(index, 0, total_blocks - 1), 1, False
        )

    def last_of(index):
        found = lax.dynamic_index_in_dim(
            block_lasts, jnp.clip(index, 0, total_blocks - 1), 1, False
        )
        return jnp.where(index >= 0, found, 0.0)

    own_features = features.reshape(groups, blocks_each, SPAN, local_units)
    weighted = [
        (own_features.astype(WIDE) * decay).astype(NARROW) for decay in decays
    ]
    products = []
    linked = []
    for own in range(blocks_each):
        row = []
        links = []
        for lag in range(LAGS):
            source = first + own - 1 - lag
            row.append(batched("sth,suh->stu", weighted[lag][:, own], block_of(source)))
            links.append((source >= 0) & (last_of(source) == last_of(first + own - 1)))
        products.append(jnp.stack(row, axis=1))
        linked.append(jnp.stack(links, axis=1))
    products = jnp.stack(products, axis=1).astype(NARROW)
    linked = jnp.stack(linked, axis=1)
    mixing = lax.psum(products, "tp")
    mixing = jnp.where(linked[..., None, None], mixing, jnp.zeros_like(mixing))

    labels = segments.astype(WIDE).reshape(groups, blocks_each, SPAN) + 1.0
    lasts = labels[:, :, -1]
    before = jnp.stack([last_of(first + own - 1) for own in range(blocks_each)], axis=1)
    keeping = (lasts == before).astype(WIDE)[:, :, None, None]
    writing = (labels == lasts[:, :, None]).astype(WIDE)[..., None]
    reading = (labels == before[:, :, None]).astype(WIDE)

    halo = jnp.zeros((groups, reach * blocks_each, SPAN, local_width), NARROW)

    def advance(halo):
        known = [halo[:, index] for index in range(reach * blocks_each)]
        recalls = []
        errors = []
        for own in range(blocks_each):
            total = 0.0
            for lag in range(LAGS):
                total = total + batched(
                    "stu,sud->std", mixing[:, own, lag], known[reach * blocks_each + own - 1 - lag]
                )
            recall = -step * scales[:, own] * total
            error = writing[:, own] * (keeping[:, own] * recall - targets[:, own])
            recalls.append(recall)
            errors.append(error)
            known.append((scales[:, own] * error).astype(NARROW))
        return (jnp.stack(recalls, 1), jnp.stack(errors, 1), jnp.stack(known[-blocks_each:], 1))

    for turn in range(parts):
        recall_seq, errors, scaled_errors = advance(halo)
        if turn < parts - 1:
            halo = jnp.concatenate(
                [passed_along(scaled_errors, "ctx", hop) for hop in range(reach, 0, -1)], axis=1
            )

    heads_view = (reading[..., None] * recall_seq).reshape(rows, local_heads, HD)
    head_factor = lax.rsqrt(jnp.mean(heads_view * heads_view, axis=-1, keepdims=True) + EPSILON)
    head_unit = heads_view * head_factor
    retrieved = (head_unit * gain_mem).reshape(rows, local_width).astype(NARROW)
    retrieved_full = lax.all_gather(retrieved, "tp", axis=1, tiled=True)
    query_w = qkv_cols[0]
    key_w = qkv_cols[1]
    value_w = qkv_cols[2]

    def heads(values):
        return values.astype(NARROW).reshape(blocks, SPAN, local_heads, HD)

    def fixed(values):
        shaped = values.astype(NARROW).reshape(1, persist_count, local_heads, HD)
        return jnp.broadcast_to(shaped, (blocks, persist_count, local_heads, HD))

    queries = heads(matmul(input_low, query_w))
    keys = jnp.concatenate(
        [
            fixed(matmul(persist, key_w)),
            heads(matmul(retrieved_full, key_w)),
            heads(matmul(input_low, key_w)),
        ],
        axis=1,
    )
    values_all = jnp.concatenate(
        [
            fixed(matmul(persist, value_w)),
            heads(matmul(retrieved_full, value_w)),
            heads(matmul(input_low, value_w)),
        ],
        axis=1,
    )
    label_rows = labels.reshape(blocks, SPAN)
    read_rows = reading.reshape(blocks, SPAN)
    position = jnp.arange(SPAN)
    causal = position[:, None] >= position[None, :]
    visible_own = causal[None] & (label_rows[:, :, None] == label_rows[:, None, :])
    visible_memory = visible_own & (read_rows[:, None, :] > 0.5)
    visible = jnp.concatenate(
        [jnp.ones((blocks, SPAN, persist_count), jnp.bool_), visible_memory, visible_own], axis=2
    )

    def scores_of():
        raw = batched("bthd,bkhd->bhtk", queries, keys) * scale
        return jnp.where(visible[:, None], raw, MASKED)

    scores = scores_of()
    highest = jnp.max(scores, axis=-1, keepdims=True)
    raised = jnp.exp(scores - highest)
    totals = jnp.sum(raised, axis=-1, keepdims=True)
    logsum = highest + jnp.log(totals)
    probs_low = (raised / totals).astype(NARROW)
    attended = (
        batched("bhtk,bkhd->bthd", probs_low, values_all).astype(NARROW).reshape(rows, local_width)
    )
    residual = own_rows(flat_tokens).astype(WIDE)
    hidden = residual + scattered(matmul(attended, out_rows))
    normed_mid, unit_mid, factor_mid = norm_rows(hidden, gain_ffn_wide)
    mid_low = collected(normed_mid)
    gate = matmul(mid_low, gate_up_cols[0])
    upper = matmul(mid_low, gate_up_cols[1])
    activ = (jax.nn.silu(gate) * upper).astype(NARROW)
    branch = scattered(matmul(activ, down_rows))
    output = collected(hidden + branch).reshape(groups, local_len, width)
    upstream_low = out_grad.reshape(rows, width)
    upstream = own_rows(upstream_low).astype(WIDE)
    grad_down = over_rows(activ, upstream_low)
    grad_act = by_rows(upstream_low, down_rows)
    grad_gate = (grad_act * upper * silu_slope(gate)).astype(NARROW)
    grad_upper = (grad_act * jax.nn.silu(gate)).astype(NARROW)
    grad_gate_up = jnp.stack([over_rows(mid_low, grad_gate), over_rows(mid_low, grad_upper)])
    grad_mid = scattered(by_rows(grad_gate, gate_up_cols[0]) + by_rows(grad_upper, gate_up_cols[1]))
    grad_gain_ffn = jnp.sum(grad_mid * unit_mid, axis=0)
    grad_hidden = upstream + norm_back(grad_mid, unit_mid, factor_mid, gain_ffn_wide)
    grad_mixed = collected(grad_hidden)
    grad_out_rows = over_rows(attended, grad_mixed)
    grad_attended = (
        by_rows(grad_mixed, out_rows).astype(NARROW).reshape(blocks, SPAN, local_heads, HD)
    )
    probs = jnp.exp(scores_of() - logsum)
    grad_probs = batched("bthd,bkhd->bhtk", grad_attended, values_all)
    grad_values = batched("bhtk,bthd->bkhd", probs.astype(NARROW), grad_attended)
    grad_scores = (
        probs * (grad_probs - jnp.sum(grad_probs * probs, axis=-1, keepdims=True))
    ).astype(NARROW)
    grad_queries = (
        (batched("bhtk,bkhd->bthd", grad_scores, keys) * scale)
        .astype(NARROW)
        .reshape(rows, local_width)
    )
    grad_keys = batched("bhtk,bthd->bkhd", grad_scores, queries) * scale

    def split_keys(grads):
        fixed_part = jnp.sum(grads[:, :persist_count], axis=0).reshape(persist_count, local_width)
        memory_part = (
            grads[:, persist_count : persist_count + SPAN].astype(NARROW).reshape(rows, local_width)
        )
        token_part = grads[:, persist_count + SPAN :].astype(NARROW).reshape(rows, local_width)
        return (fixed_part, memory_part, token_part)

    key_fixed, key_memory, key_token = split_keys(grad_keys)
    value_fixed, value_memory, value_token = split_keys(grad_values)
    persist_wide = persist.astype(WIDE)
    grad_query_w = over_rows(input_low, grad_queries)
    grad_key_w = (
        over_rows(input_low, key_token)
        + over_rows(retrieved_full, key_memory)
        + exact_product(persist_wide.T, key_fixed)
    )
    grad_value_proj = (
        over_rows(input_low, value_token)
        + over_rows(retrieved_full, value_memory)
        + exact_product(persist_wide.T, value_fixed)
    )
    grad_qkv = jnp.stack([grad_query_w, grad_key_w, grad_value_proj])
    grad_persist = exact_product(key_fixed, key_w.astype(WIDE).T) + exact_product(
        value_fixed, value_w.astype(WIDE).T
    )
    grad_input = (
        by_rows(grad_queries, query_w) + by_rows(key_token, key_w) + by_rows(value_token, value_w)
    )
    grad_retrieved = lax.psum_scatter(
        (by_rows(key_memory, key_w) + by_rows(value_memory, value_w)).astype(NARROW),
        "tp",
        scatter_dimension=1,
        tiled=True,
    ).astype(WIDE)
    grad_heads = grad_retrieved.reshape(rows, local_heads, HD)
    grad_gain_memory = jnp.sum(grad_heads * head_unit, axis=0)
    inner = grad_heads * gain_mem
    grad_masked = head_factor * (
        inner - head_unit * jnp.mean(inner * head_unit, axis=-1, keepdims=True)
    )
    grad_read = reading[..., None] * grad_masked.reshape(groups, blocks_each, SPAN, local_width)

    def retreat(later):
        known = [later[:, index] for index in range(blocks_each)]
        known = known[:0] + [0.0] * (reach * blocks_each) + known
        grad_errors = [None] * blocks_each
        grad_recalls = [None] * blocks_each
        raws = [None] * blocks_each
        for own in range(blocks_each - 1, -1, -1):
            grad_scaled = -step * known[reach * blocks_each + own]
            grad_error = scales[:, own] * grad_scaled
            grad_recall = grad_read[:, own] + writing[:, own] * keeping[:, own] * grad_error
            raw = (scales[:, own] * grad_recall).astype(NARROW)
            grad_errors[own] = grad_error
            grad_recalls[own] = grad_recall
            raws[own] = raw
            for lag in range(LAGS):
                place = reach * blocks_each + own - 1 - lag
                known[place] = known[place] + batched("stu,std->sud", mixing[:, own, lag], raw)
        sent = jnp.stack(known[: reach * blocks_each], 1).astype(NARROW)
        return (jnp.stack(grad_errors, 1), jnp.stack(grad_recalls, 1), jnp.stack(raws, 1), sent)

    later = jnp.zeros((groups, blocks_each, SPAN, local_width), WIDE)
    for turn in range(parts):
        grad_errors, grad_recalls, raws, sent = retreat(later)
        if turn < parts - 1:
            later = 0.0
            for hop in range(1, reach + 1):
                start = (reach - hop) * blocks_each
                later = later + passed_along(
                    sent[:, start : start + blocks_each], "ctx", -hop
                ).astype(WIDE)

    grad_targets = (-writing * grad_errors).astype(NARROW).reshape(rows, local_width)
    scale_part = jnp.sum(grad_recalls * recall_seq + errors * grad_errors, axis=3).reshape(rows)
    scale_sum = lax.psum(scale_part, "tp")
    known = [halo[:, index] for index in range(reach * blocks_each)]
    known = known + [scaled_errors[:, own] for own in range(blocks_each)]
    grad_mixing = []
    for own in range(blocks_each):
        row = []
        for lag in range(LAGS):
            link = linked[:, own, lag][:, None, None]
            product = batched(
                "std,sud->stu", raws[:, own], known[reach * blocks_each + own - 1 - lag]
            )
            row.append(jnp.where(link, -step * product, 0.0))
        grad_mixing.append(jnp.stack(row, axis=1))
    grad_mixing = lax.psum(jnp.stack(grad_mixing, axis=1).astype(NARROW), "tp")
    needed = {}
    for hop in range(1, reach + 1):
        pairs = [
            (own, lag)
            for own in range(blocks_each)
            for lag in range(LAGS)
            if -(-(1 + lag - own) // blocks_each) == hop
        ]
        moved = passed_along(
            jnp.stack([grad_mixing[:, own, lag] for own, lag in pairs], axis=1), "ctx", -hop
        )
        for place, (own, lag) in enumerate(pairs):
            needed[(hop * blocks_each + own, lag)] = moved[:, place]
    for own in range(blocks_each):
        for lag in range(LAGS):
            needed[(own, lag)] = grad_mixing[:, own, lag]
    grad_features = []
    grad_decays = [0.0] * LAGS
    for own in range(blocks_each):
        total = 0.0
        mine = own_features[:, own].astype(WIDE)
        for lag in range(LAGS):
            from_reads = batched("stu,suh->sth", needed[(own, lag)], block_of(first + own - 1 - lag))
            grad_decays[lag] = grad_decays[lag] + jnp.sum(mine * from_reads, axis=(0, 1))
            later = own + 1 + lag
            from_writes = batched("stu,sth->suh", needed[(later, lag)], block_of(first + later))
            total = total + decays[lag] * (from_reads + from_writes)
        grad_features.append(total)
    grad_features = jnp.stack(grad_features, 1).reshape(rows, local_units)
    grad_features = grad_features - (key_scale * key_scale * scale_sum)[:, None] * features.astype(
        WIDE
    )
    grad_retain = 0.0
    grad_moment = 0.0
    retain_slope = jnp.zeros_like(retain)
    for lag in range(1, LAGS):
        retain_slope = retain * retain_slope + decays[lag - 1]
        moment_slope = 0.0
        for power in range(1, lag + 1):
            moment_slope = moment_slope + power * retain ** (lag - power) * moment ** (power - 1)
        grad_retain = grad_retain + retain_slope * grad_decays[lag]
        grad_moment = grad_moment + moment_slope * grad_decays[lag]
    grad_rates = jnp.stack([grad_retain, grad_moment])

    grad_pre = (grad_features * silu_slope(preact)).astype(NARROW)
    grad_feature_w = over_rows(input_low, grad_pre)
    grad_target_w = over_rows(input_low, grad_targets)
    grad_input = grad_input + by_rows(grad_pre, feature_cols) + by_rows(grad_targets, value_cols)
    grad_input = scattered(grad_input)
    _, unit_in, factor_in = norm_rows(residual, gain_in_wide)
    grad_gain_in = jnp.sum(grad_input * unit_in, axis=0)
    grad_tokens = collected(
        grad_hidden + norm_back(grad_input, unit_in, factor_in, gain_in_wide)
    ).astype(WIDE)

    def shared(array, axis):
        halves = lax.psum_scatter(
            array.astype(NARROW), "shard", scatter_dimension=axis, tiled=True
        )
        return lax.psum(halves, "ctx").astype(WIDE)

    def small(array, axis, axes):
        summed = lax.psum(array, axes)
        size = summed.shape[axis] // lax.axis_size("shard")
        return lax.dynamic_slice_in_dim(summed, lax.axis_index("shard") * size, size, axis)

    return (
        output,
        grad_tokens.reshape(groups, local_len, width),
        small(grad_gain_in, 0, ("shard", "ctx", "tp")),
        small(grad_gain_ffn, 0, ("shard", "ctx", "tp")),
        small(grad_gain_memory, 1, ("shard", "ctx")),
        small(grad_rates, 0, ("shard", "ctx")),
        small(grad_persist, 1, ("shard", "ctx", "tp")),
        shared(grad_qkv, 1),
        shared(grad_out_rows, 1),
        shared(grad_target_w, 0),
        shared(grad_feature_w, 0),
        shared(grad_gate_up, 1),
        shared(grad_down, 1),
    )


def solution(mesh):
    placed = (
        P("shard", "ctx", None),
        P("shard", "ctx"),
        P("shard"),
        P("shard"),
        P("tp", "shard"),
        P("shard", None),
        P(None, "shard"),
        P(None, "shard", "tp"),
        P("tp", "shard"),
        P("shard", "tp"),
        P("shard", "tp"),
        P(None, "shard", "tp"),
        P("tp", "shard"),
        P("shard", "ctx", None),
    )
    return jax.shard_map(
        on_device,
        mesh=mesh,
        in_specs=placed,
        out_specs=(
            P("shard", "ctx", None),
            P("shard", "ctx", None),
            P("shard"),
            P("shard"),
            P("tp", "shard"),
            P("shard", "tp"),
            P(None, "shard"),
            P(None, "shard", "tp"),
            P("tp", "shard"),
            P("shard", "tp"),
            P("shard", "tp"),
            P(None, "shard", "tp"),
            P("tp", "shard"),
        ),
        check_vma=False,
    )
```

```python
import jax
import jax.numpy as jnp
from jax import lax
from jax.sharding import PartitionSpec as P

HD = 96
SPAN = 256
LIMIT = 800
LAGS = (LIMIT + SPAN - 2) // SPAN
STREAMS = 1


EPSILON = 1e-06
MASKED = -1e30
WIDE = jnp.float32
NARROW = jnp.bfloat16


def passed_along(value, axis, pairs):
    return lax.ppermute(value, axis, pairs)


def flipped(value, axis, bit):
    return lax.ppermute(value, axis, [(i, i ^ bit) for i in range(lax.axis_size(axis))])


def either(first, one, other):
    return jnp.where(first, one, other), jnp.where(first, other, one)


def pick(array, place, axis):
    return lax.dynamic_index_in_dim(array, place, axis, keepdims=False)


def after(value, *others):
    return lax.optimization_barrier((value, *others))[0]


def norm_rows(values, gain):
    factor = lax.rsqrt(jnp.mean(values * values, axis=-1, keepdims=True) + EPSILON)
    normed = values * factor
    return (normed * gain, normed, factor)


def norm_back(upstream, normed, factor, gain):
    inner = upstream * gain
    return factor * (inner - normed * jnp.mean(inner * normed, axis=-1, keepdims=True))


def silu_slope(values):
    sigmoid = jax.nn.sigmoid(values)
    return sigmoid * (1.0 + values * (1.0 - sigmoid))


def matmul(left, right):
    return jnp.dot(left, right, preferred_element_type=WIDE)


def over_rows(left, right):
    return lax.dot_general(left, right, (((0,), (0,)), ((), ())), preferred_element_type=WIDE)


def by_rows(left, right):
    return lax.dot_general(left, right, (((1,), (1,)), ((), ())), preferred_element_type=WIDE)


def exact_product(left, right):
    return jnp.dot(left, right, precision=lax.Precision.HIGHEST, preferred_element_type=WIDE)


def batched(spec, left, right):
    return jnp.einsum(spec, left, right, preferred_element_type=WIDE)


def on_device(
    tokens,
    segments,
    norm_gain,
    ffn_gain,
    memory_gain,
    memory_rates,
    persistent,
    w_qkv,
    w_out,
    w_value,
    w_feature,
    w_gate_up,
    w_down,
    out_grad,
):
    parts, ranks = (lax.axis_size("ctx"), lax.axis_size("tp"))
    part, rank = (lax.axis_index("ctx"), lax.axis_index("tp"))
    half_index = lax.axis_index("shard")
    first_half = half_index == 0
    odd_part = part % 2 == 1
    groups, local_len, width = tokens.shape
    blocks_each = local_len // SPAN
    reach = -(-LAGS // blocks_each)
    step = 6.0 / (SPAN + 8)
    scale = HD ** (-0.5)

    def joined(own, other, axis):
        return jnp.concatenate(either(first_half, own, other), axis=axis)

    pair_tokens = flipped(tokens, "ctx", 1)
    far_tokens = flipped(tokens, "ctx", 2)
    diagonal_tokens = flipped(far_tokens, "ctx", 1)
    feature_other = flipped(w_feature, "shard", 1)
    smalls = [norm_gain, ffn_gain, memory_gain, memory_rates, persistent]
    small_flat = jnp.concatenate([item.reshape(-1) for item in smalls])
    small_other = flipped(small_flat, "shard", 1)
    small_others = []
    start = 0
    for item in smalls:
        small_others.append(small_other[start : start + item.size].reshape(item.shape))
        start += item.size
    value_other, qkv_other = [
        flipped(after(item, feature_other), "shard", 1) for item in (w_value, w_qkv)
    ]
    out_other, gate_up_other = [
        flipped(after(item, value_other, qkv_other), "shard", 1) for item in (w_out, w_gate_up)
    ]
    down_other = flipped(after(w_down, out_other, gate_up_other), "shard", 1)

    gain_in_wide = joined(norm_gain, small_others[0], 0).astype(WIDE)
    gain_ffn_wide = joined(ffn_gain, small_others[1], 0).astype(WIDE)
    gain_mem = joined(memory_gain, small_others[2], 1).astype(WIDE)
    rates = joined(memory_rates, small_others[3], 0)
    persist = joined(persistent, small_others[4], 1)
    feature_cols = joined(w_feature, feature_other, 0)
    value_cols = joined(w_value, value_other, 0)
    qkv_cols = joined(w_qkv, qkv_other, 1)
    out_rows = joined(w_out, out_other, 1)
    gate_up_cols = joined(w_gate_up, gate_up_other, 1)
    down_rows = joined(w_down, down_other, 1)
    local_width = qkv_cols.shape[2]
    local_units = feature_cols.shape[1]
    local_heads = local_width // HD
    persist_count = persist.shape[0]
    query_w = qkv_cols[0]
    key_w = qkv_cols[1]
    value_w = qkv_cols[2]

    def scattered(array):
        return lax.psum_scatter(
            array.astype(NARROW), "tp", scatter_dimension=0, tiled=True
        ).astype(WIDE)

    def collected(array):
        return lax.all_gather(array.astype(NARROW), "tp", axis=0, tiled=True)

    own_units = lax.dynamic_slice_in_dim(rates.astype(WIDE), rank * local_units, local_units, 1)
    retain, moment = (own_units[0], own_units[1])
    decays = [jnp.ones_like(retain)]
    for lag in range(1, LAGS):
        decays.append(retain * decays[-1] + moment**lag)

    labels_all = segments.astype(WIDE).reshape(groups, blocks_each, SPAN) + 1.0
    lasts_all = labels_all[:, :, -1]
    block_lasts = lax.all_gather(lasts_all, "ctx", axis=1, tiled=True)
    total_blocks = parts * blocks_each
    first = part * blocks_each

    def last_of(index):
        found = lax.dynamic_index_in_dim(
            block_lasts, jnp.clip(index, 0, total_blocks - 1), 1, False
        )
        return jnp.where(index >= 0, found, 0.0)

    before_all = jnp.stack([last_of(first + own - 1) for own in range(blocks_each)], axis=1)
    linked_all = []
    for own in range(blocks_each):
        links = []
        for lag in range(LAGS - 1, -1, -1):
            source = first + own - 1 - lag
            link = (source >= 0) & (last_of(source) == last_of(first + own - 1))
            links.append(jnp.broadcast_to(link[:, None, None], (groups, 1, SPAN)))
        linked_all.append(jnp.concatenate(links, axis=2))
    linked_all = jnp.stack(linked_all, axis=1)

    def place_of(own, lag):
        return divmod(own - 1 - lag, blocks_each)

    fixed_keys = matmul(persist, key_w).astype(NARROW).reshape(1, persist_count, local_heads, HD)
    fixed_values = (
        matmul(persist, value_w).astype(NARROW).reshape(1, persist_count, local_heads, HD)
    )
    position = jnp.arange(SPAN)
    causal = position[:, None] >= position[None, :]

    count = groups // STREAMS
    rows = count * local_len
    blocks = count * blocks_each
    sub = rows // ranks

    def own_rows(array):
        return lax.dynamic_slice_in_dim(array, rank * sub, sub, 0)

    class Stream:
        pass

    def begin(one, index):
        def mine(array):
            return array[index * count : (index + 1) * count]

        one.flat = mine(tokens).reshape(rows, width)
        one.upstream_low = mine(out_grad).reshape(rows, width)
        one.labels = mine(labels_all)
        one.lasts = mine(lasts_all)
        one.before = mine(before_all)
        one.linked = mine(linked_all)
        one.keeping = (one.lasts == one.before).astype(WIDE)[:, :, None, None]
        one.writing = (one.labels == one.lasts[:, :, None]).astype(WIDE)[..., None]
        one.reading = (one.labels == one.before[:, :, None]).astype(WIDE)

        def features_of(piece):
            low = norm_rows(piece.astype(WIDE), gain_in_wide)[0].astype(NARROW)
            return low, matmul(low.reshape(rows, width), feature_cols)

        def shaped(values):
            return values.reshape(count, blocks_each, SPAN, local_units)

        low, one.preact = features_of(mine(tokens))
        one.input_low = low.reshape(rows, width)
        one.features = jax.nn.silu(one.preact).astype(NARROW)
        close = [mine(pair_tokens), mine(diagonal_tokens)]
        one.around = {0: shaped(one.features)}
        for delta, piece in (
            (-1, jnp.where(odd_part, close[0], close[1])),
            (1, jnp.where(odd_part, close[1], close[0])),
            (2, mine(far_tokens)),
        ):
            one.around[delta] = shaped(jax.nn.silu(features_of(piece)[1]).astype(NARROW))
        one.around[-2] = one.around[2]
        squares = jnp.sum(jnp.square(one.features.astype(WIDE)), axis=1)
        squares = jnp.sum(lax.all_gather(squares, "tp", axis=0), axis=0)
        one.key_scale = lax.rsqrt(squares + EPSILON)
        one.scales = one.key_scale.reshape(count, blocks_each, SPAN, 1)
        one.targets = matmul(one.input_low, value_cols).reshape(
            count, blocks_each, SPAN, local_width
        )
        weighted = [(one.around[0].astype(WIDE) * decay).astype(NARROW) for decay in decays]
        products = []
        for own in range(blocks_each):
            row = []
            for lag in range(LAGS - 1, -1, -1):
                delta, place = place_of(own, lag)
                row.append(
                    batched("sth,suh->stu", weighted[lag][:, own], one.around[delta][:, place])
                )
            products.append(jnp.concatenate(row, axis=2))
        products = jnp.stack(products, axis=1).astype(NARROW)
        mixing = lax.psum(products, "tp")
        one.mixing = jnp.where(one.linked, mixing, jnp.zeros_like(mixing))

    def span_of(own):
        start = (reach * blocks_each - LAGS + own) * SPAN
        return slice(start, start + LAGS * SPAN)

    def remember(one):
        halos = [
            jnp.zeros((count, blocks_each * SPAN, local_width), NARROW) for _ in range(reach)
        ]
        pending = {}
        for turn in range(parts):
            for hop in range(1, reach + 1):
                if (turn - hop, hop) in pending:
                    halos[reach - hop] = halos[reach - hop] + pending[(turn - hop, hop)]
            known = jnp.concatenate(halos, axis=1)
            recalls = []
            errors = []
            for own in range(blocks_each):
                total = batched("stu,sud->std", one.mixing[:, own], known[:, span_of(own)])
                recall = -step * one.scales[:, own] * total
                error = one.writing[:, own] * (
                    one.keeping[:, own] * recall - one.targets[:, own]
                )
                recalls.append(recall)
                errors.append(error)
                known = jnp.concatenate(
                    [known, (one.scales[:, own] * error).astype(NARROW)], axis=1
                )
            for hop in range(1, reach + 1):
                if turn + hop < parts:
                    pending[(turn, hop)] = passed_along(
                        known[:, reach * blocks_each * SPAN :], "ctx", [(turn, turn + hop)]
                    )
        one.known = known
        one.recall = jnp.stack(recalls, 1)
        one.errors = jnp.stack(errors, 1)
        heads_view = (one.reading[..., None] * one.recall).reshape(rows, local_heads, HD)
        one.head_factor = lax.rsqrt(
            jnp.mean(heads_view * heads_view, axis=-1, keepdims=True) + EPSILON
        )
        one.head_unit = heads_view * one.head_factor
        retrieved = (one.head_unit * gain_mem).reshape(rows, local_width).astype(NARROW)
        one.retrieved_full = lax.all_gather(retrieved, "tp", axis=1, tiled=True)

    def heads(values):
        return values.astype(NARROW).reshape(blocks, SPAN, local_heads, HD)

    def fixed(values):
        return jnp.broadcast_to(values, (blocks, persist_count, local_heads, HD))

    def scores_of(one):
        raw = batched("bthd,bkhd->bhtk", one.queries, one.keys) * scale
        return jnp.where(one.visible[:, None], raw, MASKED)

    def attend(one):
        one.queries = heads(matmul(one.input_low, query_w))
        one.keys = jnp.concatenate(
            [
                fixed(fixed_keys),
                heads(matmul(one.retrieved_full, key_w)),
                heads(matmul(one.input_low, key_w)),
            ],
            axis=1,
        )
        one.values = jnp.concatenate(
            [
                fixed(fixed_values),
                heads(matmul(one.retrieved_full, value_w)),
                heads(matmul(one.input_low, value_w)),
            ],
            axis=1,
        )
        label_rows = one.labels.reshape(blocks, SPAN)
        read_rows = one.reading.reshape(blocks, SPAN)
        visible_own = causal[None] & (label_rows[:, :, None] == label_rows[:, None, :])
        visible_memory = visible_own & (read_rows[:, None, :] > 0.5)
        one.visible = jnp.concatenate(
            [jnp.ones((blocks, SPAN, persist_count), jnp.bool_), visible_memory, visible_own],
            axis=2,
        )
        scores = scores_of(one)
        highest = jnp.max(scores, axis=-1, keepdims=True)
        raised = jnp.exp(scores - highest)
        totals = jnp.sum(raised, axis=-1, keepdims=True)
        one.logsum = highest + jnp.log(totals)
        probs_low = (raised / totals).astype(NARROW)
        one.attended = (
            batched("bhtk,bkhd->bthd", probs_low, one.values)
            .astype(NARROW)
            .reshape(rows, local_width)
        )
        one.residual = own_rows(one.flat).astype(WIDE)
        one.hidden = one.residual + scattered(matmul(one.attended, out_rows))
        normed_mid, one.unit_mid, one.factor_mid = norm_rows(one.hidden, gain_ffn_wide)
        one.mid_low = collected(normed_mid)

    def feed(one):
        gate = matmul(one.mid_low, gate_up_cols[0])
        upper = matmul(one.mid_low, gate_up_cols[1])
        one.activ = (jax.nn.silu(gate) * upper).astype(NARROW)
        grad_act = by_rows(one.upstream_low, down_rows)
        one.grad_gate = (grad_act * upper * silu_slope(gate)).astype(NARROW)
        one.grad_upper = (grad_act * jax.nn.silu(gate)).astype(NARROW)
        grad_mid = scattered(
            by_rows(one.grad_gate, gate_up_cols[0]) + by_rows(one.grad_upper, gate_up_cols[1])
        )
        one.grad_gain_ffn = jnp.sum(grad_mid * one.unit_mid, axis=0)
        upstream = own_rows(one.upstream_low).astype(WIDE)
        one.grad_hidden = upstream + norm_back(
            grad_mid, one.unit_mid, one.factor_mid, gain_ffn_wide
        )
        one.grad_mixed = collected(one.grad_hidden)

    def finish_output(one):
        branch = scattered(matmul(one.activ, down_rows))
        one.output = collected(one.hidden + branch).reshape(count, local_len, width)

    def attend_back(one):
        grad_attended = (
            by_rows(one.grad_mixed, out_rows)
            .astype(NARROW)
            .reshape(blocks, SPAN, local_heads, HD)
        )
        probs = jnp.exp(scores_of(one) - one.logsum)
        grad_probs = batched("bthd,bkhd->bhtk", grad_attended, one.values)
        grad_values = batched("bhtk,bthd->bkhd", probs.astype(NARROW), grad_attended)
        grad_scores = (
            probs * (grad_probs - jnp.sum(grad_probs * probs, axis=-1, keepdims=True))
        ).astype(NARROW)
        one.grad_queries = (
            (batched("bhtk,bkhd->bthd", grad_scores, one.keys) * scale)
            .astype(NARROW)
            .reshape(rows, local_width)
        )
        grad_keys = batched("bhtk,bthd->bkhd", grad_scores, one.queries) * scale

        def split_keys(grads):
            fixed_part = jnp.sum(grads[:, :persist_count], axis=0).reshape(
                persist_count, local_width
            )
            memory_part = (
                grads[:, persist_count : persist_count + SPAN]
                .astype(NARROW)
                .reshape(rows, local_width)
            )
            token_part = (
                grads[:, persist_count + SPAN :].astype(NARROW).reshape(rows, local_width)
            )
            return (fixed_part, memory_part, token_part)

        one.key_fixed, one.key_memory, one.key_token = split_keys(grad_keys)
        one.value_fixed, one.value_memory, one.value_token = split_keys(grad_values)
        grad_retrieved = lax.psum_scatter(
            (by_rows(one.key_memory, key_w) + by_rows(one.value_memory, value_w)).astype(NARROW),
            "tp",
            scatter_dimension=1,
            tiled=True,
        ).astype(WIDE)
        grad_heads = grad_retrieved.reshape(rows, local_heads, HD)
        one.grad_gain_memory = jnp.sum(grad_heads * one.head_unit, axis=0)
        inner = grad_heads * gain_mem
        grad_masked = one.head_factor * (
            inner - one.head_unit * jnp.mean(inner * one.head_unit, axis=-1, keepdims=True)
        )
        one.grad_read = one.reading[..., None] * grad_masked.reshape(
            count, blocks_each, SPAN, local_width
        )

    def remember_back(one):
        later = [0.0] * blocks_each
        pending = {}
        for turn in range(parts):
            for hop in range(1, reach + 1):
                if (turn - hop, hop) in pending:
                    arrived = pending[(turn - hop, hop)].astype(WIDE)
                    for own in range(blocks_each):
                        later[own] = later[own] + arrived[:, own * SPAN : (own + 1) * SPAN]
            known = [0.0] * (reach * blocks_each) + later
            grad_errors = [None] * blocks_each
            grad_recalls = [None] * blocks_each
            raws = [None] * blocks_each
            for own in range(blocks_each - 1, -1, -1):
                grad_scaled = -step * known[reach * blocks_each + own]
                grad_error = one.scales[:, own] * grad_scaled
                grad_recall = (
                    one.grad_read[:, own] + one.writing[:, own] * one.keeping[:, own] * grad_error
                )
                grad_errors[own] = jnp.broadcast_to(grad_error, grad_recall.shape)
                grad_recalls[own] = grad_recall
                raws[own] = (one.scales[:, own] * grad_recall).astype(NARROW)
                carried = batched("stu,std->sud", one.mixing[:, own], raws[own])
                for index in range(LAGS):
                    place = reach * blocks_each - LAGS + own + index
                    known[place] = (
                        known[place] + carried[:, index * SPAN : (index + 1) * SPAN]
                    )
            for hop in range(1, reach + 1):
                place = parts - 1 - turn
                if place - hop >= 0:
                    start = (reach - hop) * blocks_each
                    sent = jnp.concatenate(known[start : start + blocks_each], axis=1)
                    pending[(turn, hop)] = passed_along(
                        sent.astype(NARROW), "ctx", [(place, place - hop)]
                    )
        grad_errors = jnp.stack(grad_errors, 1)
        grad_recalls = jnp.stack(grad_recalls, 1)
        one.grad_targets = (-one.writing * grad_errors).astype(NARROW).reshape(rows, local_width)
        scale_part = jnp.sum(grad_recalls * one.recall + one.errors * grad_errors, axis=3)
        one.scale_sum = jnp.sum(lax.all_gather(scale_part.reshape(rows), "tp", axis=0), axis=0)
        grad_mixing = []
        for own in range(blocks_each):
            grad_mixing.append(
                -step * batched("std,sud->stu", raws[own], one.known[:, span_of(own)])
            )
        grad_mixing = jnp.where(one.linked, jnp.stack(grad_mixing, 1), 0.0)
        one.grad_mixing = lax.psum(grad_mixing.astype(NARROW), "tp")

    def features_back(one):
        def column(own, lag):
            start = (LAGS - 1 - lag) * SPAN
            return one.grad_mixing[:, own, :, start : start + SPAN]

        needed = {}
        for hop in range(1, reach + 1):
            pairs = [
                (own, lag)
                for own in range(blocks_each)
                for lag in range(LAGS)
                if place_of(own, lag)[0] == -hop
            ]
            moved = passed_along(
                jnp.stack([column(own, lag) for own, lag in pairs], axis=1),
                "ctx",
                [(source, source - hop) for source in range(hop, parts)],
            )
            for place, (own, lag) in enumerate(pairs):
                needed[(hop * blocks_each + own, lag)] = moved[:, place]
        for own in range(blocks_each):
            for lag in range(LAGS):
                needed[(own, lag)] = column(own, lag)
        grad_features = []
        one.grad_decays = [0.0] * LAGS
        for own in range(blocks_each):
            total = 0.0
            own_features = one.around[0][:, own].astype(WIDE)
            for lag in range(LAGS):
                delta, place = place_of(own, lag)
                from_reads = batched(
                    "stu,suh->sth", needed[(own, lag)], one.around[delta][:, place]
                )
                one.grad_decays[lag] = one.grad_decays[lag] + jnp.sum(
                    own_features * from_reads, axis=(0, 1)
                )
                later = own + 1 + lag
                delta, place = divmod(later, blocks_each)
                from_writes = batched(
                    "stu,sth->suh", needed[(later, lag)], one.around[delta][:, place]
                )
                total = total + decays[lag] * (from_reads + from_writes)
            grad_features.append(total)
        grad_features = jnp.stack(grad_features, 1).reshape(rows, local_units)
        grad_features = grad_features - (one.key_scale * one.key_scale * one.scale_sum)[
            :, None
        ] * one.features.astype(WIDE)
        one.grad_pre = (grad_features * silu_slope(one.preact)).astype(NARROW)

    def inputs_back(one):
        grad_input = (
            by_rows(one.grad_queries, query_w)
            + by_rows(one.key_token, key_w)
            + by_rows(one.value_token, value_w)
            + by_rows(one.grad_targets, value_cols)
            + by_rows(one.grad_pre, feature_cols)
        )
        grad_input = scattered(grad_input)
        _, unit_in, factor_in = norm_rows(one.residual, gain_in_wide)
        one.grad_gain_in = jnp.sum(grad_input * unit_in, axis=0)
        one.grad_tokens = (
            collected(one.grad_hidden + norm_back(grad_input, unit_in, factor_in, gain_in_wide))
            .astype(WIDE)
            .reshape(count, local_len, width)
        )

    streams = [Stream() for _ in range(STREAMS)]
    for index, one in enumerate(streams):
        begin(one, index)
    for stage in (remember, attend, feed):
        for one in streams:
            stage(one)

    def over(function):
        total = function(streams[0])
        for one in streams[1:]:
            total = total + function(one)
        return total

    core, outer = (part % 2, part // 2)
    fours = (2, 2)

    def shared(array, by_row):
        array = array.astype(NARROW)
        *lead, high, wide = array.shape
        if by_row:
            array = array.reshape(*lead, 2, *fours, high // 8, wide)
            core_axis = len(lead) + 1
            half_axis = len(lead)
        else:
            array = array.reshape(*fours, high // 4, wide)
            core_axis = 0
        sent = flipped(pick(array, 1 - core, core_axis), "ctx", 1)
        array = (pick(array, core, core_axis).astype(WIDE) + sent.astype(WIDE)).astype(NARROW)
        if by_row:
            own, other = (pick(array, place, half_axis) for place in (half_index, 1 - half_index))
            outer_axis = half_axis
        else:
            half = wide // 2
            own, other = (
                lax.dynamic_slice_in_dim(array, place * half, half, 2)
                for place in (half_index, 1 - half_index)
            )
            outer_axis = 0
        array = (own.astype(WIDE) + flipped(other, "shard", 1).astype(WIDE)).astype(NARROW)
        sent = flipped(pick(array, 1 - outer, outer_axis), "ctx", 2)
        array = (pick(array, outer, outer_axis).astype(WIDE) + sent.astype(WIDE)).astype(NARROW)
        array = jnp.stack(either(outer == 0, array, flipped(array, "ctx", 2)), axis=outer_axis)
        array = jnp.stack(either(core == 0, array, flipped(array, "ctx", 1)), axis=outer_axis)
        if by_row:
            return array.reshape(*lead, high // 2, wide).astype(WIDE)
        return array.reshape(high, wide // 2).astype(WIDE)

    grad_down = shared(over(lambda one: over_rows(one.activ, one.upstream_low)), False)
    grad_gate_up = shared(
        jnp.stack(
            [
                over(lambda one: over_rows(one.mid_low, one.grad_gate)).astype(NARROW),
                over(lambda one: over_rows(one.mid_low, one.grad_upper)).astype(NARROW),
            ]
        ),
        True,
    )
    for one in streams:
        attend_back(one)
    for one in streams:
        finish_output(one)
    grad_out_rows = shared(over(lambda one: over_rows(one.attended, one.grad_mixed)), False)
    persist_wide = persist.astype(WIDE)
    key_fixed = over(lambda one: one.key_fixed)
    value_fixed = over(lambda one: one.value_fixed)
    grad_query_w = over(lambda one: over_rows(one.input_low, one.grad_queries))
    grad_key_w = over(
        lambda one: over_rows(one.input_low, one.key_token)
        + over_rows(one.retrieved_full, one.key_memory)
    ) + exact_product(persist_wide.T, key_fixed)
    grad_value_proj = over(
        lambda one: over_rows(one.input_low, one.value_token)
        + over_rows(one.retrieved_full, one.value_memory)
    ) + exact_product(persist_wide.T, value_fixed)
    grad_qkv = shared(
        jnp.stack([item.astype(NARROW) for item in (grad_query_w, grad_key_w, grad_value_proj)]),
        True,
    )
    grad_persist = exact_product(key_fixed, key_w.astype(WIDE).T) + exact_product(
        value_fixed, value_w.astype(WIDE).T
    )
    grad_persist = lax.psum_scatter(grad_persist, "tp", scatter_dimension=0, tiled=True)

    for one in streams:
        remember_back(one)
    grad_target_w = shared(over(lambda one: over_rows(one.input_low, one.grad_targets)), True)
    for one in streams:
        features_back(one)
    grad_feature_w = shared(over(lambda one: over_rows(one.input_low, one.grad_pre)), True)
    for one in streams:
        inputs_back(one)

    grad_decays = [over(lambda one: one.grad_decays[lag]) for lag in range(LAGS)]
    grad_retain = 0.0
    grad_moment = 0.0
    retain_slope = jnp.zeros_like(retain)
    for lag in range(1, LAGS):
        retain_slope = retain * retain_slope + decays[lag - 1]
        moment_slope = 0.0
        for power in range(1, lag + 1):
            moment_slope = moment_slope + power * retain ** (lag - power) * moment ** (power - 1)
        grad_retain = grad_retain + retain_slope * grad_decays[lag]
        grad_moment = grad_moment + moment_slope * grad_decays[lag]
    grad_rates = jnp.stack([grad_retain, grad_moment])

    pieces = [
        grad_persist,
        over(lambda one: one.grad_gain_in),
        over(lambda one: one.grad_gain_ffn),
        over(lambda one: one.grad_gain_memory),
        grad_rates,
    ]
    small = jnp.concatenate([piece.reshape(-1) for piece in pieces])
    small = small + flipped(small, "ctx", 1)
    small = small + flipped(small, "shard", 1)
    small = small + flipped(small, "ctx", 2)
    cut = grad_persist.size + 2 * width
    spread = lax.all_gather(small[:cut], "tp", axis=0)
    grad_persist = spread[:, : grad_persist.size].reshape(persist_count, width)
    gains = jnp.sum(spread[:, grad_persist.size // ranks :], axis=0).reshape(2, width)
    middle = cut + local_heads * HD
    grad_gain_memory = small[cut:middle].reshape(local_heads, HD)
    grad_rates = small[middle:].reshape(2, local_units)

    def own_half(array, axis):
        size = array.shape[axis] // 2
        return lax.dynamic_slice_in_dim(array, half_index * size, size, axis)

    return (
        jnp.concatenate([one.output for one in streams], axis=0),
        jnp.concatenate([one.grad_tokens for one in streams], axis=0),
        own_half(gains[0], 0),
        own_half(gains[1], 0),
        own_half(grad_gain_memory, 1),
        own_half(grad_rates, 0),
        own_half(grad_persist, 1),
        grad_qkv,
        grad_out_rows,
        grad_target_w,
        grad_feature_w,
        grad_gate_up,
        grad_down,
    )


def solution(mesh):
    placed = (
        P("shard", "ctx", None),
        P("shard", "ctx"),
        P("shard"),
        P("shard"),
        P("tp", "shard"),
        P("shard", None),
        P(None, "shard"),
        P(None, "shard", "tp"),
        P("tp", "shard"),
        P("shard", "tp"),
        P("shard", "tp"),
        P(None, "shard", "tp"),
        P("tp", "shard"),
        P("shard", "ctx", None),
    )
    return jax.shard_map(
        on_device,
        mesh=mesh,
        in_specs=placed,
        out_specs=(
            P("shard", "ctx", None),
            P("shard", "ctx", None),
            P("shard"),
            P("shard"),
            P("tp", "shard"),
            P("shard", "tp"),
            P(None, "shard"),
            P(None, "shard", "tp"),
            P("tp", "shard"),
            P("shard", "tp"),
            P("shard", "tp"),
            P(None, "shard", "tp"),
            P("tp", "shard"),
        ),
        check_vma=False,
    )
```

```python
import jax
import jax.numpy as jnp
from jax import lax
from jax.sharding import PartitionSpec as P

HD = 96
SPAN = 256
LIMIT = 800
LAGS = (LIMIT + SPAN - 2) // SPAN
STREAMS = 1


EPSILON = 1e-06
MASKED = -1e30
WIDE = jnp.float32
NARROW = jnp.bfloat16


def passed_along(value, axis, pairs):
    return lax.ppermute(value, axis, pairs)


def flipped(value, axis, bit):
    return lax.ppermute(value, axis, [(i, i ^ bit) for i in range(lax.axis_size(axis))])


def either(first, one, other):
    return jnp.where(first, one, other), jnp.where(first, other, one)


def pick(array, place, axis):
    return lax.dynamic_index_in_dim(array, place, axis, keepdims=False)


def after(value, *others):
    return lax.optimization_barrier((value, *others))[0]


def norm_rows(values, gain):
    factor = lax.rsqrt(jnp.mean(values * values, axis=-1, keepdims=True) + EPSILON)
    normed = values * factor
    return (normed * gain, normed, factor)


def norm_back(upstream, normed, factor, gain):
    inner = upstream * gain
    return factor * (inner - normed * jnp.mean(inner * normed, axis=-1, keepdims=True))


def silu_slope(values):
    sigmoid = jax.nn.sigmoid(values)
    return sigmoid * (1.0 + values * (1.0 - sigmoid))


def matmul(left, right):
    return jnp.dot(left, right, preferred_element_type=WIDE)


def over_rows(left, right):
    return lax.dot_general(left, right, (((0,), (0,)), ((), ())), preferred_element_type=WIDE)


def by_rows(left, right):
    return lax.dot_general(left, right, (((1,), (1,)), ((), ())), preferred_element_type=WIDE)


def exact_product(left, right):
    return jnp.dot(left, right, precision=lax.Precision.HIGHEST, preferred_element_type=WIDE)


def batched(spec, left, right):
    return jnp.einsum(spec, left, right, preferred_element_type=WIDE)


def on_device(
    tokens,
    segments,
    norm_gain,
    ffn_gain,
    memory_gain,
    memory_rates,
    persistent,
    w_qkv,
    w_out,
    w_value,
    w_feature,
    w_gate_up,
    w_down,
    out_grad,
):
    parts, ranks = (lax.axis_size("ctx"), lax.axis_size("tp"))
    part, rank = (lax.axis_index("ctx"), lax.axis_index("tp"))
    half_index = lax.axis_index("shard")
    first_half = half_index == 0
    odd_part = part % 2 == 1
    groups, local_len, width = tokens.shape
    blocks_each = local_len // SPAN
    reach = -(-LAGS // blocks_each)
    step = 6.0 / (SPAN + 8)
    scale = HD ** (-0.5)

    def joined(own, other, axis):
        return jnp.concatenate(either(first_half, own, other), axis=axis)

    pair_tokens = flipped(tokens, "ctx", 1)
    far_tokens = flipped(tokens, "ctx", 2)
    diagonal_tokens = flipped(far_tokens, "ctx", 1)
    feature_other = flipped(w_feature, "shard", 1)
    smalls = [norm_gain, ffn_gain, memory_gain, memory_rates, persistent]
    small_flat = jnp.concatenate([item.reshape(-1) for item in smalls])
    small_other = flipped(small_flat, "shard", 1)
    small_others = []
    start = 0
    for item in smalls:
        small_others.append(small_other[start : start + item.size].reshape(item.shape))
        start += item.size
    value_other = flipped(w_value, "shard", 1)

    gain_in_wide = joined(norm_gain, small_others[0], 0).astype(WIDE)
    gain_ffn_wide = joined(ffn_gain, small_others[1], 0).astype(WIDE)
    gain_mem = joined(memory_gain, small_others[2], 1).astype(WIDE)
    rates = joined(memory_rates, small_others[3], 0)
    persist = joined(persistent, small_others[4], 1)
    feature_cols = joined(w_feature, feature_other, 0)
    value_cols = joined(w_value, value_other, 0)
    weights = {}

    def fetch(name, array, start):
        weights[name] = flipped(after(array, start), "shard", 1)
        return weights[name]

    local_width = w_qkv.shape[2]
    local_units = feature_cols.shape[1]
    local_heads = local_width // HD
    persist_count = persist.shape[0]

    def scattered(array):
        return lax.psum_scatter(
            array.astype(NARROW), "tp", scatter_dimension=0, tiled=True
        ).astype(WIDE)

    def collected(array):
        return lax.all_gather(array.astype(NARROW), "tp", axis=0, tiled=True)

    own_units = lax.dynamic_slice_in_dim(rates.astype(WIDE), rank * local_units, local_units, 1)
    retain, moment = (own_units[0], own_units[1])
    decays = [jnp.ones_like(retain)]
    for lag in range(1, LAGS):
        decays.append(retain * decays[-1] + moment**lag)

    labels_all = segments.astype(WIDE).reshape(groups, blocks_each, SPAN) + 1.0
    lasts_all = labels_all[:, :, -1]
    block_lasts = lax.all_gather(lasts_all, "ctx", axis=1, tiled=True)
    total_blocks = parts * blocks_each
    first = part * blocks_each

    def last_of(index):
        found = lax.dynamic_index_in_dim(
            block_lasts, jnp.clip(index, 0, total_blocks - 1), 1, False
        )
        return jnp.where(index >= 0, found, 0.0)

    before_all = jnp.stack([last_of(first + own - 1) for own in range(blocks_each)], axis=1)
    linked_all = []
    for own in range(blocks_each):
        links = []
        for lag in range(LAGS - 1, -1, -1):
            source = first + own - 1 - lag
            link = (source >= 0) & (last_of(source) == last_of(first + own - 1))
            links.append(jnp.broadcast_to(link[:, None, None], (groups, 1, SPAN)))
        linked_all.append(jnp.concatenate(links, axis=2))
    linked_all = jnp.stack(linked_all, axis=1)

    def place_of(own, lag):
        return divmod(own - 1 - lag, blocks_each)

    position = jnp.arange(SPAN)
    causal = position[:, None] >= position[None, :]

    count = groups // STREAMS
    rows = count * local_len
    blocks = count * blocks_each
    sub = rows // ranks

    def own_rows(array):
        return lax.dynamic_slice_in_dim(array, rank * sub, sub, 0)

    class Stream:
        pass

    def begin(one, index):
        def mine(array):
            return array[index * count : (index + 1) * count]

        one.flat = mine(tokens).reshape(rows, width)
        one.upstream_low = mine(out_grad).reshape(rows, width)
        one.labels = mine(labels_all)
        one.lasts = mine(lasts_all)
        one.before = mine(before_all)
        one.linked = mine(linked_all)
        one.keeping = (one.lasts == one.before).astype(WIDE)[:, :, None, None]
        one.writing = (one.labels == one.lasts[:, :, None]).astype(WIDE)[..., None]
        one.reading = (one.labels == one.before[:, :, None]).astype(WIDE)

        def features_of(piece):
            low = norm_rows(piece.astype(WIDE), gain_in_wide)[0].astype(NARROW)
            return low, matmul(low.reshape(rows, width), feature_cols)

        def shaped(values):
            return values.reshape(count, blocks_each, SPAN, local_units)

        low, one.preact = features_of(mine(tokens))
        one.input_low = low.reshape(rows, width)
        one.features = jax.nn.silu(one.preact).astype(NARROW)
        far, pair, diagonal, one.features = lax.optimization_barrier(
            (mine(far_tokens), mine(pair_tokens), mine(diagonal_tokens), one.features)
        )
        close = [pair, diagonal]
        one.around = {0: shaped(one.features)}
        for delta, piece in (
            (-1, jnp.where(odd_part, close[0], close[1])),
            (1, jnp.where(odd_part, close[1], close[0])),
            (2, far),
        ):
            one.around[delta] = shaped(jax.nn.silu(features_of(piece)[1]).astype(NARROW))
        one.around[-2] = one.around[2]
        squares = jnp.sum(jnp.square(one.features.astype(WIDE)), axis=1)
        squares = jnp.sum(lax.all_gather(squares, "tp", axis=0), axis=0)
        one.key_scale = lax.rsqrt(squares + EPSILON)
        one.targets = matmul(one.input_low, value_cols).reshape(
            count, blocks_each, SPAN, local_width
        )
        weighted = [(one.around[0].astype(WIDE) * decay).astype(NARROW) for decay in decays]
        products = []
        for own in range(blocks_each):
            row = []
            for lag in range(LAGS - 1, -1, -1):
                delta, place = place_of(own, lag)
                row.append(
                    batched("sth,suh->stu", weighted[lag][:, own], one.around[delta][:, place])
                )
            products.append(jnp.concatenate(row, axis=2))
        products = jnp.stack(products, axis=1).astype(NARROW)
        products, one.key_scale = lax.optimization_barrier((products, one.key_scale))
        one.products = products
        one.mixing = lax.psum(products, "tp")

    def span_of(own):
        start = (reach * blocks_each - LAGS + own) * SPAN
        return slice(start, start + LAGS * SPAN)

    def remember(one):
        one.mixing = jnp.where(one.linked, one.mixing, jnp.zeros_like(one.mixing))
        one.scales = one.key_scale.reshape(count, blocks_each, SPAN, 1)
        halos = [
            jnp.zeros((count, blocks_each * SPAN, local_width), NARROW) for _ in range(reach)
        ]
        pending = {}
        for turn in range(parts):
            for hop in range(1, reach + 1):
                if (turn - hop, hop) in pending:
                    halos[reach - hop] = halos[reach - hop] + pending[(turn - hop, hop)]
            known = jnp.concatenate(halos, axis=1)
            recalls = []
            errors = []
            for own in range(blocks_each):
                total = batched("stu,sud->std", one.mixing[:, own], known[:, span_of(own)])
                recall = -step * one.scales[:, own] * total
                error = one.writing[:, own] * (
                    one.keeping[:, own] * recall - one.targets[:, own]
                )
                recalls.append(recall)
                errors.append(error)
                known = jnp.concatenate(
                    [known, (one.scales[:, own] * error).astype(NARROW)], axis=1
                )
            for hop in range(1, reach + 1):
                if turn + hop < parts:
                    pending[(turn, hop)] = passed_along(
                        known[:, reach * blocks_each * SPAN :], "ctx", [(turn, turn + hop)]
                    )
        one.known = known
        one.recall = jnp.stack(recalls, 1)
        one.errors = jnp.stack(errors, 1)
        heads_view = (one.reading[..., None] * one.recall).reshape(rows, local_heads, HD)
        one.head_factor = lax.rsqrt(
            jnp.mean(heads_view * heads_view, axis=-1, keepdims=True) + EPSILON
        )
        one.head_unit = heads_view * one.head_factor
        retrieved = (one.head_unit * gain_mem).reshape(rows, local_width).astype(NARROW)
        one.retrieved_full = lax.all_gather(retrieved, "tp", axis=1, tiled=True)

    def heads(values):
        return values.astype(NARROW).reshape(blocks, SPAN, local_heads, HD)

    def fixed(values):
        return jnp.broadcast_to(values, (blocks, persist_count, local_heads, HD))

    def scores_of(one):
        raw = batched("bthd,bkhd->bhtk", one.queries, one.keys) * scale
        return jnp.where(one.visible[:, None], raw, MASKED)

    def attend(one):
        one.queries = heads(matmul(one.input_low, query_w))
        one.keys = jnp.concatenate(
            [
                fixed(fixed_keys),
                heads(matmul(one.retrieved_full, key_w)),
                heads(matmul(one.input_low, key_w)),
            ],
            axis=1,
        )
        one.values = jnp.concatenate(
            [
                fixed(fixed_values),
                heads(matmul(one.retrieved_full, value_w)),
                heads(matmul(one.input_low, value_w)),
            ],
            axis=1,
        )
        label_rows = one.labels.reshape(blocks, SPAN)
        read_rows = one.reading.reshape(blocks, SPAN)
        visible_own = causal[None] & (label_rows[:, :, None] == label_rows[:, None, :])
        visible_memory = visible_own & (read_rows[:, None, :] > 0.5)
        one.visible = jnp.concatenate(
            [jnp.ones((blocks, SPAN, persist_count), jnp.bool_), visible_memory, visible_own],
            axis=2,
        )
        scores = scores_of(one)
        highest = jnp.max(scores, axis=-1, keepdims=True)
        raised = jnp.exp(scores - highest)
        totals = jnp.sum(raised, axis=-1, keepdims=True)
        one.logsum = highest + jnp.log(totals)
        probs_low = (raised / totals).astype(NARROW)
        one.attended = (
            batched("bhtk,bkhd->bthd", probs_low, one.values)
            .astype(NARROW)
            .reshape(rows, local_width)
        )
        one.residual = own_rows(one.flat).astype(WIDE)
        one.branch = scattered(matmul(one.attended, weights["out"]))

    def middle(one):
        one.hidden = one.residual + one.branch
        normed_mid, one.unit_mid, one.factor_mid = norm_rows(one.hidden, gain_ffn_wide)
        one.mid_low = collected(normed_mid)

    def feed(one):
        gate = matmul(one.mid_low, weights["gate"])
        upper = matmul(one.mid_low, weights["up"])
        one.activ = (jax.nn.silu(gate) * upper).astype(NARROW)
        grad_act = by_rows(one.upstream_low, weights["down"])
        one.grad_gate = (grad_act * upper * silu_slope(gate)).astype(NARROW)
        one.grad_upper = (grad_act * jax.nn.silu(gate)).astype(NARROW)
        one.grad_mid = scattered(
            by_rows(one.grad_gate, weights["gate"]) + by_rows(one.grad_upper, weights["up"])
        )

    def middle_back(one):
        grad_mid = one.grad_mid
        one.grad_gain_ffn = jnp.sum(grad_mid * one.unit_mid, axis=0)
        upstream = own_rows(one.upstream_low).astype(WIDE)
        one.grad_hidden = upstream + norm_back(
            grad_mid, one.unit_mid, one.factor_mid, gain_ffn_wide
        )
        one.grad_mixed = collected(one.grad_hidden)

    def branch_out(one):
        activ, one.grad_mixed = lax.optimization_barrier((one.activ, one.grad_mixed))
        one.branch = scattered(matmul(activ, weights["down"]))

    def finish_output(one):
        hidden, one.grad_retrieved = lax.optimization_barrier(
            (one.hidden + one.branch, one.grad_retrieved)
        )
        one.output = collected(hidden)

    def attend_back(one):
        grad_attended = (
            by_rows(one.grad_mixed, weights["out"])
            .astype(NARROW)
            .reshape(blocks, SPAN, local_heads, HD)
        )
        probs = jnp.exp(scores_of(one) - one.logsum)
        grad_probs = batched("bthd,bkhd->bhtk", grad_attended, one.values)
        grad_values = batched("bhtk,bthd->bkhd", probs.astype(NARROW), grad_attended)
        grad_scores = (
            probs * (grad_probs - jnp.sum(grad_probs * probs, axis=-1, keepdims=True))
        ).astype(NARROW)
        one.grad_queries = (
            (batched("bhtk,bkhd->bthd", grad_scores, one.keys) * scale)
            .astype(NARROW)
            .reshape(rows, local_width)
        )
        grad_keys = batched("bhtk,bthd->bkhd", grad_scores, one.queries) * scale

        def split_keys(grads):
            fixed_part = jnp.sum(grads[:, :persist_count], axis=0).reshape(
                persist_count, local_width
            )
            memory_part = (
                grads[:, persist_count : persist_count + SPAN]
                .astype(NARROW)
                .reshape(rows, local_width)
            )
            token_part = (
                grads[:, persist_count + SPAN :].astype(NARROW).reshape(rows, local_width)
            )
            return (fixed_part, memory_part, token_part)

        one.key_fixed, one.key_memory, one.key_token = split_keys(grad_keys)
        one.value_fixed, one.value_memory, one.value_token = split_keys(grad_values)
        partial = by_rows(one.key_memory, key_w) + by_rows(one.value_memory, value_w)
        partial, one.branch = lax.optimization_barrier((partial.astype(NARROW), one.branch))
        one.grad_retrieved = lax.psum_scatter(partial, "tp", scatter_dimension=1, tiled=True)

    def heads_back(one):
        grad_heads = one.grad_retrieved.astype(WIDE).reshape(rows, local_heads, HD)
        one.grad_gain_memory = jnp.sum(grad_heads * one.head_unit, axis=0)
        inner = grad_heads * gain_mem
        grad_masked = one.head_factor * (
            inner - one.head_unit * jnp.mean(inner * one.head_unit, axis=-1, keepdims=True)
        )
        one.grad_read = one.reading[..., None] * grad_masked.reshape(
            count, blocks_each, SPAN, local_width
        )

    def remember_back(one):
        later = [0.0] * blocks_each
        pending = {}
        for turn in range(parts):
            for hop in range(1, reach + 1):
                if (turn - hop, hop) in pending:
                    arrived = pending[(turn - hop, hop)].astype(WIDE)
                    for own in range(blocks_each):
                        later[own] = later[own] + arrived[:, own * SPAN : (own + 1) * SPAN]
            known = [0.0] * (reach * blocks_each) + later
            grad_errors = [None] * blocks_each
            grad_recalls = [None] * blocks_each
            raws = [None] * blocks_each
            for own in range(blocks_each - 1, -1, -1):
                grad_scaled = -step * known[reach * blocks_each + own]
                grad_error = one.scales[:, own] * grad_scaled
                grad_recall = (
                    one.grad_read[:, own] + one.writing[:, own] * one.keeping[:, own] * grad_error
                )
                grad_errors[own] = jnp.broadcast_to(grad_error, grad_recall.shape)
                grad_recalls[own] = grad_recall
                raws[own] = (one.scales[:, own] * grad_recall).astype(NARROW)
                carried = batched("stu,std->sud", one.mixing[:, own], raws[own])
                for index in range(LAGS):
                    place = reach * blocks_each - LAGS + own + index
                    known[place] = (
                        known[place] + carried[:, index * SPAN : (index + 1) * SPAN]
                    )
            for hop in range(1, reach + 1):
                place = parts - 1 - turn
                if place - hop >= 0:
                    start = (reach - hop) * blocks_each
                    sent = jnp.concatenate(known[start : start + blocks_each], axis=1)
                    pending[(turn, hop)] = passed_along(
                        sent.astype(NARROW), "ctx", [(place, place - hop)]
                    )
        grad_errors = jnp.stack(grad_errors, 1)
        grad_recalls = jnp.stack(grad_recalls, 1)
        one.grad_targets = (-one.writing * grad_errors).astype(NARROW).reshape(rows, local_width)
        scale_part = jnp.sum(grad_recalls * one.recall + one.errors * grad_errors, axis=3)
        one.scale_sum = jnp.sum(lax.all_gather(scale_part.reshape(rows), "tp", axis=0), axis=0)
        grad_mixing = []
        for own in range(blocks_each):
            grad_mixing.append(
                -step * batched("std,sud->stu", raws[own], one.known[:, span_of(own)])
            )
        grad_mixing = jnp.where(one.linked, jnp.stack(grad_mixing, 1), 0.0).astype(NARROW)
        grad_mixing, one.scale_sum, one.output = lax.optimization_barrier(
            (grad_mixing, one.scale_sum, one.output)
        )
        one.grad_mixing = lax.psum(grad_mixing, "tp")

    def features_back(one):
        def column(own, lag):
            start = (LAGS - 1 - lag) * SPAN
            return one.grad_mixing[:, own, :, start : start + SPAN]

        needed = {}
        for hop in range(1, reach + 1):
            pairs = [
                (own, lag)
                for own in range(blocks_each)
                for lag in range(LAGS)
                if place_of(own, lag)[0] == -hop
            ]
            moved = passed_along(
                jnp.stack([column(own, lag) for own, lag in pairs], axis=1),
                "ctx",
                [(source, source - hop) for source in range(hop, parts)],
            )
            for place, (own, lag) in enumerate(pairs):
                needed[(hop * blocks_each + own, lag)] = moved[:, place]
        for own in range(blocks_each):
            for lag in range(LAGS):
                needed[(own, lag)] = column(own, lag)
        grad_features = []
        one.grad_decays = [0.0] * LAGS
        for own in range(blocks_each):
            total = 0.0
            own_features = one.around[0][:, own].astype(WIDE)
            for lag in range(LAGS):
                delta, place = place_of(own, lag)
                from_reads = batched(
                    "stu,suh->sth", needed[(own, lag)], one.around[delta][:, place]
                )
                one.grad_decays[lag] = one.grad_decays[lag] + jnp.sum(
                    own_features * from_reads, axis=(0, 1)
                )
                later = own + 1 + lag
                delta, place = divmod(later, blocks_each)
                from_writes = batched(
                    "stu,sth->suh", needed[(later, lag)], one.around[delta][:, place]
                )
                total = total + decays[lag] * (from_reads + from_writes)
            grad_features.append(total)
        grad_features = jnp.stack(grad_features, 1).reshape(rows, local_units)
        grad_features = grad_features - (one.key_scale * one.key_scale * one.scale_sum)[
            :, None
        ] * one.features.astype(WIDE)
        one.grad_pre = (grad_features * silu_slope(one.preact)).astype(NARROW)

    def inputs_back(one):
        grad_input = (
            by_rows(one.grad_queries, query_w)
            + by_rows(one.key_token, key_w)
            + by_rows(one.value_token, value_w)
            + by_rows(one.grad_targets, value_cols)
            + by_rows(one.grad_pre, feature_cols)
        )
        one.grad_input = scattered(grad_input)

    def tokens_back(one):
        grad_input = one.grad_input
        _, unit_in, factor_in = norm_rows(one.residual, gain_in_wide)
        one.grad_gain_in = jnp.sum(grad_input * unit_in, axis=0)
        one.grad_tokens = (
            collected(one.grad_hidden + norm_back(grad_input, unit_in, factor_in, gain_in_wide))
            .astype(WIDE)
            .reshape(count, local_len, width)
        )

    streams = [Stream() for _ in range(STREAMS)]

    def over(function):
        total = function(streams[0])
        for one in streams[1:]:
            total = total + function(one)
        return total

    def every(stage):
        for one in streams:
            stage(one)

    core, outer = (part % 2, part // 2)

    class Reduction:
        def __init__(self, array, by_row):
            array = array.astype(NARROW)
            *self.lead, self.high, self.wide = array.shape
            self.by_row = by_row
            self.axis = len(self.lead)
            if by_row:
                array = array.reshape(*self.lead, 2, 2, 2, self.high // 8, self.wide)
            else:
                array = array.reshape(2, 2, self.high // 4, self.wide)
            self.array = array
            self.exchange(core, self.axis + 1 if by_row else 0, "ctx", 1)

        def exchange(self, index, axis, over_axis, bit):
            own, other = (pick(self.array, place, axis) for place in (index, 1 - index))
            self.add(own, flipped(other, over_axis, bit))

        def add(self, own, arrived):
            self.array = (own.astype(WIDE) + arrived.astype(WIDE)).astype(NARROW)

        def across(self):
            if self.by_row:
                self.exchange(half_index, self.axis, "shard", 1)
                return
            half = self.wide // 2
            own, other = (
                lax.dynamic_slice_in_dim(self.array, place * half, half, 2)
                for place in (half_index, 1 - half_index)
            )
            self.add(own, flipped(other, "shard", 1))

        def apart(self):
            self.exchange(outer, self.axis if self.by_row else 0, "ctx", 2)

        def together(self):
            pair = either(outer == 0, self.array, flipped(self.array, "ctx", 2))
            self.array = jnp.stack(pair, axis=self.axis if self.by_row else 0)

        def result(self):
            pair = either(core == 0, self.array, flipped(self.array, "ctx", 1))
            array = jnp.stack(pair, axis=self.axis if self.by_row else 0).astype(WIDE)
            if self.by_row:
                return array.reshape(*self.lead, self.high // 2, self.wide)
            return array.reshape(self.high, self.wide // 2)

    def tied(names, *reductions):
        held = [[getattr(one, name) for name in names] for one in streams]
        held, arrays = lax.optimization_barrier((held, [item.array for item in reductions]))
        for one, values in zip(streams, held):
            for name, value in zip(names, values):
                setattr(one, name, value)
        for item, array in zip(reductions, arrays):
            item.array = array

    class Holder:
        def __init__(self, array):
            self.array = array

    def fetched(names, *arrays):
        holders = [Holder(fetch(str(index), item, start)) for index, (item, start) in enumerate(arrays)]
        tied(names, *holders)
        return [holder.array for holder in holders]

    for index, one in enumerate(streams):
        begin(one, index)
    last = streams[-1]
    (qkv_other,) = fetched(["mixing"], (w_qkv, last.products))
    qkv_cols = joined(w_qkv, qkv_other, 1)
    query_w = qkv_cols[0]
    key_w = qkv_cols[1]
    value_w = qkv_cols[2]
    fixed_keys = matmul(persist, key_w).astype(NARROW).reshape(1, persist_count, local_heads, HD)
    fixed_values = (
        matmul(persist, value_w).astype(NARROW).reshape(1, persist_count, local_heads, HD)
    )
    every(remember)
    out_other, down_other = fetched(
        ["retrieved_full"], (w_out, last.recall), (w_down, last.recall)
    )
    weights["out"] = joined(w_out, out_other, 1)
    weights["down"] = joined(w_down, down_other, 1)
    every(attend)
    (gate_other,) = fetched(["branch"], (w_gate_up[0], last.attended))
    weights["gate"] = joined(w_gate_up[0], gate_other, 0)
    every(middle)
    (up_other,) = fetched(["mid_low"], (w_gate_up[1], last.hidden))
    weights["up"] = joined(w_gate_up[1], up_other, 0)
    every(feed)
    feed_reductions = [
        Reduction(over(lambda one: over_rows(one.activ, one.upstream_low)), False),
        Reduction(
            jnp.stack(
                [
                    over(lambda one: over_rows(one.mid_low, one.grad_gate)).astype(NARROW),
                    over(lambda one: over_rows(one.mid_low, one.grad_upper)).astype(NARROW),
                ]
            ),
            True,
        ),
    ]
    tied(["grad_mid"], *feed_reductions)
    every(middle_back)
    for item in feed_reductions:
        item.across()
    tied(["grad_mixed"], *feed_reductions)
    every(branch_out)
    every(attend_back)
    persist_wide = persist.astype(WIDE)
    key_fixed = over(lambda one: one.key_fixed)
    value_fixed = over(lambda one: one.value_fixed)
    grad_query_w = over(lambda one: over_rows(one.input_low, one.grad_queries))
    grad_key_w = over(
        lambda one: over_rows(one.input_low, one.key_token)
        + over_rows(one.retrieved_full, one.key_memory)
    ) + exact_product(persist_wide.T, key_fixed)
    grad_value_proj = over(
        lambda one: over_rows(one.input_low, one.value_token)
        + over_rows(one.retrieved_full, one.value_memory)
    ) + exact_product(persist_wide.T, value_fixed)
    mix_reductions = [
        Reduction(over(lambda one: over_rows(one.attended, one.grad_mixed)), False),
        Reduction(
            jnp.stack(
                [item.astype(NARROW) for item in (grad_query_w, grad_key_w, grad_value_proj)]
            ),
            True,
        ),
    ]
    grad_persist = exact_product(key_fixed, key_w.astype(WIDE).T) + exact_product(
        value_fixed, value_w.astype(WIDE).T
    )
    for item in feed_reductions:
        item.apart()
    tied(["grad_retrieved"], *feed_reductions, *mix_reductions)
    every(finish_output)
    every(heads_back)
    every(remember_back)
    grad_persist = after(grad_persist, last.grad_mixing)
    grad_persist = lax.psum_scatter(grad_persist, "tp", scatter_dimension=0, tiled=True)
    target_reduction = Reduction(over(lambda one: over_rows(one.input_low, one.grad_targets)), True)
    for item in feed_reductions:
        item.together()
    for item in mix_reductions:
        item.across()
    tied(["grad_mixing"], *feed_reductions, *mix_reductions, target_reduction)
    every(features_back)
    every(inputs_back)

    grad_decays = [over(lambda one: one.grad_decays[lag]) for lag in range(LAGS)]
    grad_retain = 0.0
    grad_moment = 0.0
    retain_slope = jnp.zeros_like(retain)
    for lag in range(1, LAGS):
        retain_slope = retain * retain_slope + decays[lag - 1]
        moment_slope = 0.0
        for power in range(1, lag + 1):
            moment_slope = moment_slope + power * retain ** (lag - power) * moment ** (power - 1)
        grad_retain = grad_retain + retain_slope * grad_decays[lag]
        grad_moment = grad_moment + moment_slope * grad_decays[lag]
    grad_rates = jnp.stack([grad_retain, grad_moment])

    def summed(pieces):
        small = jnp.concatenate([piece.reshape(-1) for piece in pieces])
        for axis, bit in (("ctx", 1), ("shard", 1), ("ctx", 2)):
            small = small + flipped(small, axis, bit)
        return small

    small = summed(
        [
            grad_persist,
            over(lambda one: one.grad_gain_ffn),
            over(lambda one: one.grad_gain_memory),
            grad_rates,
        ]
    )
    cut = grad_persist.size + width
    spread = Holder(lax.all_gather(small[:cut], "tp", axis=0))
    feature_reduction = Reduction(over(lambda one: over_rows(one.input_low, one.grad_pre)), True)
    late_reductions = [feature_reduction, target_reduction]
    for item in mix_reductions:
        item.apart()
    for item in late_reductions:
        item.across()
    tied(["grad_input"], spread, *mix_reductions, *late_reductions)
    every(tokens_back)
    for item in mix_reductions:
        item.together()
    for item in late_reductions:
        item.apart()
        item.together()
    small_in = lax.all_gather(summed([over(lambda one: one.grad_gain_in)]), "tp", axis=0)
    grad_persist = spread.array[:, : grad_persist.size].reshape(persist_count, width)
    gain_ffn_sum = jnp.sum(spread.array[:, cut - width :], axis=0)
    gain_in_sum = jnp.sum(small_in, axis=0)
    middle_cut = cut + local_heads * HD
    grad_gain_memory = small[cut:middle_cut].reshape(local_heads, HD)
    grad_rates = small[middle_cut:].reshape(2, local_units)
    grad_down, grad_gate_up = [item.result() for item in feed_reductions]
    grad_out_rows, grad_qkv = [item.result() for item in mix_reductions]
    grad_feature_w, grad_target_w = [item.result() for item in late_reductions]

    def own_half(array, axis):
        size = array.shape[axis] // 2
        return lax.dynamic_slice_in_dim(array, half_index * size, size, axis)

    return (
        jnp.concatenate([one.output for one in streams], axis=0).reshape(tokens.shape),
        jnp.concatenate([one.grad_tokens for one in streams], axis=0),
        own_half(gain_in_sum, 0),
        own_half(gain_ffn_sum, 0),
        own_half(grad_gain_memory, 1),
        own_half(grad_rates, 0),
        own_half(grad_persist, 1),
        grad_qkv,
        grad_out_rows,
        grad_target_w,
        grad_feature_w,
        grad_gate_up,
        grad_down,
    )


def solution(mesh):
    placed = (
        P("shard", "ctx", None),
        P("shard", "ctx"),
        P("shard"),
        P("shard"),
        P("tp", "shard"),
        P("shard", None),
        P(None, "shard"),
        P(None, "shard", "tp"),
        P("tp", "shard"),
        P("shard", "tp"),
        P("shard", "tp"),
        P(None, "shard", "tp"),
        P("tp", "shard"),
        P("shard", "ctx", None),
    )
    return jax.shard_map(
        on_device,
        mesh=mesh,
        in_specs=placed,
        out_specs=(
            P("shard", "ctx", None),
            P("shard", "ctx", None),
            P("shard"),
            P("shard"),
            P("tp", "shard"),
            P("shard", "tp"),
            P(None, "shard"),
            P(None, "shard", "tp"),
            P("tp", "shard"),
            P("shard", "tp"),
            P("shard", "tp"),
            P(None, "shard", "tp"),
            P("tp", "shard"),
        ),
        check_vma=False,
    )
```

```python
import jax
import jax.numpy as jnp
from jax import lax
from jax.sharding import PartitionSpec as P

HD = 96
SPAN = 256
LIMIT = 800
LAGS = (LIMIT + SPAN - 2) // SPAN
CORNER = LIMIT - (LAGS - 1) * SPAN
STREAMS = 1


EPSILON = 1e-06
MASKED = -1e30
WIDE = jnp.float32
NARROW = jnp.bfloat16


def passed_along(value, axis, pairs):
    return lax.ppermute(value, axis, pairs)


def flipped(value, axis, bit):
    return lax.ppermute(value, axis, [(i, i ^ bit) for i in range(lax.axis_size(axis))])


def either(first, one, other):
    return jnp.where(first, one, other), jnp.where(first, other, one)


def pick(array, place, axis):
    return lax.dynamic_index_in_dim(array, place, axis, keepdims=False)


def after(value, *others):
    return lax.optimization_barrier((value, *others))[0]


def norm_rows(values, gain):
    factor = lax.rsqrt(jnp.mean(values * values, axis=-1, keepdims=True) + EPSILON)
    normed = values * factor
    return (normed * gain, normed, factor)


def norm_back(upstream, normed, factor, gain):
    inner = upstream * gain
    return factor * (inner - normed * jnp.mean(inner * normed, axis=-1, keepdims=True))


def silu_slope(values):
    sigmoid = jax.nn.sigmoid(values)
    return sigmoid * (1.0 + values * (1.0 - sigmoid))


def matmul(left, right):
    return jnp.dot(left, right, preferred_element_type=WIDE)


def over_rows(left, right):
    return lax.dot_general(left, right, (((0,), (0,)), ((), ())), preferred_element_type=WIDE)


def by_rows(left, right):
    return lax.dot_general(left, right, (((1,), (1,)), ((), ())), preferred_element_type=WIDE)


def exact_product(left, right):
    return jnp.dot(left, right, precision=lax.Precision.HIGHEST, preferred_element_type=WIDE)


def batched(spec, left, right):
    return jnp.einsum(spec, left, right, preferred_element_type=WIDE)


def on_device(
    tokens,
    segments,
    norm_gain,
    ffn_gain,
    memory_gain,
    memory_rates,
    persistent,
    w_qkv,
    w_out,
    w_value,
    w_feature,
    w_gate_up,
    w_down,
    out_grad,
):
    parts, ranks = (lax.axis_size("ctx"), lax.axis_size("tp"))
    part, rank = (lax.axis_index("ctx"), lax.axis_index("tp"))
    half_index = lax.axis_index("shard")
    first_half = half_index == 0
    odd_part = part % 2 == 1
    groups, local_len, width = tokens.shape
    blocks_each = local_len // SPAN
    reach = -(-LAGS // blocks_each)
    step = 6.0 / (SPAN + 8)
    scale = HD ** (-0.5)

    def joined(own, other, axis):
        return jnp.concatenate(either(first_half, own, other), axis=axis)

    pair_tokens = flipped(tokens, "ctx", 1)
    far_tokens = flipped(tokens, "ctx", 2)
    feature_other = flipped(w_feature, "shard", 1)
    smalls = [norm_gain, ffn_gain, memory_gain, memory_rates, persistent]
    small_flat = jnp.concatenate([item.reshape(-1) for item in smalls])
    small_other = flipped(small_flat, "shard", 1)
    small_others = []
    start = 0
    for item in smalls:
        small_others.append(small_other[start : start + item.size].reshape(item.shape))
        start += item.size
    value_other = flipped(w_value, "shard", 1)

    gain_in_wide = joined(norm_gain, small_others[0], 0).astype(WIDE)
    gain_ffn_wide = joined(ffn_gain, small_others[1], 0).astype(WIDE)
    gain_mem = joined(memory_gain, small_others[2], 1).astype(WIDE)
    rates = joined(memory_rates, small_others[3], 0)
    persist = joined(persistent, small_others[4], 1)
    feature_cols = joined(w_feature, feature_other, 0)
    value_cols = joined(w_value, value_other, 0)
    weights = {}

    def fetch(name, array, start):
        weights[name] = flipped(after(array, start), "shard", 1)
        return weights[name]

    local_width = w_qkv.shape[2]
    local_units = feature_cols.shape[1]
    local_heads = local_width // HD
    persist_count = persist.shape[0]

    def scattered(array):
        return lax.psum_scatter(
            array.astype(NARROW), "tp", scatter_dimension=0, tiled=True
        ).astype(WIDE)

    def collected(array):
        return lax.all_gather(array.astype(NARROW), "tp", axis=0, tiled=True)

    own_units = lax.dynamic_slice_in_dim(rates.astype(WIDE), rank * local_units, local_units, 1)
    retain, moment = (own_units[0], own_units[1])
    decays = [jnp.ones_like(retain)]
    for lag in range(1, LAGS):
        decays.append(retain * decays[-1] + moment**lag)

    labels_all = segments.astype(WIDE).reshape(groups, blocks_each, SPAN) + 1.0
    lasts_all = labels_all[:, :, -1]
    late_lasts = after(lasts_all, far_tokens)
    far_lasts = flipped(late_lasts, "ctx", 2)
    lasts_around = jnp.stack(
        [lasts_all, flipped(late_lasts, "ctx", 1), far_lasts, flipped(far_lasts, "ctx", 1)]
    )

    def last_of(index):
        delta, place = divmod(index, blocks_each)
        source = part + delta
        found = pick(lasts_around, jnp.clip(source, 0, parts - 1) ^ part, 0)[:, place]
        return jnp.where(source >= 0, found, 0.0)

    before_all = jnp.stack([last_of(own - 1) for own in range(blocks_each)], axis=1)
    linked_all = []
    for own in range(blocks_each):
        for lag in range(LAGS):
            source = own - 1 - lag
            present = part + source // blocks_each >= 0
            linked_all.append(present & (last_of(source) == last_of(own - 1)))
    linked_all = jnp.stack(linked_all, axis=1).reshape(groups, blocks_each, LAGS)

    def place_of(own, lag):
        return divmod(own - 1 - lag, blocks_each)

    position = jnp.arange(SPAN)
    causal = position[:, None] >= position[None, :]

    count = groups // STREAMS
    rows = count * local_len
    blocks = count * blocks_each
    sub = rows // ranks

    def own_rows(array):
        return lax.dynamic_slice_in_dim(array, rank * sub, sub, 0)

    class Stream:
        pass

    def linked(one, square, corner):
        spread = jnp.repeat(one.linked[:, :, LAGS - 2 :: -1], SPAN, axis=2)[:, :, None]
        square = jnp.where(spread, square, jnp.zeros_like(square))
        corner = jnp.where(
            one.linked[:, :, LAGS - 1, None, None], corner, jnp.zeros_like(corner)
        )
        return square, corner

    def packed(square, corner):
        wide = square.shape[-1]
        lanes = corner.transpose(2, 0, 1, 3).reshape(CORNER, -1)
        lanes = jnp.pad(lanes, ((0, 0), (0, wide - lanes.shape[1])))
        return jnp.concatenate([square.reshape(-1, wide), lanes], axis=0)

    def unpacked(array):
        square = array[:-CORNER].reshape(count, blocks_each, SPAN, -1)
        corner = array[-CORNER:, : blocks * CORNER]
        corner = corner.reshape(CORNER, count, blocks_each, CORNER).transpose(1, 2, 0, 3)
        return square, corner

    def begin(one, index):
        def mine(array):
            return array[index * count : (index + 1) * count]

        one.flat = mine(tokens).reshape(rows, width)
        one.upstream_low = mine(out_grad).reshape(rows, width)
        one.labels = mine(labels_all)
        one.lasts = mine(lasts_all)
        one.before = mine(before_all)
        one.linked = mine(linked_all)
        one.keeping = (one.lasts == one.before).astype(WIDE)[:, :, None, None]
        one.writing = (one.labels == one.lasts[:, :, None]).astype(WIDE)[..., None]
        one.reading = (one.labels == one.before[:, :, None]).astype(WIDE)

        def features_of(piece):
            low = norm_rows(piece.astype(WIDE), gain_in_wide)[0].astype(NARROW)
            return low, matmul(low.reshape(rows, width), feature_cols)

        def shaped(values):
            return values.reshape(count, blocks_each, SPAN, local_units)

        low, one.preact = features_of(mine(tokens))
        one.input_low = low.reshape(rows, width)
        one.features = jax.nn.silu(one.preact).astype(NARROW)
        squares = jnp.sum(jnp.square(one.features.astype(WIDE)), axis=1)
        squares = jnp.sum(lax.all_gather(squares, "tp", axis=0), axis=0)
        one.key_scale = lax.rsqrt(squares + EPSILON)
        far, pair, one.features, one.key_scale = lax.optimization_barrier(
            (mine(far_tokens), mine(pair_tokens), one.features, one.key_scale)
        )
        close = [pair, flipped(far, "ctx", 1)]
        one.around = {0: shaped(one.features)}
        for delta, piece in (
            (-1, jnp.where(odd_part, close[0], close[1])),
            (1, jnp.where(odd_part, close[1], close[0])),
            (2, far),
        ):
            one.around[delta] = shaped(jax.nn.silu(features_of(piece)[1]).astype(NARROW))
        one.around[-2] = one.around[2]
        one.targets = matmul(one.input_low, value_cols).reshape(
            count, blocks_each, SPAN, local_width
        )
        weighted = [(one.around[0].astype(WIDE) * decay).astype(NARROW) for decay in decays]
        products = []
        corners = []
        for own in range(blocks_each):
            row = []
            for lag in range(LAGS - 1, -1, -1):
                delta, place = place_of(own, lag)
                near, past = weighted[lag][:, own], one.around[delta][:, place]
                if lag == LAGS - 1:
                    near, past = near[:, :CORNER], past[:, SPAN - CORNER :]
                    corners.append(batched("sth,suh->stu", near, past))
                else:
                    row.append(batched("sth,suh->stu", near, past))
            products.append(jnp.concatenate(row, axis=2))
        one.products = packed(
            jnp.stack(products, axis=1).astype(NARROW), jnp.stack(corners, axis=1).astype(NARROW)
        )
        one.mixing = lax.psum(one.products, "tp")

    def span_of(own):
        start = (reach * blocks_each - LAGS + own) * SPAN
        return slice(start, start + LAGS * SPAN)

    def remember(one):
        square, corner = linked(one, *unpacked(one.mixing))
        corner = jnp.pad(
            corner, ((0, 0), (0, 0), (0, SPAN - CORNER), (SPAN - CORNER, 0))
        )
        one.mixing = jnp.concatenate([corner, square], axis=3)
        one.scales = one.key_scale.reshape(count, blocks_each, SPAN, 1)
        halos = [
            jnp.zeros((count, blocks_each * SPAN, local_width), NARROW) for _ in range(reach)
        ]
        pending = {}
        for turn in range(parts):
            for hop in range(1, reach + 1):
                if (turn - hop, hop) in pending:
                    halos[reach - hop] = halos[reach - hop] + pending[(turn - hop, hop)]
            known = jnp.concatenate(halos, axis=1)
            recalls = []
            errors = []
            for own in range(blocks_each):
                total = batched("stu,sud->std", one.mixing[:, own], known[:, span_of(own)])
                recall = -step * one.scales[:, own] * total
                error = one.writing[:, own] * (
                    one.keeping[:, own] * recall - one.targets[:, own]
                )
                recalls.append(recall)
                errors.append(error)
                known = jnp.concatenate(
                    [known, (one.scales[:, own] * error).astype(NARROW)], axis=1
                )
            for hop in range(1, reach + 1):
                if turn + hop < parts:
                    pending[(turn, hop)] = passed_along(
                        known[:, reach * blocks_each * SPAN :], "ctx", [(turn, turn + hop)]
                    )
        one.known = known
        one.recall = jnp.stack(recalls, 1)
        one.errors = jnp.stack(errors, 1)
        heads_view = (one.reading[..., None] * one.recall).reshape(rows, local_heads, HD)
        one.head_factor = lax.rsqrt(
            jnp.mean(heads_view * heads_view, axis=-1, keepdims=True) + EPSILON
        )
        one.head_unit = heads_view * one.head_factor
        retrieved = (one.head_unit * gain_mem).reshape(rows, local_width).astype(NARROW)
        one.retrieved_full = lax.all_gather(retrieved, "tp", axis=1, tiled=True)

    def heads(values):
        return values.astype(NARROW).reshape(blocks, SPAN, local_heads, HD)

    def fixed(values):
        return jnp.broadcast_to(values, (blocks, persist_count, local_heads, HD))

    def scores_of(one):
        raw = batched("bthd,bkhd->bhtk", one.queries, one.keys) * scale
        return jnp.where(one.visible[:, None], raw, MASKED)

    def attend(one):
        one.queries = heads(matmul(one.input_low, query_w))
        one.keys = jnp.concatenate(
            [
                fixed(fixed_keys),
                heads(matmul(one.retrieved_full, key_w)),
                heads(matmul(one.input_low, key_w)),
            ],
            axis=1,
        )
        one.values = jnp.concatenate(
            [
                fixed(fixed_values),
                heads(matmul(one.retrieved_full, value_w)),
                heads(matmul(one.input_low, value_w)),
            ],
            axis=1,
        )
        label_rows = one.labels.reshape(blocks, SPAN)
        read_rows = one.reading.reshape(blocks, SPAN)
        visible_own = causal[None] & (label_rows[:, :, None] == label_rows[:, None, :])
        visible_memory = visible_own & (read_rows[:, None, :] > 0.5)
        one.visible = jnp.concatenate(
            [jnp.ones((blocks, SPAN, persist_count), jnp.bool_), visible_memory, visible_own],
            axis=2,
        )
        scores = scores_of(one)
        highest = jnp.max(scores, axis=-1, keepdims=True)
        raised = jnp.exp(scores - highest)
        totals = jnp.sum(raised, axis=-1, keepdims=True)
        one.logsum = highest + jnp.log(totals)
        probs_low = (raised / totals).astype(NARROW)
        one.attended = (
            batched("bhtk,bkhd->bthd", probs_low, one.values)
            .astype(NARROW)
            .reshape(rows, local_width)
        )
        one.residual = own_rows(one.flat).astype(WIDE)
        one.branch = scattered(matmul(one.attended, weights["out"]))

    def middle(one):
        one.hidden = one.residual + one.branch
        normed_mid, one.unit_mid, one.factor_mid = norm_rows(one.hidden, gain_ffn_wide)
        one.mid_low = collected(normed_mid)

    def feed(one):
        gate = matmul(one.mid_low, weights["gate"])
        upper = matmul(one.mid_low, weights["up"])
        one.activ = (jax.nn.silu(gate) * upper).astype(NARROW)
        grad_act = by_rows(one.upstream_low, weights["down"])
        one.grad_gate = (grad_act * upper * silu_slope(gate)).astype(NARROW)
        one.grad_upper = (grad_act * jax.nn.silu(gate)).astype(NARROW)
        one.grad_mid = scattered(
            by_rows(one.grad_gate, weights["gate"]) + by_rows(one.grad_upper, weights["up"])
        )

    def middle_back(one):
        grad_mid = one.grad_mid
        one.grad_gain_ffn = jnp.sum(grad_mid * one.unit_mid, axis=0)
        upstream = own_rows(one.upstream_low).astype(WIDE)
        one.grad_hidden = upstream + norm_back(
            grad_mid, one.unit_mid, one.factor_mid, gain_ffn_wide
        )
        one.grad_mixed = collected(one.grad_hidden)

    def branch_out(one):
        activ, one.grad_mixed = lax.optimization_barrier((one.activ, one.grad_mixed))
        one.branch = scattered(matmul(activ, weights["down"]))

    def finish_output(one):
        hidden, one.grad_retrieved = lax.optimization_barrier(
            (one.hidden + one.branch, one.grad_retrieved)
        )
        one.output = collected(hidden)

    def attend_back(one):
        grad_attended = (
            by_rows(one.grad_mixed, weights["out"])
            .astype(NARROW)
            .reshape(blocks, SPAN, local_heads, HD)
        )
        probs = jnp.exp(scores_of(one) - one.logsum)
        grad_probs = batched("bthd,bkhd->bhtk", grad_attended, one.values)
        grad_values = batched("bhtk,bthd->bkhd", probs.astype(NARROW), grad_attended)
        grad_scores = (
            probs * (grad_probs - jnp.sum(grad_probs * probs, axis=-1, keepdims=True))
        ).astype(NARROW)
        one.grad_queries = (
            (batched("bhtk,bkhd->bthd", grad_scores, one.keys) * scale)
            .astype(NARROW)
            .reshape(rows, local_width)
        )
        grad_keys = batched("bhtk,bthd->bkhd", grad_scores, one.queries) * scale

        def split_keys(grads):
            fixed_part = jnp.sum(grads[:, :persist_count], axis=0).reshape(
                persist_count, local_width
            )
            memory_part = (
                grads[:, persist_count : persist_count + SPAN]
                .astype(NARROW)
                .reshape(rows, local_width)
            )
            token_part = (
                grads[:, persist_count + SPAN :].astype(NARROW).reshape(rows, local_width)
            )
            return (fixed_part, memory_part, token_part)

        one.key_fixed, one.key_memory, one.key_token = split_keys(grad_keys)
        one.value_fixed, one.value_memory, one.value_token = split_keys(grad_values)
        partial = by_rows(one.key_memory, key_w) + by_rows(one.value_memory, value_w)
        partial, one.branch = lax.optimization_barrier((partial.astype(NARROW), one.branch))
        one.grad_retrieved = lax.psum_scatter(partial, "tp", scatter_dimension=1, tiled=True)

    def heads_back(one):
        grad_heads = one.grad_retrieved.astype(WIDE).reshape(rows, local_heads, HD)
        one.grad_gain_memory = jnp.sum(grad_heads * one.head_unit, axis=0)
        inner = grad_heads * gain_mem
        grad_masked = one.head_factor * (
            inner - one.head_unit * jnp.mean(inner * one.head_unit, axis=-1, keepdims=True)
        )
        one.grad_read = one.reading[..., None] * grad_masked.reshape(
            count, blocks_each, SPAN, local_width
        )

    def remember_back(one):
        later = [0.0] * blocks_each
        pending = {}
        for turn in range(parts):
            for hop in range(1, reach + 1):
                if (turn - hop, hop) in pending:
                    arrived = pending[(turn - hop, hop)].astype(WIDE)
                    for own in range(blocks_each):
                        later[own] = later[own] + arrived[:, own * SPAN : (own + 1) * SPAN]
            known = [0.0] * (reach * blocks_each) + later
            grad_errors = [None] * blocks_each
            grad_recalls = [None] * blocks_each
            raws = [None] * blocks_each
            for own in range(blocks_each - 1, -1, -1):
                grad_scaled = -step * known[reach * blocks_each + own]
                grad_error = one.scales[:, own] * grad_scaled
                grad_recall = (
                    one.grad_read[:, own] + one.writing[:, own] * one.keeping[:, own] * grad_error
                )
                grad_errors[own] = jnp.broadcast_to(grad_error, grad_recall.shape)
                grad_recalls[own] = grad_recall
                raws[own] = (one.scales[:, own] * grad_recall).astype(NARROW)
                carried = batched("stu,std->sud", one.mixing[:, own], raws[own])
                for index in range(LAGS):
                    place = reach * blocks_each - LAGS + own + index
                    known[place] = (
                        known[place] + carried[:, index * SPAN : (index + 1) * SPAN]
                    )
            for hop in range(1, reach + 1):
                place = parts - 1 - turn
                if place - hop >= 0:
                    start = (reach - hop) * blocks_each
                    sent = jnp.concatenate(known[start : start + blocks_each], axis=1)
                    pending[(turn, hop)] = passed_along(
                        sent.astype(NARROW), "ctx", [(place, place - hop)]
                    )
        grad_errors = jnp.stack(grad_errors, 1)
        grad_recalls = jnp.stack(grad_recalls, 1)
        one.grad_targets = (-one.writing * grad_errors).astype(NARROW).reshape(rows, local_width)
        scale_part = jnp.sum(grad_recalls * one.recall + one.errors * grad_errors, axis=3)
        one.scale_sum = jnp.sum(lax.all_gather(scale_part.reshape(rows), "tp", axis=0), axis=0)
        grad_mixing = []
        for own in range(blocks_each):
            grad_mixing.append(
                -step * batched("std,sud->stu", raws[own], one.known[:, span_of(own)])
            )
        grad_mixing = jnp.stack(grad_mixing, 1)
        square, corner = linked(
            one, grad_mixing[..., SPAN:], grad_mixing[:, :, :CORNER, SPAN - CORNER : SPAN]
        )
        grad_mixing, one.output = lax.optimization_barrier(
            (packed(square.astype(NARROW), corner.astype(NARROW)), one.output)
        )
        one.grad_mixing = lax.psum(grad_mixing, "tp")

    def features_back(one):
        square, corner = unpacked(one.grad_mixing)

        def column(own, lag):
            if lag == LAGS - 1:
                return corner[:, own]
            start = (LAGS - 2 - lag) * SPAN
            return square[:, own, :, start : start + SPAN]

        needed = {}
        for hop in range(1, reach + 1):
            sends = [(source, source - hop) for source in range(hop, parts)]
            for last_lag in (False, True):
                pairs = [
                    (own, lag)
                    for own in range(blocks_each)
                    for lag in range(LAGS)
                    if place_of(own, lag)[0] == -hop and (lag == LAGS - 1) == last_lag
                ]
                if not pairs:
                    continue
                moved = passed_along(
                    jnp.stack([column(own, lag) for own, lag in pairs], axis=1), "ctx", sends
                )
                for place, (own, lag) in enumerate(pairs):
                    needed[(hop * blocks_each + own, lag)] = moved[:, place]
        for own in range(blocks_each):
            for lag in range(LAGS):
                needed[(own, lag)] = column(own, lag)
        grad_features = []
        one.grad_decays = [0.0] * LAGS
        rest = SPAN - CORNER
        for own in range(blocks_each):
            total = 0.0
            for lag in range(LAGS):
                own_features = one.around[0][:, own].astype(WIDE)
                delta, place = place_of(own, lag)
                past = one.around[delta][:, place]
                later = own + 1 + lag
                delta, place = divmod(later, blocks_each)
                future = one.around[delta][:, place]
                if lag == LAGS - 1:
                    own_features, past, future = (
                        own_features[:, :CORNER],
                        past[:, rest:],
                        future[:, :CORNER],
                    )
                from_reads = batched("stu,suh->sth", needed[(own, lag)], past)
                one.grad_decays[lag] = one.grad_decays[lag] + jnp.sum(
                    own_features * from_reads, axis=(0, 1)
                )
                from_writes = batched("stu,sth->suh", needed[(later, lag)], future)
                if lag == LAGS - 1:
                    from_reads = jnp.pad(from_reads, ((0, 0), (0, rest), (0, 0)))
                    from_writes = jnp.pad(from_writes, ((0, 0), (rest, 0), (0, 0)))
                total = total + decays[lag] * (from_reads + from_writes)
            grad_features.append(total)
        grad_features = jnp.stack(grad_features, 1).reshape(rows, local_units)
        grad_features = grad_features - (one.key_scale * one.key_scale * one.scale_sum)[
            :, None
        ] * one.features.astype(WIDE)
        one.grad_pre = (grad_features * silu_slope(one.preact)).astype(NARROW)

    def inputs_back(one):
        grad_input = (
            by_rows(one.grad_queries, query_w)
            + by_rows(one.key_token, key_w)
            + by_rows(one.value_token, value_w)
            + by_rows(one.grad_targets, value_cols)
            + by_rows(one.grad_pre, feature_cols)
        )
        one.grad_input = scattered(grad_input)

    def tokens_back(one):
        grad_input = one.grad_input
        _, unit_in, factor_in = norm_rows(one.residual, gain_in_wide)
        one.grad_gain_in = jnp.sum(grad_input * unit_in, axis=0)
        one.grad_tokens = (
            collected(one.grad_hidden + norm_back(grad_input, unit_in, factor_in, gain_in_wide))
            .astype(WIDE)
            .reshape(count, local_len, width)
        )

    streams = [Stream() for _ in range(STREAMS)]

    def over(function):
        total = function(streams[0])
        for one in streams[1:]:
            total = total + function(one)
        return total

    def every(stage):
        for one in streams:
            stage(one)

    core, outer = (part % 2, part // 2)

    class Reduction:
        def __init__(self, array, by_row):
            array = array.astype(NARROW)
            *self.lead, self.high, self.wide = array.shape
            self.by_row = by_row
            self.axis = len(self.lead)
            if by_row:
                array = array.reshape(*self.lead, 2, 2, 2, self.high // 8, self.wide)
            else:
                array = array.reshape(2, 2, self.high // 4, self.wide)
            self.array = array
            self.exchange(core, self.axis + 1 if by_row else 0, "ctx", 1)

        def exchange(self, index, axis, over_axis, bit):
            own, other = (pick(self.array, place, axis) for place in (index, 1 - index))
            self.add(own, flipped(other, over_axis, bit))

        def add(self, own, arrived):
            self.array = (own.astype(WIDE) + arrived.astype(WIDE)).astype(NARROW)

        def across(self):
            if self.by_row:
                self.exchange(half_index, self.axis, "shard", 1)
                return
            half = self.wide // 2
            own, other = (
                lax.dynamic_slice_in_dim(self.array, place * half, half, 2)
                for place in (half_index, 1 - half_index)
            )
            self.add(own, flipped(other, "shard", 1))

        def apart(self):
            self.exchange(outer, self.axis if self.by_row else 0, "ctx", 2)

        def together(self):
            pair = either(outer == 0, self.array, flipped(self.array, "ctx", 2))
            self.array = jnp.stack(pair, axis=self.axis if self.by_row else 0)

        def result(self):
            pair = either(core == 0, self.array, flipped(self.array, "ctx", 1))
            array = jnp.stack(pair, axis=self.axis if self.by_row else 0).astype(WIDE)
            if self.by_row:
                return array.reshape(*self.lead, self.high // 2, self.wide)
            return array.reshape(self.high, self.wide // 2)

    def tied(names, *reductions):
        held = [[getattr(one, name) for name in names] for one in streams]
        held, arrays = lax.optimization_barrier((held, [item.array for item in reductions]))
        for one, values in zip(streams, held):
            for name, value in zip(names, values):
                setattr(one, name, value)
        for item, array in zip(reductions, arrays):
            item.array = array

    class Holder:
        def __init__(self, array):
            self.array = array

    def fetched(names, *arrays):
        holders = [Holder(fetch(str(index), item, start)) for index, (item, start) in enumerate(arrays)]
        tied(names, *holders)
        return [holder.array for holder in holders]

    for index, one in enumerate(streams):
        begin(one, index)
    last = streams[-1]
    (qkv_other,) = fetched(["mixing"], (w_qkv, last.products))
    qkv_cols = joined(w_qkv, qkv_other, 1)
    query_w = qkv_cols[0]
    key_w = qkv_cols[1]
    value_w = qkv_cols[2]
    fixed_keys = matmul(persist, key_w).astype(NARROW).reshape(1, persist_count, local_heads, HD)
    fixed_values = (
        matmul(persist, value_w).astype(NARROW).reshape(1, persist_count, local_heads, HD)
    )
    every(remember)
    out_other, down_other = fetched(
        ["retrieved_full"], (w_out, last.recall), (w_down, last.recall)
    )
    weights["out"] = joined(w_out, out_other, 1)
    weights["down"] = joined(w_down, down_other, 1)
    every(attend)
    (gate_other,) = fetched(["branch"], (w_gate_up[0], last.attended))
    weights["gate"] = joined(w_gate_up[0], gate_other, 0)
    every(middle)
    (up_other,) = fetched(["mid_low"], (w_gate_up[1], last.hidden))
    weights["up"] = joined(w_gate_up[1], up_other, 0)
    every(feed)
    feed_reductions = [
        Reduction(over(lambda one: over_rows(one.activ, one.upstream_low)), False),
        Reduction(
            jnp.stack(
                [
                    over(lambda one: over_rows(one.mid_low, one.grad_gate)).astype(NARROW),
                    over(lambda one: over_rows(one.mid_low, one.grad_upper)).astype(NARROW),
                ]
            ),
            True,
        ),
    ]
    tied(["grad_mid"], *feed_reductions)
    every(middle_back)
    for item in feed_reductions:
        item.across()
    tied(["grad_mixed"], *feed_reductions)
    every(branch_out)
    every(attend_back)
    persist_wide = persist.astype(WIDE)
    key_fixed = over(lambda one: one.key_fixed)
    value_fixed = over(lambda one: one.value_fixed)
    grad_query_w = over(lambda one: over_rows(one.input_low, one.grad_queries))
    grad_key_w = over(
        lambda one: over_rows(one.input_low, one.key_token)
        + over_rows(one.retrieved_full, one.key_memory)
    ) + exact_product(persist_wide.T, key_fixed)
    grad_value_proj = over(
        lambda one: over_rows(one.input_low, one.value_token)
        + over_rows(one.retrieved_full, one.value_memory)
    ) + exact_product(persist_wide.T, value_fixed)
    mix_reductions = [
        Reduction(over(lambda one: over_rows(one.attended, one.grad_mixed)), False),
        Reduction(
            jnp.stack(
                [item.astype(NARROW) for item in (grad_query_w, grad_key_w, grad_value_proj)]
            ),
            True,
        ),
    ]
    grad_persist = exact_product(key_fixed, key_w.astype(WIDE).T) + exact_product(
        value_fixed, value_w.astype(WIDE).T
    )
    for item in feed_reductions:
        item.apart()
    tied(["grad_retrieved"], *feed_reductions, *mix_reductions)
    every(finish_output)
    every(heads_back)
    every(remember_back)
    grad_persist = after(grad_persist, last.grad_mixing)
    grad_persist = lax.psum_scatter(grad_persist, "tp", scatter_dimension=0, tiled=True)
    target_reduction = Reduction(over(lambda one: over_rows(one.input_low, one.grad_targets)), True)
    for item in feed_reductions:
        item.together()
    for item in mix_reductions:
        item.across()
    tied(["grad_mixing", "scale_sum"], *feed_reductions, *mix_reductions, target_reduction)
    every(features_back)
    every(inputs_back)

    grad_decays = [over(lambda one: one.grad_decays[lag]) for lag in range(LAGS)]
    grad_retain = 0.0
    grad_moment = 0.0
    retain_slope = jnp.zeros_like(retain)
    for lag in range(1, LAGS):
        retain_slope = retain * retain_slope + decays[lag - 1]
        moment_slope = 0.0
        for power in range(1, lag + 1):
            moment_slope = moment_slope + power * retain ** (lag - power) * moment ** (power - 1)
        grad_retain = grad_retain + retain_slope * grad_decays[lag]
        grad_moment = grad_moment + moment_slope * grad_decays[lag]
    grad_rates = jnp.stack([grad_retain, grad_moment])

    def summed(pieces):
        small = jnp.concatenate([piece.reshape(-1) for piece in pieces])
        for axis, bit in (("ctx", 1), ("shard", 1), ("ctx", 2)):
            small = small + flipped(small, axis, bit)
        return small

    small = summed(
        [
            grad_persist,
            over(lambda one: one.grad_gain_ffn),
            over(lambda one: one.grad_gain_memory),
            grad_rates,
        ]
    )
    cut = grad_persist.size + width
    spread = Holder(lax.all_gather(small[:cut], "tp", axis=0))
    feature_reduction = Reduction(over(lambda one: over_rows(one.input_low, one.grad_pre)), True)
    late_reductions = [feature_reduction, target_reduction]
    for item in mix_reductions:
        item.apart()
    for item in late_reductions:
        item.across()
    tied(["grad_input"], spread, *mix_reductions, *late_reductions)
    every(tokens_back)
    for item in mix_reductions:
        item.together()
    for item in late_reductions:
        item.apart()
        item.together()
    small_in = lax.all_gather(summed([over(lambda one: one.grad_gain_in)]), "tp", axis=0)
    grad_persist = spread.array[:, : grad_persist.size].reshape(persist_count, width)
    gain_ffn_sum = jnp.sum(spread.array[:, cut - width :], axis=0)
    gain_in_sum = jnp.sum(small_in, axis=0)
    middle_cut = cut + local_heads * HD
    grad_gain_memory = small[cut:middle_cut].reshape(local_heads, HD)
    grad_rates = small[middle_cut:].reshape(2, local_units)
    grad_down, grad_gate_up = [item.result() for item in feed_reductions]
    grad_out_rows, grad_qkv = [item.result() for item in mix_reductions]
    grad_feature_w, grad_target_w = [item.result() for item in late_reductions]

    def own_half(array, axis):
        size = array.shape[axis] // 2
        return lax.dynamic_slice_in_dim(array, half_index * size, size, axis)

    return (
        jnp.concatenate([one.output for one in streams], axis=0).reshape(tokens.shape),
        jnp.concatenate([one.grad_tokens for one in streams], axis=0),
        own_half(gain_in_sum, 0),
        own_half(gain_ffn_sum, 0),
        own_half(grad_gain_memory, 1),
        own_half(grad_rates, 0),
        own_half(grad_persist, 1),
        grad_qkv,
        grad_out_rows,
        grad_target_w,
        grad_feature_w,
        grad_gate_up,
        grad_down,
    )


def solution(mesh):
    placed = (
        P("shard", "ctx", None),
        P("shard", "ctx"),
        P("shard"),
        P("shard"),
        P("tp", "shard"),
        P("shard", None),
        P(None, "shard"),
        P(None, "shard", "tp"),
        P("tp", "shard"),
        P("shard", "tp"),
        P("shard", "tp"),
        P(None, "shard", "tp"),
        P("tp", "shard"),
        P("shard", "ctx", None),
    )
    return jax.shard_map(
        on_device,
        mesh=mesh,
        in_specs=placed,
        out_specs=(
            P("shard", "ctx", None),
            P("shard", "ctx", None),
            P("shard"),
            P("shard"),
            P("tp", "shard"),
            P("shard", "tp"),
            P(None, "shard"),
            P(None, "shard", "tp"),
            P("tp", "shard"),
            P("shard", "tp"),
            P("shard", "tp"),
            P(None, "shard", "tp"),
            P("tp", "shard"),
        ),
        check_vma=False,
    )
```

```python
import jax
import jax.numpy as jnp
from jax import lax
from jax.sharding import PartitionSpec as P

HD = 96
SPAN = 256
LIMIT = 800
LAGS = (LIMIT + SPAN - 2) // SPAN
CORNER = LIMIT - (LAGS - 1) * SPAN
STREAMS = 2


EPSILON = 1e-06
MASKED = -1e30
WIDE = jnp.float32
NARROW = jnp.bfloat16


def passed_along(value, axis, pairs):
    return lax.ppermute(value, axis, pairs)


def flipped(value, axis, bit):
    return lax.ppermute(value, axis, [(i, i ^ bit) for i in range(lax.axis_size(axis))])


def either(first, one, other):
    return jnp.where(first, one, other), jnp.where(first, other, one)


def pick(array, place, axis):
    return lax.dynamic_index_in_dim(array, place, axis, keepdims=False)


def after(value, *others):
    return lax.optimization_barrier((value, *others))[0]


def norm_rows(values, gain):
    factor = lax.rsqrt(jnp.mean(values * values, axis=-1, keepdims=True) + EPSILON)
    normed = values * factor
    return (normed * gain, normed, factor)


def norm_back(upstream, normed, factor, gain):
    inner = upstream * gain
    return factor * (inner - normed * jnp.mean(inner * normed, axis=-1, keepdims=True))


def silu_slope(values):
    sigmoid = jax.nn.sigmoid(values)
    return sigmoid * (1.0 + values * (1.0 - sigmoid))


def matmul(left, right):
    return jnp.dot(left, right, preferred_element_type=WIDE)


def over_rows(left, right):
    return lax.dot_general(left, right, (((0,), (0,)), ((), ())), preferred_element_type=WIDE)


def by_rows(left, right):
    return lax.dot_general(left, right, (((1,), (1,)), ((), ())), preferred_element_type=WIDE)


def exact_product(left, right):
    return jnp.dot(left, right, precision=lax.Precision.HIGHEST, preferred_element_type=WIDE)


def batched(spec, left, right):
    return jnp.einsum(spec, left, right, preferred_element_type=WIDE)


def on_device(
    tokens,
    segments,
    norm_gain,
    ffn_gain,
    memory_gain,
    memory_rates,
    persistent,
    w_qkv,
    w_out,
    w_value,
    w_feature,
    w_gate_up,
    w_down,
    out_grad,
):
    parts, ranks = (lax.axis_size("ctx"), lax.axis_size("tp"))
    part, rank = (lax.axis_index("ctx"), lax.axis_index("tp"))
    half_index = lax.axis_index("shard")
    first_half = half_index == 0
    odd_part = part % 2 == 1
    groups, local_len, width = tokens.shape
    blocks_each = local_len // SPAN
    reach = -(-LAGS // blocks_each)
    step = 6.0 / (SPAN + 8)
    scale = HD ** (-0.5)

    def joined(own, other, axis):
        return jnp.concatenate(either(first_half, own, other), axis=axis)

    pair_tokens = flipped(tokens, "ctx", 1)
    far_tokens = flipped(tokens, "ctx", 2)
    core, outer = (part % 2, part // 2)
    feature_half = pick(w_feature.reshape(2, -1, w_feature.shape[1]), core, 0)
    feature_half = flipped(feature_half, "shard", 1)
    feature_other = jnp.concatenate(
        either(core == 0, feature_half, flipped(feature_half, "ctx", 1)), axis=0
    )
    smalls = [norm_gain, ffn_gain, memory_gain, memory_rates, persistent]
    small_flat = jnp.concatenate([item.reshape(-1) for item in smalls])
    small_other = flipped(small_flat, "shard", 1)
    small_others = []
    start = 0
    for item in smalls:
        small_others.append(small_other[start : start + item.size].reshape(item.shape))
        start += item.size
    value_other = flipped(after(w_value, feature_half), "shard", 1)

    gain_in_wide = joined(norm_gain, small_others[0], 0).astype(WIDE)
    gain_ffn_wide = joined(ffn_gain, small_others[1], 0).astype(WIDE)
    gain_mem = joined(memory_gain, small_others[2], 1).astype(WIDE)
    rates = joined(memory_rates, small_others[3], 0)
    persist = joined(persistent, small_others[4], 1)
    feature_cols = joined(w_feature, feature_other, 0)
    value_cols = joined(w_value, value_other, 0)
    weights = {}
    local_width = w_qkv.shape[2]
    local_units = feature_cols.shape[1]
    local_heads = local_width // HD
    persist_count = persist.shape[0]

    def scattered(array):
        return lax.psum_scatter(
            array.astype(NARROW), "tp", scatter_dimension=0, tiled=True
        ).astype(WIDE)

    def collected(array):
        return lax.all_gather(array.astype(NARROW), "tp", axis=0, tiled=True)

    def summed_over_ranks(array):
        bit = 1
        while bit < ranks:
            array = array + flipped(array, "tp", bit)
            bit *= 2
        return array

    own_units = lax.dynamic_slice_in_dim(rates.astype(WIDE), rank * local_units, local_units, 1)
    retain, moment = (own_units[0], own_units[1])
    decays = [jnp.ones_like(retain)]
    for lag in range(1, LAGS):
        decays.append(retain * decays[-1] + moment**lag)

    labels_all = segments.astype(WIDE).reshape(groups, blocks_each, SPAN) + 1.0
    lasts_all = labels_all[:, :, -1]
    late_lasts = after(lasts_all, far_tokens)
    far_lasts = flipped(late_lasts, "ctx", 2)
    lasts_around = jnp.stack(
        [lasts_all, flipped(late_lasts, "ctx", 1), far_lasts, flipped(far_lasts, "ctx", 1)]
    )

    def last_of(index):
        delta, place = divmod(index, blocks_each)
        source = part + delta
        found = pick(lasts_around, jnp.clip(source, 0, parts - 1) ^ part, 0)[:, place]
        return jnp.where(source >= 0, found, 0.0)

    before_all = jnp.stack([last_of(own - 1) for own in range(blocks_each)], axis=1)
    linked_all = []
    for own in range(blocks_each):
        for lag in range(LAGS):
            source = own - 1 - lag
            present = part + source // blocks_each >= 0
            linked_all.append(present & (last_of(source) == last_of(own - 1)))
    linked_all = jnp.stack(linked_all, axis=1).reshape(groups, blocks_each, LAGS)

    def place_of(own, lag):
        return divmod(own - 1 - lag, blocks_each)

    position = jnp.arange(SPAN)
    causal = position[:, None] >= position[None, :]

    count = groups
    rows = count * local_len
    blocks = count * blocks_each
    part_rows = rows // STREAMS
    part_blocks = blocks // STREAMS

    def own_rows(array):
        sub = array.shape[0] // ranks
        return lax.dynamic_slice_in_dim(array, rank * sub, sub, 0)

    class Stream:
        pass

    def linked(one, square, corner):
        spread = jnp.repeat(one.linked[:, :, LAGS - 2 :: -1], SPAN, axis=2)[:, :, None]
        square = jnp.where(spread, square, jnp.zeros_like(square))
        corner = jnp.where(
            one.linked[:, :, LAGS - 1, None, None], corner, jnp.zeros_like(corner)
        )
        return square, corner

    def packed(square, corner):
        wide = square.shape[-1]
        lanes = corner.transpose(2, 0, 1, 3).reshape(CORNER, -1)
        lanes = jnp.pad(lanes, ((0, 0), (0, wide - lanes.shape[1])))
        return jnp.concatenate([square.reshape(-1, wide), lanes], axis=0)

    def unpacked(array):
        square = array[:-CORNER].reshape(count, blocks_each, SPAN, -1)
        corner = array[-CORNER:, : blocks * CORNER]
        corner = corner.reshape(CORNER, count, blocks_each, CORNER).transpose(1, 2, 0, 3)
        return square, corner

    def begin(one, index):
        def mine(array):
            return array[index * count : (index + 1) * count]

        one.flat = mine(tokens).reshape(rows, width)
        one.upstream_low = mine(out_grad).reshape(rows, width)
        one.labels = mine(labels_all)
        one.lasts = mine(lasts_all)
        one.before = mine(before_all)
        one.linked = mine(linked_all)
        one.keeping = (one.lasts == one.before).astype(WIDE)[:, :, None, None]
        one.writing = (one.labels == one.lasts[:, :, None]).astype(WIDE)[..., None]
        one.reading = (one.labels == one.before[:, :, None]).astype(WIDE)

        def features_of(piece):
            low = norm_rows(piece.astype(WIDE), gain_in_wide)[0].astype(NARROW)
            return low, matmul(low.reshape(rows, width), feature_cols)

        def shaped(values):
            return values.reshape(count, blocks_each, SPAN, local_units)

        low, one.preact = features_of(mine(tokens))
        one.input_low = low.reshape(rows, width)
        one.features = jax.nn.silu(one.preact).astype(NARROW)
        squares = jnp.sum(jnp.square(one.features.astype(WIDE)), axis=1)
        one.key_scale = lax.rsqrt(summed_over_ranks(squares) + EPSILON)
        far, pair, one.features, one.key_scale = lax.optimization_barrier(
            (mine(far_tokens), mine(pair_tokens), one.features, one.key_scale)
        )
        close = [pair, flipped(far, "ctx", 1)]
        one.around = {0: shaped(one.features)}
        for delta, piece in (
            (-1, jnp.where(odd_part, close[0], close[1])),
            (1, jnp.where(odd_part, close[1], close[0])),
            (2, far),
        ):
            one.around[delta] = shaped(jax.nn.silu(features_of(piece)[1]).astype(NARROW))
        one.around[-2] = one.around[2]
        one.targets = matmul(one.input_low, value_cols).reshape(
            count, blocks_each, SPAN, local_width
        )
        weighted = [(one.around[0].astype(WIDE) * decay).astype(NARROW) for decay in decays]
        products = []
        corners = []
        for own in range(blocks_each):
            row = []
            for lag in range(LAGS - 1, -1, -1):
                delta, place = place_of(own, lag)
                near, past = weighted[lag][:, own], one.around[delta][:, place]
                if lag == LAGS - 1:
                    near, past = near[:, :CORNER], past[:, SPAN - CORNER :]
                    corners.append(batched("sth,suh->stu", near, past))
                else:
                    row.append(batched("sth,suh->stu", near, past))
            products.append(jnp.concatenate(row, axis=2))
        one.products = packed(
            jnp.stack(products, axis=1).astype(NARROW), jnp.stack(corners, axis=1).astype(NARROW)
        )
        one.mixing = lax.psum(one.products, "tp")

    def span_of(own):
        start = (reach * blocks_each - LAGS + own) * SPAN
        return slice(start, start + LAGS * SPAN)

    def remember(one):
        square, corner = linked(one, *unpacked(one.mixing))
        corner = jnp.pad(
            corner, ((0, 0), (0, 0), (0, SPAN - CORNER), (SPAN - CORNER, 0))
        )
        one.mixing = jnp.concatenate([corner, square], axis=3)
        one.scales = one.key_scale.reshape(count, blocks_each, SPAN, 1)
        halos = [
            jnp.zeros((count, blocks_each * SPAN, local_width), NARROW) for _ in range(reach)
        ]
        pending = {}
        for turn in range(parts):
            for hop in range(1, reach + 1):
                if (turn - hop, hop) in pending:
                    halos[reach - hop] = halos[reach - hop] + pending[(turn - hop, hop)]
            known = jnp.concatenate(halos, axis=1)
            recalls = []
            errors = []
            for own in range(blocks_each):
                total = batched("stu,sud->std", one.mixing[:, own], known[:, span_of(own)])
                recall = -step * one.scales[:, own] * total
                error = one.writing[:, own] * (
                    one.keeping[:, own] * recall - one.targets[:, own]
                )
                recalls.append(recall)
                errors.append(error)
                known = jnp.concatenate(
                    [known, (one.scales[:, own] * error).astype(NARROW)], axis=1
                )
            for hop in range(1, reach + 1):
                if turn + hop < parts:
                    pending[(turn, hop)] = passed_along(
                        known[:, reach * blocks_each * SPAN :], "ctx", [(turn, turn + hop)]
                    )
        one.known = known
        one.recall = jnp.stack(recalls, 1)
        one.errors = jnp.stack(errors, 1)
        heads_view = (one.reading[..., None] * one.recall).reshape(rows, local_heads, HD)
        one.head_factor = lax.rsqrt(
            jnp.mean(heads_view * heads_view, axis=-1, keepdims=True) + EPSILON
        )
        one.head_unit = heads_view * one.head_factor
        retrieved = (one.head_unit * gain_mem).reshape(rows, local_width).astype(NARROW)
        one.retrieved_full = lax.all_gather(retrieved, "tp", axis=1, tiled=True)

    def heads(values):
        return values.astype(NARROW).reshape(-1, SPAN, local_heads, HD)

    def fixed(values):
        return jnp.broadcast_to(values, (part_blocks, persist_count, local_heads, HD))

    def scores_of(one):
        raw = batched("bthd,bkhd->bhtk", one.queries, one.keys) * scale
        return jnp.where(one.visible[:, None], raw, MASKED)

    def attend(one):
        one.queries = heads(matmul(one.input_low, query_w))
        one.keys = jnp.concatenate(
            [
                fixed(fixed_keys),
                heads(matmul(one.retrieved_full, key_w)),
                heads(matmul(one.input_low, key_w)),
            ],
            axis=1,
        )
        one.values = jnp.concatenate(
            [
                fixed(fixed_values),
                heads(matmul(one.retrieved_full, value_w)),
                heads(matmul(one.input_low, value_w)),
            ],
            axis=1,
        )
        label_rows = one.labels.reshape(part_blocks, SPAN)
        read_rows = one.reading.reshape(part_blocks, SPAN)
        visible_own = causal[None] & (label_rows[:, :, None] == label_rows[:, None, :])
        visible_memory = visible_own & (read_rows[:, None, :] > 0.5)
        one.visible = jnp.concatenate(
            [jnp.ones((part_blocks, SPAN, persist_count), jnp.bool_), visible_memory, visible_own],
            axis=2,
        )
        scores = scores_of(one)
        highest = jnp.max(scores, axis=-1, keepdims=True)
        raised = jnp.exp(scores - highest)
        totals = jnp.sum(raised, axis=-1, keepdims=True)
        one.logsum = highest + jnp.log(totals)
        probs_low = (raised / totals).astype(NARROW)
        one.attended = (
            batched("bhtk,bkhd->bthd", probs_low, one.values)
            .astype(NARROW)
            .reshape(part_rows, local_width)
        )
        one.residual = own_rows(one.flat).astype(WIDE)
        one.branch = scattered(matmul(one.attended, weights["out"]))

    def middle(one):
        if one is not streams[0]:
            one.branch = after(one.branch, streams[0].mid_own)
        one.hidden = one.residual + one.branch
        normed_mid, one.unit_mid, one.factor_mid = norm_rows(one.hidden, gain_ffn_wide)
        one.mid_own = normed_mid.astype(NARROW)
        one.mid_low = collected(one.mid_own)

    def feed(one):
        gate = matmul(one.mid_low, weights["gate"])
        upper = matmul(one.mid_low, weights["up"])
        one.activ = (jax.nn.silu(gate) * upper).astype(NARROW)
        grad_act = by_rows(one.upstream_low, weights["down"])
        one.grad_gate = (grad_act * upper * silu_slope(gate)).astype(NARROW)
        one.grad_upper = (grad_act * jax.nn.silu(gate)).astype(NARROW)
        one.grad_mid = scattered(
            by_rows(one.grad_gate, weights["gate"]) + by_rows(one.grad_upper, weights["up"])
        )

    def middle_back(one):
        if one is not streams[0]:
            one.grad_mid = after(one.grad_mid, streams[0].grad_hidden)
        grad_mid = one.grad_mid
        one.grad_gain_ffn = jnp.sum(grad_mid * one.unit_mid, axis=0)
        upstream = own_rows(one.upstream_low).astype(WIDE)
        one.grad_hidden = upstream + norm_back(
            grad_mid, one.unit_mid, one.factor_mid, gain_ffn_wide
        )
        one.grad_mixed = collected(one.grad_hidden)

    def branch_out(one):
        activ = after(one.activ, whole.grad_retrieved)
        one.branch = scattered(matmul(activ, weights["down"]))

    def finish_output(one):
        one.output = collected(after(one.hidden + one.branch, whole.grad_mixing))

    def attend_back(one):
        grad_attended = (
            by_rows(one.grad_mixed, weights["out"])
            .astype(NARROW)
            .reshape(part_blocks, SPAN, local_heads, HD)
        )
        probs = jnp.exp(scores_of(one) - one.logsum)
        grad_probs = batched("bthd,bkhd->bhtk", grad_attended, one.values)
        grad_values = batched("bhtk,bthd->bkhd", probs.astype(NARROW), grad_attended)
        grad_scores = (
            probs * (grad_probs - jnp.sum(grad_probs * probs, axis=-1, keepdims=True))
        ).astype(NARROW)
        one.grad_queries = (
            (batched("bhtk,bkhd->bthd", grad_scores, one.keys) * scale)
            .astype(NARROW)
            .reshape(part_rows, local_width)
        )
        grad_keys = batched("bhtk,bthd->bkhd", grad_scores, one.queries) * scale

        def split_keys(grads):
            fixed_part = jnp.sum(grads[:, :persist_count], axis=0).reshape(
                persist_count, local_width
            )
            memory_part = (
                grads[:, persist_count : persist_count + SPAN]
                .astype(NARROW)
                .reshape(part_rows, local_width)
            )
            token_part = (
                grads[:, persist_count + SPAN :].astype(NARROW).reshape(part_rows, local_width)
            )
            return (fixed_part, memory_part, token_part)

        one.key_fixed, one.key_memory, one.key_token = split_keys(grad_keys)
        one.value_fixed, one.value_memory, one.value_token = split_keys(grad_values)
        partial = by_rows(one.key_memory, key_w) + by_rows(one.value_memory, value_w)
        one.partial = partial.astype(NARROW)
        one.grad_retrieved = lax.psum_scatter(one.partial, "tp", scatter_dimension=1, tiled=True)

    def heads_back(one):
        grad_heads = one.grad_retrieved.astype(WIDE).reshape(rows, local_heads, HD)
        one.grad_gain_memory = jnp.sum(grad_heads * one.head_unit, axis=0)
        inner = grad_heads * gain_mem
        grad_masked = one.head_factor * (
            inner - one.head_unit * jnp.mean(inner * one.head_unit, axis=-1, keepdims=True)
        )
        one.grad_read = one.reading[..., None] * grad_masked.reshape(
            count, blocks_each, SPAN, local_width
        )

    def remember_back(one):
        later = [0.0] * blocks_each
        pending = {}
        for turn in range(parts):
            for hop in range(1, reach + 1):
                if (turn - hop, hop) in pending:
                    arrived = pending[(turn - hop, hop)].astype(WIDE)
                    for own in range(blocks_each):
                        later[own] = later[own] + arrived[:, own * SPAN : (own + 1) * SPAN]
            known = [0.0] * (reach * blocks_each) + later
            grad_errors = [None] * blocks_each
            grad_recalls = [None] * blocks_each
            raws = [None] * blocks_each
            for own in range(blocks_each - 1, -1, -1):
                grad_scaled = -step * known[reach * blocks_each + own]
                grad_error = one.scales[:, own] * grad_scaled
                grad_recall = (
                    one.grad_read[:, own] + one.writing[:, own] * one.keeping[:, own] * grad_error
                )
                grad_errors[own] = jnp.broadcast_to(grad_error, grad_recall.shape)
                grad_recalls[own] = grad_recall
                raws[own] = (one.scales[:, own] * grad_recall).astype(NARROW)
                carried = batched("stu,std->sud", one.mixing[:, own], raws[own])
                for index in range(LAGS):
                    place = reach * blocks_each - LAGS + own + index
                    known[place] = (
                        known[place] + carried[:, index * SPAN : (index + 1) * SPAN]
                    )
            for hop in range(1, reach + 1):
                place = parts - 1 - turn
                if place - hop >= 0:
                    start = (reach - hop) * blocks_each
                    sent = jnp.concatenate(known[start : start + blocks_each], axis=1)
                    pending[(turn, hop)] = passed_along(
                        sent.astype(NARROW), "ctx", [(place, place - hop)]
                    )
        grad_errors = jnp.stack(grad_errors, 1)
        grad_recalls = jnp.stack(grad_recalls, 1)
        one.grad_targets = (-one.writing * grad_errors).astype(NARROW).reshape(rows, local_width)
        scale_part = jnp.sum(grad_recalls * one.recall + one.errors * grad_errors, axis=3)
        one.scale_sum = summed_over_ranks(scale_part.reshape(rows))
        grad_mixing = []
        for own in range(blocks_each):
            grad_mixing.append(
                -step * batched("std,sud->stu", raws[own], one.known[:, span_of(own)])
            )
        grad_mixing = jnp.stack(grad_mixing, 1)
        square, corner = linked(
            one, grad_mixing[..., SPAN:], grad_mixing[:, :, :CORNER, SPAN - CORNER : SPAN]
        )
        grad_mixing = packed(square.astype(NARROW), corner.astype(NARROW))
        branches = [item.branch for item in streams]
        grad_mixing, branches = lax.optimization_barrier((grad_mixing, branches))
        for item, branch in zip(streams, branches):
            item.branch = branch
        one.grad_mixing = lax.psum(grad_mixing, "tp")

    def features_back(one):
        square, corner = unpacked(one.grad_mixing)

        def column(own, lag):
            if lag == LAGS - 1:
                return corner[:, own]
            start = (LAGS - 2 - lag) * SPAN
            return square[:, own, :, start : start + SPAN]

        needed = {}
        for hop in range(1, reach + 1):
            sends = [(source, source - hop) for source in range(hop, parts)]
            for last_lag in (False, True):
                pairs = [
                    (own, lag)
                    for own in range(blocks_each)
                    for lag in range(LAGS)
                    if place_of(own, lag)[0] == -hop and (lag == LAGS - 1) == last_lag
                ]
                if not pairs:
                    continue
                moved = passed_along(
                    jnp.stack([column(own, lag) for own, lag in pairs], axis=1), "ctx", sends
                )
                for place, (own, lag) in enumerate(pairs):
                    needed[(hop * blocks_each + own, lag)] = moved[:, place]
        for own in range(blocks_each):
            for lag in range(LAGS):
                needed[(own, lag)] = column(own, lag)
        grad_features = []
        one.grad_decays = [0.0] * LAGS
        rest = SPAN - CORNER
        for own in range(blocks_each):
            total = 0.0
            for lag in range(LAGS):
                own_features = one.around[0][:, own].astype(WIDE)
                delta, place = place_of(own, lag)
                past = one.around[delta][:, place]
                later = own + 1 + lag
                delta, place = divmod(later, blocks_each)
                future = one.around[delta][:, place]
                if lag == LAGS - 1:
                    own_features, past, future = (
                        own_features[:, :CORNER],
                        past[:, rest:],
                        future[:, :CORNER],
                    )
                from_reads = batched("stu,suh->sth", needed[(own, lag)], past)
                one.grad_decays[lag] = one.grad_decays[lag] + jnp.sum(
                    own_features * from_reads, axis=(0, 1)
                )
                from_writes = batched("stu,sth->suh", needed[(later, lag)], future)
                if lag == LAGS - 1:
                    from_reads = jnp.pad(from_reads, ((0, 0), (0, rest), (0, 0)))
                    from_writes = jnp.pad(from_writes, ((0, 0), (rest, 0), (0, 0)))
                total = total + decays[lag] * (from_reads + from_writes)
            grad_features.append(total)
        grad_features = jnp.stack(grad_features, 1).reshape(rows, local_units)
        grad_features = grad_features - (one.key_scale * one.key_scale * one.scale_sum)[
            :, None
        ] * one.features.astype(WIDE)
        one.grad_pre = (grad_features * silu_slope(one.preact)).astype(NARROW)

    def inputs_back(one):
        one.grad_input = (one.early + by_rows(one.grad_pre, feature_cols)).astype(NARROW)

    def input_early(one):
        one.early = (
            by_rows(one.grad_queries, query_w)
            + by_rows(one.key_token, key_w)
            + by_rows(one.value_token, value_w)
            + by_rows(one.grad_targets, value_cols)
        )

    def tokens_back(one):
        if one is not streams[0]:
            one.grad_input = after(one.grad_input, streams[0].grad_own)
        grad_input = one.grad_input
        _, unit_in, factor_in = norm_rows(one.residual, gain_in_wide)
        one.grad_gain_in = jnp.sum(grad_input * unit_in, axis=0)
        grad_own = one.grad_hidden + norm_back(grad_input, unit_in, factor_in, gain_in_wide)
        one.grad_own = grad_own.astype(NARROW)
        one.grad_tokens = collected(one.grad_own).astype(WIDE).reshape(-1, local_len, width)

    whole = Stream()
    streams = [Stream() for _ in range(STREAMS)]

    def over(function):
        total = function(streams[0])
        for one in streams[1:]:
            total = total + function(one)
        return total

    def every(stage):
        for one in streams:
            stage(one)

    class Reduction:
        def __init__(self, array, by_row):
            array = array.astype(NARROW)
            *self.lead, self.high, self.wide = array.shape
            self.by_row = by_row
            self.axis = len(self.lead)
            if by_row:
                array = array.reshape(*self.lead, 2, 2, 2, self.high // 8, self.wide)
            else:
                array = array.reshape(2, 2, self.high // 4, self.wide)
            self.array = array
            self.exchange(core, self.axis + 1 if by_row else 0, "ctx", 1)

        def exchange(self, index, axis, over_axis, bit):
            own, other = (pick(self.array, place, axis) for place in (index, 1 - index))
            self.add(own, flipped(other, over_axis, bit))

        def add(self, own, arrived):
            self.array = (own.astype(WIDE) + arrived.astype(WIDE)).astype(NARROW)

        def across(self):
            if self.by_row:
                self.exchange(half_index, self.axis, "shard", 1)
                return
            half = self.wide // 2
            own, other = (
                lax.dynamic_slice_in_dim(self.array, place * half, half, 2)
                for place in (half_index, 1 - half_index)
            )
            self.add(own, flipped(other, "shard", 1))

        def apart(self):
            self.exchange(outer, self.axis if self.by_row else 0, "ctx", 2)

        def together(self):
            pair = either(outer == 0, self.array, flipped(self.array, "ctx", 2))
            self.array = jnp.stack(pair, axis=self.axis if self.by_row else 0)

        def result(self):
            pair = either(core == 0, self.array, flipped(self.array, "ctx", 1))
            array = jnp.stack(pair, axis=self.axis if self.by_row else 0).astype(WIDE)
            if self.by_row:
                return array.reshape(*self.lead, self.high // 2, self.wide)
            return array.reshape(self.high, self.wide // 2)

    def tied(one, names, *reductions):
        held = [getattr(one, name) for name in names]
        held, arrays = lax.optimization_barrier((held, [item.array for item in reductions]))
        for name, value in zip(names, held):
            setattr(one, name, value)
        for item, array in zip(reductions, arrays):
            item.array = array

    class Holder:
        def __init__(self, array):
            self.array = array

    def fetched(one, names, start, *arrays):
        holders = [Holder(flipped(after(item, start), "shard", 1)) for item in arrays]
        tied(one, names, *holders)
        return [holder.array for holder in holders]

    def merged(name):
        setattr(
            whole, name, jnp.concatenate([getattr(one, name) for one in streams], axis=0)
        )

    begin(whole, 0)
    (qkv_other,) = fetched(whole, ["mixing"], whole.products, w_qkv)
    qkv_cols = joined(w_qkv, qkv_other, 1)
    query_w = qkv_cols[0]
    key_w = qkv_cols[1]
    value_w = qkv_cols[2]
    fixed_keys = matmul(persist, key_w).astype(NARROW).reshape(1, persist_count, local_heads, HD)
    fixed_values = (
        matmul(persist, value_w).astype(NARROW).reshape(1, persist_count, local_heads, HD)
    )
    remember(whole)
    out_other, down_other = fetched(whole, ["retrieved_full"], whole.recall, w_out, w_down)
    weights["out"] = joined(w_out, out_other, 1)
    weights["down"] = joined(w_down, down_other, 1)
    for index, one in enumerate(streams):
        for name in ("flat", "upstream_low", "input_low", "retrieved_full", "labels", "reading"):
            array = getattr(whole, name)
            size = array.shape[0] // STREAMS
            setattr(one, name, array[index * size : (index + 1) * size])
        attend(one)
    first_stream, last_stream = streams[0], streams[-1]
    (gate_other,) = fetched(last_stream, ["branch"], first_stream.attended, w_gate_up[0])
    weights["gate"] = joined(w_gate_up[0], gate_other, 0)
    every(middle)
    (up_other,) = fetched(first_stream, ["mid_low"], first_stream.hidden, w_gate_up[1])
    weights["up"] = joined(w_gate_up[1], up_other, 0)
    first_stream.mid_low = after(first_stream.mid_low, last_stream.hidden)
    every(feed)
    first_stream.grad_mid = after(first_stream.grad_mid, last_stream.mid_low)
    feed_reductions = [
        Reduction(over(lambda one: over_rows(one.activ, one.upstream_low)), False),
        Reduction(
            jnp.stack(
                [
                    over(lambda one: over_rows(one.mid_low, one.grad_gate)).astype(NARROW),
                    over(lambda one: over_rows(one.mid_low, one.grad_upper)).astype(NARROW),
                ]
            ),
            True,
        ),
    ]
    every(middle_back)
    first_stream.grad_mixed = after(first_stream.grad_mixed, last_stream.grad_mid)
    for item in feed_reductions:
        item.across()
    attend_back(first_stream)
    tied(last_stream, ["grad_mixed"], *feed_reductions, Holder(first_stream.partial))
    attend_back(last_stream)
    for name in (
        "grad_retrieved",
        "grad_queries",
        "key_token",
        "value_token",
        "key_memory",
        "value_memory",
    ):
        merged(name)
    persist_wide = persist.astype(WIDE)
    key_fixed = over(lambda one: one.key_fixed)
    value_fixed = over(lambda one: one.value_fixed)
    grad_query_w = over_rows(whole.input_low, whole.grad_queries)
    grad_key_w = (
        over_rows(whole.input_low, whole.key_token)
        + over_rows(whole.retrieved_full, whole.key_memory)
        + exact_product(persist_wide.T, key_fixed)
    )
    grad_value_proj = (
        over_rows(whole.input_low, whole.value_token)
        + over_rows(whole.retrieved_full, whole.value_memory)
        + exact_product(persist_wide.T, value_fixed)
    )
    mix_reductions = [
        Reduction(over(lambda one: over_rows(one.attended, one.grad_mixed)), False),
        Reduction(
            jnp.stack(
                [item.astype(NARROW) for item in (grad_query_w, grad_key_w, grad_value_proj)]
            ),
            True,
        ),
    ]
    grad_persist = exact_product(key_fixed, key_w.astype(WIDE).T) + exact_product(
        value_fixed, value_w.astype(WIDE).T
    )
    for item in feed_reductions:
        item.apart()
    tied(whole, ["grad_retrieved"], *feed_reductions, *mix_reductions)
    every(branch_out)
    heads_back(whole)
    remember_back(whole)
    input_early(whole)
    grad_persist = after(grad_persist, whole.grad_mixing)
    grad_persist = lax.psum_scatter(grad_persist, "tp", scatter_dimension=0, tiled=True)
    target_reduction = Reduction(over_rows(whole.input_low, whole.grad_targets), True)
    for item in feed_reductions:
        item.together()
    for item in mix_reductions:
        item.across()
    tied(
        whole,
        ["grad_mixing", "scale_sum", "early"],
        *feed_reductions,
        *mix_reductions,
        target_reduction,
    )
    every(finish_output)
    features_back(whole)
    inputs_back(whole)
    outputs = [one.output for one in streams]
    whole.grad_input, outputs = lax.optimization_barrier((whole.grad_input, outputs))
    for index, one in enumerate(streams):
        one.grad_input = scattered(whole.grad_input[index * part_rows : (index + 1) * part_rows])

    grad_decays = whole.grad_decays
    grad_retain = 0.0
    grad_moment = 0.0
    retain_slope = jnp.zeros_like(retain)
    for lag in range(1, LAGS):
        retain_slope = retain * retain_slope + decays[lag - 1]
        moment_slope = 0.0
        for power in range(1, lag + 1):
            moment_slope = moment_slope + power * retain ** (lag - power) * moment ** (power - 1)
        grad_retain = grad_retain + retain_slope * grad_decays[lag]
        grad_moment = grad_moment + moment_slope * grad_decays[lag]
    grad_rates = jnp.stack([grad_retain, grad_moment])

    def summed(pieces):
        small = jnp.concatenate([piece.reshape(-1) for piece in pieces])
        for axis, bit in (("ctx", 1), ("shard", 1), ("ctx", 2)):
            small = small + flipped(small, axis, bit)
        return small

    small = summed(
        [
            grad_persist,
            over(lambda one: one.grad_gain_ffn),
            whole.grad_gain_memory,
            grad_rates,
        ]
    )
    cut = grad_persist.size + width
    spread = Holder(lax.all_gather(small[:cut], "tp", axis=0))
    feature_reduction = Reduction(over_rows(whole.input_low, whole.grad_pre), True)
    late_reductions = [feature_reduction, target_reduction]
    for item in mix_reductions:
        item.apart()
    for item in late_reductions:
        item.across()
    tied(last_stream, ["grad_input"], spread, *mix_reductions, *late_reductions)
    every(tokens_back)
    for item in mix_reductions:
        item.together()
    for item in late_reductions:
        item.apart()
        item.together()
    gain_in_sum = summed_over_ranks(summed([over(lambda one: one.grad_gain_in)]))
    grad_persist = spread.array[:, : grad_persist.size].reshape(persist_count, width)
    gain_ffn_sum = jnp.sum(spread.array[:, cut - width :], axis=0)
    middle_cut = cut + local_heads * HD
    grad_gain_memory = small[cut:middle_cut].reshape(local_heads, HD)
    grad_rates = small[middle_cut:].reshape(2, local_units)
    grad_down, grad_gate_up = [item.result() for item in feed_reductions]
    grad_out_rows, grad_qkv = [item.result() for item in mix_reductions]
    grad_feature_w, grad_target_w = [item.result() for item in late_reductions]

    def own_half(array, axis):
        size = array.shape[axis] // 2
        return lax.dynamic_slice_in_dim(array, half_index * size, size, axis)

    return (
        jnp.concatenate(outputs, axis=0).reshape(tokens.shape),
        jnp.concatenate([one.grad_tokens for one in streams], axis=0),
        own_half(gain_in_sum, 0),
        own_half(gain_ffn_sum, 0),
        own_half(grad_gain_memory, 1),
        own_half(grad_rates, 0),
        own_half(grad_persist, 1),
        grad_qkv,
        grad_out_rows,
        grad_target_w,
        grad_feature_w,
        grad_gate_up,
        grad_down,
    )


def solution(mesh):
    placed = (
        P("shard", "ctx", None),
        P("shard", "ctx"),
        P("shard"),
        P("shard"),
        P("tp", "shard"),
        P("shard", None),
        P(None, "shard"),
        P(None, "shard", "tp"),
        P("tp", "shard"),
        P("shard", "tp"),
        P("shard", "tp"),
        P(None, "shard", "tp"),
        P("tp", "shard"),
        P("shard", "ctx", None),
    )
    return jax.shard_map(
        on_device,
        mesh=mesh,
        in_specs=placed,
        out_specs=(
            P("shard", "ctx", None),
            P("shard", "ctx", None),
            P("shard"),
            P("shard"),
            P("tp", "shard"),
            P("shard", "tp"),
            P(None, "shard"),
            P(None, "shard", "tp"),
            P("tp", "shard"),
            P("shard", "tp"),
            P("shard", "tp"),
            P(None, "shard", "tp"),
            P("tp", "shard"),
        ),
        check_vma=False,
    )
```

```python
import jax
import jax.numpy as jnp
from jax import lax
from jax.experimental import pallas as pl
from jax.experimental.pallas import tpu as pltpu
from jax.sharding import PartitionSpec as P

HD = 96
SPAN = 256
LANES = 128
LIMIT = 800
LAGS = (LIMIT + SPAN - 2) // SPAN
CORNER = LIMIT - (LAGS - 1) * SPAN
STREAMS = 2


EPSILON = 1e-06
MASKED = -1e30
WIDE = jnp.float32
NARROW = jnp.bfloat16


def passed_along(value, axis, pairs):
    return lax.ppermute(value, axis, pairs)


def flipped(value, axis, bit):
    return lax.ppermute(value, axis, [(i, i ^ bit) for i in range(lax.axis_size(axis))])


def either(first, one, other):
    return jnp.where(first, one, other), jnp.where(first, other, one)


def pick(array, place, axis):
    return lax.dynamic_index_in_dim(array, place, axis, keepdims=False)


def after(value, *others):
    return lax.optimization_barrier((value, *others))[0]


def norm_rows(values, gain):
    factor = lax.rsqrt(jnp.mean(values * values, axis=-1, keepdims=True) + EPSILON)
    normed = values * factor
    return (normed * gain, normed, factor)


def norm_back(upstream, normed, factor, gain):
    inner = upstream * gain
    return factor * (inner - normed * jnp.mean(inner * normed, axis=-1, keepdims=True))


def silu_slope(values):
    sigmoid = jax.nn.sigmoid(values)
    return sigmoid * (1.0 + values * (1.0 - sigmoid))


def matmul(left, right):
    return jnp.dot(left, right, preferred_element_type=WIDE)


def over_rows(left, right):
    return lax.dot_general(left, right, (((0,), (0,)), ((), ())), preferred_element_type=WIDE)


def by_rows(left, right):
    return lax.dot_general(left, right, (((1,), (1,)), ((), ())), preferred_element_type=WIDE)


def exact_product(left, right):
    return jnp.dot(left, right, precision=lax.Precision.HIGHEST, preferred_element_type=WIDE)


def batched(spec, left, right):
    return jnp.einsum(spec, left, right, preferred_element_type=WIDE)


def windows(width):
    found = []
    for start in range(0, width, HD):
        low = start // LANES * LANES
        high = min(-(-(start + HD) // LANES) * LANES, width)
        found.append((low, high, start - low))
    return found


def masks_of(label_col, label_row, read_row):
    rows = lax.broadcasted_iota(jnp.int32, (SPAN, SPAN), 0)
    columns = lax.broadcasted_iota(jnp.int32, (SPAN, SPAN), 1)
    own = (rows >= columns) & (label_col == label_row)
    return own & (read_row > 0.5), own


def head_probs(query, keys, visible_memory, visible_own):
    scale = HD ** (-0.5)
    scores = [by_rows(query, key) * scale for key in keys]
    scores[1] = jnp.where(visible_memory, scores[1], MASKED)
    scores[2] = jnp.where(visible_own, scores[2], MASKED)
    highest = jnp.max(scores[0], axis=-1, keepdims=True)
    for item in scores[1:]:
        highest = jnp.maximum(highest, jnp.max(item, axis=-1, keepdims=True))
    raised = [jnp.exp(item - highest) for item in scores]
    totals = sum(jnp.sum(item, axis=-1, keepdims=True) for item in raised)
    inverse = 1.0 / totals
    return [item * inverse for item in raised]


def attention_kernel(
    query, key_memory, key_own, value_memory, value_own, key_fixed, value_fixed,
    label_col, label_row, read_row, out, total,
):
    visible_memory, visible_own = masks_of(label_col[0], label_row[0], read_row[0])
    total[...] = jnp.zeros_like(total)
    for low, high, offset in windows(query.shape[1]):
        lanes = lax.broadcasted_iota(jnp.int32, (SPAN, high - low), 1)
        inside = (lanes >= offset) & (lanes < offset + HD)
        mine = jnp.where(inside, query[:, low:high], jnp.zeros((), NARROW))
        keys = [item[:, low:high] for item in (key_fixed, key_memory, key_own)]
        values = [item[:, low:high] for item in (value_fixed, value_memory, value_own)]
        probs = head_probs(mine, keys, visible_memory, visible_own)
        result = sum(matmul(item.astype(NARROW), value) for item, value in zip(probs, values))
        total[:, low:high] += jnp.where(inside, result, 0.0)
    out[...] = total[...].astype(NARROW)


def attention_back_kernel(
    query, key_memory, key_own, value_memory, value_own, key_fixed, value_fixed,
    label_col, label_row, read_row, upstream,
    grad_query, grad_key_memory, grad_key_own, grad_value_memory, grad_value_own,
    grad_key_fixed, grad_value_fixed, *totals,
):
    scale = HD ** (-0.5)
    visible_memory, visible_own = masks_of(label_col[0], label_row[0], read_row[0])
    for total in totals:
        total[...] = jnp.zeros_like(total)

    @pl.when(pl.program_id(0) == 0)
    def _():
        grad_key_fixed[...] = jnp.zeros_like(grad_key_fixed)
        grad_value_fixed[...] = jnp.zeros_like(grad_value_fixed)

    key_sums = (grad_key_fixed, totals[1], totals[2])
    value_sums = (grad_value_fixed, totals[3], totals[4])
    for low, high, offset in windows(query.shape[1]):
        lanes = lax.broadcasted_iota(jnp.int32, (SPAN, high - low), 1)
        inside = (lanes >= offset) & (lanes < offset + HD)
        mine = jnp.where(inside, query[:, low:high], jnp.zeros((), NARROW))
        above = jnp.where(inside, upstream[:, low:high], jnp.zeros((), NARROW))
        keys = [item[:, low:high] for item in (key_fixed, key_memory, key_own)]
        values = [item[:, low:high] for item in (value_fixed, value_memory, value_own)]
        probs = head_probs(mine, keys, visible_memory, visible_own)
        grads = [by_rows(above, value) for value in values]
        inner = sum(
            jnp.sum(grad * item, axis=-1, keepdims=True) for grad, item in zip(grads, probs)
        )
        result = 0.0
        for index in range(3):
            slope = (probs[index] * (grads[index] - inner)).astype(NARROW)
            result = result + matmul(slope, keys[index])
            key_sums[index][:, low:high] += over_rows(slope, mine) * scale
            value_sums[index][:, low:high] += over_rows(probs[index].astype(NARROW), above)
        totals[0][:, low:high] += jnp.where(inside, result, 0.0) * scale
    places = (grad_query, grad_key_memory, grad_key_own, grad_value_memory, grad_value_own)
    for place, total in zip(places, totals):
        place[...] = total[...].astype(NARROW)


def attention_specs(blocks, width, fixed_count):
    rows = pl.BlockSpec((SPAN, width), lambda block: (block, 0))
    fixed = pl.BlockSpec((fixed_count, width), lambda block: (0, 0))
    col = pl.BlockSpec((1, SPAN, 1), lambda block: (block, 0, 0))
    row = pl.BlockSpec((1, 1, SPAN), lambda block: (block, 0, 0))
    return rows, fixed, [rows] * 5 + [fixed] * 2 + [col, row, row]


def attention(*operands):
    blocks, width, fixed_count = (operands[7].shape[0], operands[0].shape[1], operands[5].shape[0])
    rows, _, specs = attention_specs(blocks, width, fixed_count)
    pairs = blocks * SPAN * (2 * SPAN + fixed_count)
    return pl.pallas_call(
        attention_kernel,
        grid=(blocks,),
        in_specs=specs,
        out_specs=rows,
        out_shape=jax.ShapeDtypeStruct((blocks * SPAN, width), NARROW),
        scratch_shapes=[pltpu.VMEM((SPAN, width), WIDE)],
        cost_estimate=pl.CostEstimate(
            flops=16 * pairs * width,
            bytes_accessed=12 * blocks * SPAN * width,
            transcendentals=pairs * width // HD,
        ),
    )(*operands)


def attention_back(*operands):
    blocks, width, fixed_count = (operands[7].shape[0], operands[0].shape[1], operands[5].shape[0])
    rows, fixed, specs = attention_specs(blocks, width, fixed_count)
    pairs = blocks * SPAN * (2 * SPAN + fixed_count)
    return pl.pallas_call(
        attention_back_kernel,
        grid=(blocks,),
        in_specs=specs + [rows],
        out_specs=[rows] * 5 + [fixed] * 2,
        out_shape=[jax.ShapeDtypeStruct((blocks * SPAN, width), NARROW)] * 5
        + [jax.ShapeDtypeStruct((fixed_count, width), WIDE)] * 2,
        scratch_shapes=[pltpu.VMEM((SPAN, width), WIDE)] * 5,
        cost_estimate=pl.CostEstimate(
            flops=40 * pairs * width,
            bytes_accessed=24 * blocks * SPAN * width,
            transcendentals=pairs * width // HD,
        ),
    )(*operands)


def on_device(
    tokens,
    segments,
    norm_gain,
    ffn_gain,
    memory_gain,
    memory_rates,
    persistent,
    w_qkv,
    w_out,
    w_value,
    w_feature,
    w_gate_up,
    w_down,
    out_grad,
):
    parts, ranks = (lax.axis_size("ctx"), lax.axis_size("tp"))
    part, rank = (lax.axis_index("ctx"), lax.axis_index("tp"))
    half_index = lax.axis_index("shard")
    first_half = half_index == 0
    odd_part = part % 2 == 1
    groups, local_len, width = tokens.shape
    blocks_each = local_len // SPAN
    reach = -(-LAGS // blocks_each)
    step = 6.0 / (SPAN + 8)
    scale = HD ** (-0.5)

    def joined(own, other, axis):
        return jnp.concatenate(either(first_half, own, other), axis=axis)

    pair_tokens = flipped(tokens, "ctx", 1)
    far_tokens = flipped(tokens, "ctx", 2)
    core, outer = (part % 2, part // 2)
    feature_half = pick(w_feature.reshape(2, -1, w_feature.shape[1]), core, 0)
    feature_half = flipped(feature_half, "shard", 1)
    feature_other = jnp.concatenate(
        either(core == 0, feature_half, flipped(feature_half, "ctx", 1)), axis=0
    )
    smalls = [norm_gain, ffn_gain, memory_gain, memory_rates, persistent]
    small_flat = jnp.concatenate([item.reshape(-1) for item in smalls])
    small_other = flipped(small_flat, "shard", 1)
    small_others = []
    start = 0
    for item in smalls:
        small_others.append(small_other[start : start + item.size].reshape(item.shape))
        start += item.size
    value_other = flipped(after(w_value, feature_half), "shard", 1)

    gain_in_wide = joined(norm_gain, small_others[0], 0).astype(WIDE)
    gain_ffn_wide = joined(ffn_gain, small_others[1], 0).astype(WIDE)
    gain_mem = joined(memory_gain, small_others[2], 1).astype(WIDE)
    rates = joined(memory_rates, small_others[3], 0)
    persist = joined(persistent, small_others[4], 1)
    feature_cols = joined(w_feature, feature_other, 0)
    value_cols = joined(w_value, value_other, 0)
    weights = {}
    local_width = w_qkv.shape[2]
    local_units = feature_cols.shape[1]
    local_heads = local_width // HD
    persist_count = persist.shape[0]

    def scattered(array):
        return lax.psum_scatter(
            array.astype(NARROW), "tp", scatter_dimension=0, tiled=True
        ).astype(WIDE)

    def collected(array):
        return lax.all_gather(array.astype(NARROW), "tp", axis=0, tiled=True)

    def summed_over_ranks(array):
        bit = 1
        while bit < ranks:
            array = array + flipped(array, "tp", bit)
            bit *= 2
        return array

    own_units = lax.dynamic_slice_in_dim(rates.astype(WIDE), rank * local_units, local_units, 1)
    retain, moment = (own_units[0], own_units[1])
    decays = [jnp.ones_like(retain)]
    for lag in range(1, LAGS):
        decays.append(retain * decays[-1] + moment**lag)

    labels_all = segments.astype(WIDE).reshape(groups, blocks_each, SPAN) + 1.0
    lasts_all = labels_all[:, :, -1]
    late_lasts = after(lasts_all, far_tokens)
    far_lasts = flipped(late_lasts, "ctx", 2)
    lasts_around = jnp.stack(
        [lasts_all, flipped(late_lasts, "ctx", 1), far_lasts, flipped(far_lasts, "ctx", 1)]
    )

    def last_of(index):
        delta, place = divmod(index, blocks_each)
        source = part + delta
        found = pick(lasts_around, jnp.clip(source, 0, parts - 1) ^ part, 0)[:, place]
        return jnp.where(source >= 0, found, 0.0)

    before_all = jnp.stack([last_of(own - 1) for own in range(blocks_each)], axis=1)
    linked_all = []
    for own in range(blocks_each):
        for lag in range(LAGS):
            source = own - 1 - lag
            present = part + source // blocks_each >= 0
            linked_all.append(present & (last_of(source) == last_of(own - 1)))
    linked_all = jnp.stack(linked_all, axis=1).reshape(groups, blocks_each, LAGS)

    def place_of(own, lag):
        return divmod(own - 1 - lag, blocks_each)

    head_of = (jnp.arange(local_width)[:, None] // HD == jnp.arange(local_heads)).astype(WIDE)
    gain_flat = gain_mem.reshape(local_width)

    def head_mean(values):
        return exact_product(values, head_of) / HD

    def head_spread(values):
        return exact_product(values, head_of.T)

    count = groups
    rows = count * local_len
    blocks = count * blocks_each
    part_rows = rows // STREAMS
    part_blocks = blocks // STREAMS

    def own_rows(array):
        sub = array.shape[0] // ranks
        return lax.dynamic_slice_in_dim(array, rank * sub, sub, 0)

    class Stream:
        pass

    def linked(one, square, corner):
        spread = jnp.repeat(one.linked[:, :, LAGS - 2 :: -1], SPAN, axis=2)[:, :, None]
        square = jnp.where(spread, square, jnp.zeros_like(square))
        corner = jnp.where(
            one.linked[:, :, LAGS - 1, None, None], corner, jnp.zeros_like(corner)
        )
        return square, corner

    def packed(square, corner):
        wide = square.shape[-1]
        lanes = corner.transpose(2, 0, 1, 3).reshape(CORNER, -1)
        lanes = jnp.pad(lanes, ((0, 0), (0, wide - lanes.shape[1])))
        return jnp.concatenate([square.reshape(-1, wide), lanes], axis=0)

    def unpacked(array):
        square = array[:-CORNER].reshape(count, blocks_each, SPAN, -1)
        corner = array[-CORNER:, : blocks * CORNER]
        corner = corner.reshape(CORNER, count, blocks_each, CORNER).transpose(1, 2, 0, 3)
        return square, corner

    def begin(one, index):
        def mine(array):
            return array[index * count : (index + 1) * count]

        one.flat = mine(tokens).reshape(rows, width)
        one.upstream_low = mine(out_grad).reshape(rows, width)
        one.labels = mine(labels_all)
        one.lasts = mine(lasts_all)
        one.before = mine(before_all)
        one.linked = mine(linked_all)
        one.keeping = (one.lasts == one.before).astype(WIDE)[:, :, None, None]
        one.writing = (one.labels == one.lasts[:, :, None]).astype(WIDE)[..., None]
        one.reading = (one.labels == one.before[:, :, None]).astype(WIDE)

        def features_of(piece):
            low = norm_rows(piece.astype(WIDE), gain_in_wide)[0].astype(NARROW)
            return low, matmul(low.reshape(rows, width), feature_cols)

        def shaped(values):
            return values.reshape(count, blocks_each, SPAN, local_units)

        low, one.preact = features_of(mine(tokens))
        one.input_low = low.reshape(rows, width)
        one.features = jax.nn.silu(one.preact).astype(NARROW)
        squares = jnp.sum(jnp.square(one.features.astype(WIDE)), axis=1)
        one.key_scale = lax.rsqrt(summed_over_ranks(squares) + EPSILON)
        far, pair, one.features, one.key_scale = lax.optimization_barrier(
            (mine(far_tokens), mine(pair_tokens), one.features, one.key_scale)
        )
        close = [pair, flipped(far, "ctx", 1)]
        one.around = {0: shaped(one.features)}
        for delta, piece in (
            (-1, jnp.where(odd_part, close[0], close[1])),
            (1, jnp.where(odd_part, close[1], close[0])),
            (2, far),
        ):
            one.around[delta] = shaped(jax.nn.silu(features_of(piece)[1]).astype(NARROW))
        one.around[-2] = one.around[2]
        one.targets = matmul(one.input_low, value_cols).reshape(
            count, blocks_each, SPAN, local_width
        )
        weighted = [(one.around[0].astype(WIDE) * decay).astype(NARROW) for decay in decays]
        products = []
        corners = []
        for own in range(blocks_each):
            row = []
            for lag in range(LAGS - 1, -1, -1):
                delta, place = place_of(own, lag)
                near, past = weighted[lag][:, own], one.around[delta][:, place]
                if lag == LAGS - 1:
                    near, past = near[:, :CORNER], past[:, SPAN - CORNER :]
                    corners.append(batched("sth,suh->stu", near, past))
                else:
                    row.append(batched("sth,suh->stu", near, past))
            products.append(jnp.concatenate(row, axis=2))
        one.products = packed(
            jnp.stack(products, axis=1).astype(NARROW), jnp.stack(corners, axis=1).astype(NARROW)
        )
        one.mixing = lax.psum(one.products, "tp")

    def span_of(own):
        start = (reach * blocks_each - LAGS + own) * SPAN
        return slice(start, start + LAGS * SPAN)

    def remember(one):
        square, corner = linked(one, *unpacked(one.mixing))
        corner = jnp.pad(
            corner, ((0, 0), (0, 0), (0, SPAN - CORNER), (SPAN - CORNER, 0))
        )
        one.mixing = jnp.concatenate([corner, square], axis=3)
        one.scales = one.key_scale.reshape(count, blocks_each, SPAN, 1)
        halos = [
            jnp.zeros((count, blocks_each * SPAN, local_width), NARROW) for _ in range(reach)
        ]
        pending = {}
        for turn in range(parts):
            for hop in range(1, reach + 1):
                if (turn - hop, hop) in pending:
                    halos[reach - hop] = halos[reach - hop] + pending[(turn - hop, hop)]
            known = jnp.concatenate(halos, axis=1)
            recalls = []
            errors = []
            for own in range(blocks_each):
                total = batched("stu,sud->std", one.mixing[:, own], known[:, span_of(own)])
                recall = -step * one.scales[:, own] * total
                error = one.writing[:, own] * (
                    one.keeping[:, own] * recall - one.targets[:, own]
                )
                recalls.append(recall)
                errors.append(error)
                known = jnp.concatenate(
                    [known, (one.scales[:, own] * error).astype(NARROW)], axis=1
                )
            for hop in range(1, reach + 1):
                if turn + hop < parts:
                    pending[(turn, hop)] = passed_along(
                        known[:, reach * blocks_each * SPAN :], "ctx", [(turn, turn + hop)]
                    )
        one.known = known
        one.recall = jnp.stack(recalls, 1)
        one.errors = jnp.stack(errors, 1)
        masked = (one.reading[..., None] * one.recall).reshape(rows, local_width)
        one.head_factor = head_spread(lax.rsqrt(head_mean(masked * masked) + EPSILON))
        one.head_unit = masked * one.head_factor
        retrieved = (one.head_unit * gain_flat).astype(NARROW)
        one.retrieved_full = lax.all_gather(retrieved, "tp", axis=1, tiled=True)

    def attend(one):
        def projected(values, weight):
            return matmul(values, weight).astype(NARROW)

        labels = one.labels.reshape(part_blocks, SPAN)
        reading = one.reading.reshape(part_blocks, SPAN)
        one.operands = (
            projected(one.input_low, query_w),
            projected(one.retrieved_full, key_w),
            projected(one.input_low, key_w),
            projected(one.retrieved_full, value_w),
            projected(one.input_low, value_w),
            fixed_keys,
            fixed_values,
            labels[:, :, None],
            labels[:, None, :],
            reading[:, None, :],
        )
        one.attended = attention(*one.operands)
        one.residual = own_rows(one.flat).astype(WIDE)
        one.branch = scattered(matmul(one.attended, weights["out"]))

    def middle(one):
        if one is not streams[0]:
            one.branch = after(one.branch, streams[0].mid_own)
        one.hidden = one.residual + one.branch
        normed_mid, one.unit_mid, one.factor_mid = norm_rows(one.hidden, gain_ffn_wide)
        one.mid_own = normed_mid.astype(NARROW)
        one.mid_low = collected(one.mid_own)

    def feed(one):
        gate = matmul(one.mid_low, weights["gate"])
        upper = matmul(one.mid_low, weights["up"])
        one.activ = (jax.nn.silu(gate) * upper).astype(NARROW)
        grad_act = by_rows(one.upstream_low, weights["down"])
        one.grad_gate = (grad_act * upper * silu_slope(gate)).astype(NARROW)
        one.grad_upper = (grad_act * jax.nn.silu(gate)).astype(NARROW)
        one.grad_mid = scattered(
            by_rows(one.grad_gate, weights["gate"]) + by_rows(one.grad_upper, weights["up"])
        )

    def middle_back(one):
        if one is not streams[0]:
            one.grad_mid = after(one.grad_mid, streams[0].grad_hidden)
        grad_mid = one.grad_mid
        one.grad_gain_ffn = jnp.sum(grad_mid * one.unit_mid, axis=0)
        upstream = own_rows(one.upstream_low).astype(WIDE)
        one.grad_hidden = upstream + norm_back(
            grad_mid, one.unit_mid, one.factor_mid, gain_ffn_wide
        )
        one.grad_mixed = collected(one.grad_hidden)

    def branch_out(one):
        activ = after(one.activ, whole.grad_retrieved)
        one.branch = scattered(matmul(activ, weights["down"]))

    def finish_output(one):
        one.output = collected(after(one.hidden + one.branch, whole.grad_mixing))

    def attend_back(one):
        grad_attended = by_rows(one.grad_mixed, weights["out"]).astype(NARROW)
        (
            one.grad_queries,
            one.key_memory,
            one.key_token,
            one.value_memory,
            one.value_token,
            one.key_fixed,
            one.value_fixed,
        ) = attention_back(*one.operands, grad_attended)
        partial = by_rows(one.key_memory, key_w) + by_rows(one.value_memory, value_w)
        one.partial = partial.astype(NARROW)
        one.grad_retrieved = lax.psum_scatter(one.partial, "tp", scatter_dimension=1, tiled=True)

    def heads_back(one):
        grad_heads = one.grad_retrieved.astype(WIDE)
        one.grad_gain_memory = jnp.sum(grad_heads * one.head_unit, axis=0)
        inner = grad_heads * gain_flat
        grad_masked = one.head_factor * (
            inner - one.head_unit * head_spread(head_mean(inner * one.head_unit))
        )
        one.grad_read = one.reading[..., None] * grad_masked.reshape(
            count, blocks_each, SPAN, local_width
        )

    def remember_back(one):
        later = [0.0] * blocks_each
        pending = {}
        for turn in range(parts):
            for hop in range(1, reach + 1):
                if (turn - hop, hop) in pending:
                    arrived = pending[(turn - hop, hop)].astype(WIDE)
                    for own in range(blocks_each):
                        later[own] = later[own] + arrived[:, own * SPAN : (own + 1) * SPAN]
            known = [0.0] * (reach * blocks_each) + later
            grad_errors = [None] * blocks_each
            grad_recalls = [None] * blocks_each
            raws = [None] * blocks_each
            for own in range(blocks_each - 1, -1, -1):
                grad_scaled = -step * known[reach * blocks_each + own]
                grad_error = one.scales[:, own] * grad_scaled
                grad_recall = (
                    one.grad_read[:, own] + one.writing[:, own] * one.keeping[:, own] * grad_error
                )
                grad_errors[own] = jnp.broadcast_to(grad_error, grad_recall.shape)
                grad_recalls[own] = grad_recall
                raws[own] = (one.scales[:, own] * grad_recall).astype(NARROW)
                carried = batched("stu,std->sud", one.mixing[:, own], raws[own])
                for index in range(LAGS):
                    place = reach * blocks_each - LAGS + own + index
                    known[place] = (
                        known[place] + carried[:, index * SPAN : (index + 1) * SPAN]
                    )
            for hop in range(1, reach + 1):
                place = parts - 1 - turn
                if place - hop >= 0:
                    start = (reach - hop) * blocks_each
                    sent = jnp.concatenate(known[start : start + blocks_each], axis=1)
                    pending[(turn, hop)] = passed_along(
                        sent.astype(NARROW), "ctx", [(place, place - hop)]
                    )
        grad_errors = jnp.stack(grad_errors, 1)
        grad_recalls = jnp.stack(grad_recalls, 1)
        one.grad_targets = (-one.writing * grad_errors).astype(NARROW).reshape(rows, local_width)
        scale_part = jnp.sum(grad_recalls * one.recall + one.errors * grad_errors, axis=3)
        one.scale_sum = summed_over_ranks(scale_part.reshape(rows))
        grad_mixing = []
        for own in range(blocks_each):
            grad_mixing.append(
                -step * batched("std,sud->stu", raws[own], one.known[:, span_of(own)])
            )
        grad_mixing = jnp.stack(grad_mixing, 1)
        square, corner = linked(
            one, grad_mixing[..., SPAN:], grad_mixing[:, :, :CORNER, SPAN - CORNER : SPAN]
        )
        grad_mixing = packed(square.astype(NARROW), corner.astype(NARROW))
        branches = [item.branch for item in streams]
        grad_mixing, branches = lax.optimization_barrier((grad_mixing, branches))
        for item, branch in zip(streams, branches):
            item.branch = branch
        one.grad_mixing = lax.psum(grad_mixing, "tp")

    def features_back(one):
        square, corner = unpacked(one.grad_mixing)

        def column(own, lag):
            if lag == LAGS - 1:
                return corner[:, own]
            start = (LAGS - 2 - lag) * SPAN
            return square[:, own, :, start : start + SPAN]

        needed = {}
        for hop in range(1, reach + 1):
            sends = [(source, source - hop) for source in range(hop, parts)]
            for last_lag in (False, True):
                pairs = [
                    (own, lag)
                    for own in range(blocks_each)
                    for lag in range(LAGS)
                    if place_of(own, lag)[0] == -hop and (lag == LAGS - 1) == last_lag
                ]
                if not pairs:
                    continue
                moved = passed_along(
                    jnp.stack([column(own, lag) for own, lag in pairs], axis=1), "ctx", sends
                )
                for place, (own, lag) in enumerate(pairs):
                    needed[(hop * blocks_each + own, lag)] = moved[:, place]
        for own in range(blocks_each):
            for lag in range(LAGS):
                needed[(own, lag)] = column(own, lag)
        grad_features = []
        one.grad_decays = [0.0] * LAGS
        rest = SPAN - CORNER
        for own in range(blocks_each):
            total = 0.0
            for lag in range(LAGS):
                own_features = one.around[0][:, own].astype(WIDE)
                delta, place = place_of(own, lag)
                past = one.around[delta][:, place]
                later = own + 1 + lag
                delta, place = divmod(later, blocks_each)
                future = one.around[delta][:, place]
                if lag == LAGS - 1:
                    own_features, past, future = (
                        own_features[:, :CORNER],
                        past[:, rest:],
                        future[:, :CORNER],
                    )
                from_reads = batched("stu,suh->sth", needed[(own, lag)], past)
                one.grad_decays[lag] = one.grad_decays[lag] + jnp.sum(
                    own_features * from_reads, axis=(0, 1)
                )
                from_writes = batched("stu,sth->suh", needed[(later, lag)], future)
                if lag == LAGS - 1:
                    from_reads = jnp.pad(from_reads, ((0, 0), (0, rest), (0, 0)))
                    from_writes = jnp.pad(from_writes, ((0, 0), (rest, 0), (0, 0)))
                total = total + decays[lag] * (from_reads + from_writes)
            grad_features.append(total)
        grad_features = jnp.stack(grad_features, 1).reshape(rows, local_units)
        grad_features = grad_features - (one.key_scale * one.key_scale * one.scale_sum)[
            :, None
        ] * one.features.astype(WIDE)
        one.grad_pre = (grad_features * silu_slope(one.preact)).astype(NARROW)

    def inputs_back(one):
        one.grad_input = (one.early + by_rows(one.grad_pre, feature_cols)).astype(NARROW)

    def input_early(one):
        one.early = (
            by_rows(one.grad_queries, query_w)
            + by_rows(one.key_token, key_w)
            + by_rows(one.value_token, value_w)
            + by_rows(one.grad_targets, value_cols)
        )

    def tokens_back(one):
        if one is not streams[0]:
            one.grad_input = after(one.grad_input, streams[0].grad_own)
        grad_input = one.grad_input
        _, unit_in, factor_in = norm_rows(one.residual, gain_in_wide)
        one.grad_gain_in = jnp.sum(grad_input * unit_in, axis=0)
        grad_own = one.grad_hidden + norm_back(grad_input, unit_in, factor_in, gain_in_wide)
        one.grad_own = grad_own.astype(NARROW)
        one.grad_tokens = collected(one.grad_own).astype(WIDE).reshape(-1, local_len, width)

    whole = Stream()
    streams = [Stream() for _ in range(STREAMS)]

    def over(function):
        total = function(streams[0])
        for one in streams[1:]:
            total = total + function(one)
        return total

    def every(stage):
        for one in streams:
            stage(one)

    class Reduction:
        def __init__(self, array, by_row):
            array = array.astype(NARROW)
            *self.lead, self.high, self.wide = array.shape
            self.by_row = by_row
            self.axis = len(self.lead)
            if by_row:
                array = array.reshape(*self.lead, 2, 2, 2, self.high // 8, self.wide)
            else:
                array = array.reshape(2, 2, self.high // 4, self.wide)
            self.array = array
            self.exchange(core, self.axis + 1 if by_row else 0, "ctx", 1)

        def exchange(self, index, axis, over_axis, bit):
            own, other = (pick(self.array, place, axis) for place in (index, 1 - index))
            self.add(own, flipped(other, over_axis, bit))

        def add(self, own, arrived):
            self.array = (own.astype(WIDE) + arrived.astype(WIDE)).astype(NARROW)

        def across(self):
            if self.by_row:
                self.exchange(half_index, self.axis, "shard", 1)
                return
            half = self.wide // 2
            own, other = (
                lax.dynamic_slice_in_dim(self.array, place * half, half, 2)
                for place in (half_index, 1 - half_index)
            )
            self.add(own, flipped(other, "shard", 1))

        def apart(self):
            self.exchange(outer, self.axis if self.by_row else 0, "ctx", 2)

        def together(self):
            pair = either(outer == 0, self.array, flipped(self.array, "ctx", 2))
            self.array = jnp.stack(pair, axis=self.axis if self.by_row else 0)

        def result(self):
            pair = either(core == 0, self.array, flipped(self.array, "ctx", 1))
            array = jnp.stack(pair, axis=self.axis if self.by_row else 0).astype(WIDE)
            if self.by_row:
                return array.reshape(*self.lead, self.high // 2, self.wide)
            return array.reshape(self.high, self.wide // 2)

    def tied(one, names, *reductions):
        held = [getattr(one, name) for name in names]
        held, arrays = lax.optimization_barrier((held, [item.array for item in reductions]))
        for name, value in zip(names, held):
            setattr(one, name, value)
        for item, array in zip(reductions, arrays):
            item.array = array

    class Holder:
        def __init__(self, array):
            self.array = array

    def fetched(one, names, start, *arrays):
        holders = [Holder(flipped(after(item, start), "shard", 1)) for item in arrays]
        tied(one, names, *holders)
        return [holder.array for holder in holders]

    def merged(name):
        setattr(
            whole, name, jnp.concatenate([getattr(one, name) for one in streams], axis=0)
        )

    begin(whole, 0)
    (qkv_other,) = fetched(whole, ["mixing"], whole.products, w_qkv)
    qkv_cols = joined(w_qkv, qkv_other, 1)
    query_w = qkv_cols[0]
    key_w = qkv_cols[1]
    value_w = qkv_cols[2]
    fixed_keys = matmul(persist, key_w).astype(NARROW)
    fixed_values = matmul(persist, value_w).astype(NARROW)
    remember(whole)
    out_other, down_other = fetched(whole, ["retrieved_full"], whole.recall, w_out, w_down)
    weights["out"] = joined(w_out, out_other, 1)
    weights["down"] = joined(w_down, down_other, 1)
    for index, one in enumerate(streams):
        for name in ("flat", "upstream_low", "input_low", "retrieved_full", "labels", "reading"):
            array = getattr(whole, name)
            size = array.shape[0] // STREAMS
            setattr(one, name, array[index * size : (index + 1) * size])
        attend(one)
    first_stream, last_stream = streams[0], streams[-1]
    (gate_other,) = fetched(last_stream, ["branch"], first_stream.attended, w_gate_up[0])
    weights["gate"] = joined(w_gate_up[0], gate_other, 0)
    every(middle)
    (up_other,) = fetched(first_stream, ["mid_low"], first_stream.hidden, w_gate_up[1])
    weights["up"] = joined(w_gate_up[1], up_other, 0)
    first_stream.mid_low = after(first_stream.mid_low, last_stream.hidden)
    every(feed)
    first_stream.grad_mid = after(first_stream.grad_mid, last_stream.mid_low)
    feed_reductions = [
        Reduction(over(lambda one: over_rows(one.activ, one.upstream_low)), False),
        Reduction(
            jnp.stack(
                [
                    over(lambda one: over_rows(one.mid_low, one.grad_gate)).astype(NARROW),
                    over(lambda one: over_rows(one.mid_low, one.grad_upper)).astype(NARROW),
                ]
            ),
            True,
        ),
    ]
    every(middle_back)
    first_stream.grad_mixed = after(first_stream.grad_mixed, last_stream.grad_mid)
    for item in feed_reductions:
        item.across()
    attend_back(first_stream)
    tied(last_stream, ["grad_mixed"], *feed_reductions, Holder(first_stream.partial))
    attend_back(last_stream)
    for name in (
        "grad_retrieved",
        "grad_queries",
        "key_token",
        "value_token",
        "key_memory",
        "value_memory",
    ):
        merged(name)
    persist_wide = persist.astype(WIDE)
    key_fixed = over(lambda one: one.key_fixed)
    value_fixed = over(lambda one: one.value_fixed)
    grad_query_w = over_rows(whole.input_low, whole.grad_queries)
    grad_key_w = (
        over_rows(whole.input_low, whole.key_token)
        + over_rows(whole.retrieved_full, whole.key_memory)
        + exact_product(persist_wide.T, key_fixed)
    )
    grad_value_proj = (
        over_rows(whole.input_low, whole.value_token)
        + over_rows(whole.retrieved_full, whole.value_memory)
        + exact_product(persist_wide.T, value_fixed)
    )
    mix_reductions = [
        Reduction(over(lambda one: over_rows(one.attended, one.grad_mixed)), False),
        Reduction(
            jnp.stack(
                [item.astype(NARROW) for item in (grad_query_w, grad_key_w, grad_value_proj)]
            ),
            True,
        ),
    ]
    grad_persist = exact_product(key_fixed, key_w.astype(WIDE).T) + exact_product(
        value_fixed, value_w.astype(WIDE).T
    )
    for item in feed_reductions:
        item.apart()
    tied(whole, ["grad_retrieved"], *feed_reductions, *mix_reductions)
    every(branch_out)
    heads_back(whole)
    remember_back(whole)
    input_early(whole)
    grad_persist = after(grad_persist, whole.grad_mixing)
    grad_persist = lax.psum_scatter(grad_persist, "tp", scatter_dimension=0, tiled=True)
    target_reduction = Reduction(over_rows(whole.input_low, whole.grad_targets), True)
    for item in feed_reductions:
        item.together()
    for item in mix_reductions:
        item.across()
    tied(
        whole,
        ["grad_mixing", "scale_sum", "early"],
        *feed_reductions,
        *mix_reductions,
        target_reduction,
    )
    every(finish_output)
    features_back(whole)
    inputs_back(whole)
    outputs = [one.output for one in streams]
    whole.grad_input, outputs = lax.optimization_barrier((whole.grad_input, outputs))
    for index, one in enumerate(streams):
        one.grad_input = scattered(whole.grad_input[index * part_rows : (index + 1) * part_rows])

    grad_decays = whole.grad_decays
    grad_retain = 0.0
    grad_moment = 0.0
    retain_slope = jnp.zeros_like(retain)
    for lag in range(1, LAGS):
        retain_slope = retain * retain_slope + decays[lag - 1]
        moment_slope = 0.0
        for power in range(1, lag + 1):
            moment_slope = moment_slope + power * retain ** (lag - power) * moment ** (power - 1)
        grad_retain = grad_retain + retain_slope * grad_decays[lag]
        grad_moment = grad_moment + moment_slope * grad_decays[lag]
    grad_rates = jnp.stack([grad_retain, grad_moment])

    def summed(pieces):
        small = jnp.concatenate([piece.reshape(-1) for piece in pieces])
        for axis, bit in (("ctx", 1), ("shard", 1), ("ctx", 2)):
            small = small + flipped(small, axis, bit)
        return small

    small = summed(
        [
            grad_persist,
            over(lambda one: one.grad_gain_ffn),
            whole.grad_gain_memory,
            grad_rates,
        ]
    )
    cut = grad_persist.size + width
    spread = Holder(lax.all_gather(small[:cut], "tp", axis=0))
    feature_reduction = Reduction(over_rows(whole.input_low, whole.grad_pre), True)
    late_reductions = [feature_reduction, target_reduction]
    for item in mix_reductions:
        item.apart()
    for item in late_reductions:
        item.across()
    tied(last_stream, ["grad_input"], spread, *mix_reductions, *late_reductions)
    every(tokens_back)
    for item in mix_reductions:
        item.together()
    for item in late_reductions:
        item.apart()
        item.together()
    gain_in_sum = summed_over_ranks(summed([over(lambda one: one.grad_gain_in)]))
    grad_persist = spread.array[:, : grad_persist.size].reshape(persist_count, width)
    gain_ffn_sum = jnp.sum(spread.array[:, cut - width :], axis=0)
    middle_cut = cut + local_heads * HD
    grad_gain_memory = small[cut:middle_cut].reshape(local_heads, HD)
    grad_rates = small[middle_cut:].reshape(2, local_units)
    grad_down, grad_gate_up = [item.result() for item in feed_reductions]
    grad_out_rows, grad_qkv = [item.result() for item in mix_reductions]
    grad_feature_w, grad_target_w = [item.result() for item in late_reductions]

    def own_half(array, axis):
        size = array.shape[axis] // 2
        return lax.dynamic_slice_in_dim(array, half_index * size, size, axis)

    return (
        jnp.concatenate(outputs, axis=0).reshape(tokens.shape),
        jnp.concatenate([one.grad_tokens for one in streams], axis=0),
        own_half(gain_in_sum, 0),
        own_half(gain_ffn_sum, 0),
        own_half(grad_gain_memory, 1),
        own_half(grad_rates, 0),
        own_half(grad_persist, 1),
        grad_qkv,
        grad_out_rows,
        grad_target_w,
        grad_feature_w,
        grad_gate_up,
        grad_down,
    )


def solution(mesh):
    placed = (
        P("shard", "ctx", None),
        P("shard", "ctx"),
        P("shard"),
        P("shard"),
        P("tp", "shard"),
        P("shard", None),
        P(None, "shard"),
        P(None, "shard", "tp"),
        P("tp", "shard"),
        P("shard", "tp"),
        P("shard", "tp"),
        P(None, "shard", "tp"),
        P("tp", "shard"),
        P("shard", "ctx", None),
    )
    return jax.shard_map(
        on_device,
        mesh=mesh,
        in_specs=placed,
        out_specs=(
            P("shard", "ctx", None),
            P("shard", "ctx", None),
            P("shard"),
            P("shard"),
            P("tp", "shard"),
            P("shard", "tp"),
            P(None, "shard"),
            P(None, "shard", "tp"),
            P("tp", "shard"),
            P("shard", "tp"),
            P("shard", "tp"),
            P(None, "shard", "tp"),
            P("tp", "shard"),
        ),
        check_vma=False,
    )
```

```python
import jax
import jax.numpy as jnp
from jax import lax
from jax.experimental import pallas as pl
from jax.experimental.pallas import tpu as pltpu
from jax.sharding import PartitionSpec as P

HD = 96
SPAN = 256
LANES = 128
LIMIT = 800
LAGS = (LIMIT + SPAN - 2) // SPAN
CORNER = LIMIT - (LAGS - 1) * SPAN
STREAMS = 2


EPSILON = 1e-06
MASKED = -1e30
WIDE = jnp.float32
NARROW = jnp.bfloat16


def passed_along(value, axis, pairs):
    return lax.ppermute(value, axis, pairs)


def flipped(value, axis, bit):
    return lax.ppermute(value, axis, [(i, i ^ bit) for i in range(lax.axis_size(axis))])


def either(first, one, other):
    return jnp.where(first, one, other), jnp.where(first, other, one)


def pick(array, place, axis):
    return lax.dynamic_index_in_dim(array, place, axis, keepdims=False)


def after(value, *others):
    return lax.optimization_barrier((value, *others))[0]


def norm_rows(values, gain):
    factor = lax.rsqrt(jnp.mean(values * values, axis=-1, keepdims=True) + EPSILON)
    normed = values * factor
    return (normed * gain, normed, factor)


def norm_back(upstream, normed, factor, gain):
    inner = upstream * gain
    return factor * (inner - normed * jnp.mean(inner * normed, axis=-1, keepdims=True))


def silu_slope(values):
    sigmoid = jax.nn.sigmoid(values)
    return sigmoid * (1.0 + values * (1.0 - sigmoid))


def matmul(left, right):
    return jnp.dot(left, right, preferred_element_type=WIDE)


def over_rows(left, right):
    return lax.dot_general(left, right, (((0,), (0,)), ((), ())), preferred_element_type=WIDE)


def by_rows(left, right):
    return lax.dot_general(left, right, (((1,), (1,)), ((), ())), preferred_element_type=WIDE)


def exact_product(left, right):
    return jnp.dot(left, right, precision=lax.Precision.HIGHEST, preferred_element_type=WIDE)


def batched(spec, left, right):
    return jnp.einsum(spec, left, right, preferred_element_type=WIDE)


def windows(width):
    found = []
    for start in range(0, width, HD):
        low = start // LANES * LANES
        high = min(-(-(start + HD) // LANES) * LANES, width)
        found.append((low, high, start - low))
    return found


def masks_of(label_col, label_row, read_row):
    rows = lax.broadcasted_iota(jnp.int32, (SPAN, SPAN), 0)
    columns = lax.broadcasted_iota(jnp.int32, (SPAN, SPAN), 1)
    own = (rows >= columns) & (label_col == label_row)
    return own & (read_row > 0.5), own


def head_probs(query, keys, visible_memory, visible_own):
    scale = HD ** (-0.5)
    scores = [by_rows(query, key) * scale for key in keys]
    scores[1] = jnp.where(visible_memory, scores[1], MASKED)
    scores[2] = jnp.where(visible_own, scores[2], MASKED)
    highest = jnp.max(scores[0], axis=-1, keepdims=True)
    for item in scores[1:]:
        highest = jnp.maximum(highest, jnp.max(item, axis=-1, keepdims=True))
    raised = [jnp.exp(item - highest) for item in scores]
    totals = sum(jnp.sum(item, axis=-1, keepdims=True) for item in raised)
    inverse = 1.0 / totals
    return [item * inverse for item in raised]


def attention_kernel(
    query, key_memory, key_own, value_memory, value_own, key_fixed, value_fixed,
    label_col, label_row, read_row, out, total,
):
    visible_memory, visible_own = masks_of(label_col[0], label_row[0], read_row[0])
    total[...] = jnp.zeros_like(total)
    for low, high, offset in windows(query.shape[1]):
        lanes = lax.broadcasted_iota(jnp.int32, (SPAN, high - low), 1)
        inside = (lanes >= offset) & (lanes < offset + HD)
        mine = jnp.where(inside, query[:, low:high], jnp.zeros((), NARROW))
        keys = [item[:, low:high] for item in (key_fixed, key_memory, key_own)]
        values = [item[:, low:high] for item in (value_fixed, value_memory, value_own)]
        probs = head_probs(mine, keys, visible_memory, visible_own)
        result = sum(matmul(item.astype(NARROW), value) for item, value in zip(probs, values))
        total[:, low:high] += jnp.where(inside, result, 0.0)
    out[...] = total[...].astype(NARROW)


def attention_back_kernel(
    query, key_memory, key_own, value_memory, value_own, key_fixed, value_fixed,
    label_col, label_row, read_row, upstream,
    grad_query, grad_key_memory, grad_key_own, grad_value_memory, grad_value_own,
    grad_key_fixed, grad_value_fixed, *totals,
):
    scale = HD ** (-0.5)
    visible_memory, visible_own = masks_of(label_col[0], label_row[0], read_row[0])
    for total in totals:
        total[...] = jnp.zeros_like(total)

    @pl.when(pl.program_id(0) == 0)
    def _():
        grad_key_fixed[...] = jnp.zeros_like(grad_key_fixed)
        grad_value_fixed[...] = jnp.zeros_like(grad_value_fixed)

    key_sums = (grad_key_fixed, totals[1], totals[2])
    value_sums = (grad_value_fixed, totals[3], totals[4])
    for low, high, offset in windows(query.shape[1]):
        lanes = lax.broadcasted_iota(jnp.int32, (SPAN, high - low), 1)
        inside = (lanes >= offset) & (lanes < offset + HD)
        mine = jnp.where(inside, query[:, low:high], jnp.zeros((), NARROW))
        above = jnp.where(inside, upstream[:, low:high], jnp.zeros((), NARROW))
        keys = [item[:, low:high] for item in (key_fixed, key_memory, key_own)]
        values = [item[:, low:high] for item in (value_fixed, value_memory, value_own)]
        probs = head_probs(mine, keys, visible_memory, visible_own)
        grads = [by_rows(above, value) for value in values]
        inner = sum(
            jnp.sum(grad * item, axis=-1, keepdims=True) for grad, item in zip(grads, probs)
        )
        result = 0.0
        for index in range(3):
            slope = (probs[index] * (grads[index] - inner)).astype(NARROW)
            result = result + matmul(slope, keys[index])
            key_sums[index][:, low:high] += over_rows(slope, mine) * scale
            value_sums[index][:, low:high] += over_rows(probs[index].astype(NARROW), above)
        totals[0][:, low:high] += jnp.where(inside, result, 0.0) * scale
    places = (grad_query, grad_key_memory, grad_key_own, grad_value_memory, grad_value_own)
    for place, total in zip(places, totals):
        place[...] = total[...].astype(NARROW)


def attention_specs(blocks, width, fixed_count):
    rows = pl.BlockSpec((SPAN, width), lambda block: (block, 0))
    fixed = pl.BlockSpec((fixed_count, width), lambda block: (0, 0))
    col = pl.BlockSpec((1, SPAN, 1), lambda block: (block, 0, 0))
    row = pl.BlockSpec((1, 1, SPAN), lambda block: (block, 0, 0))
    return rows, fixed, [rows] * 5 + [fixed] * 2 + [col, row, row]


def attention(*operands):
    blocks, width, fixed_count = (operands[7].shape[0], operands[0].shape[1], operands[5].shape[0])
    rows, _, specs = attention_specs(blocks, width, fixed_count)
    pairs = blocks * SPAN * (2 * SPAN + fixed_count)
    return pl.pallas_call(
        attention_kernel,
        grid=(blocks,),
        in_specs=specs,
        out_specs=rows,
        out_shape=jax.ShapeDtypeStruct((blocks * SPAN, width), NARROW),
        scratch_shapes=[pltpu.VMEM((SPAN, width), WIDE)],
        cost_estimate=pl.CostEstimate(
            flops=16 * pairs * width,
            bytes_accessed=12 * blocks * SPAN * width,
            transcendentals=pairs * width // HD,
        ),
    )(*operands)


def attention_back(*operands):
    blocks, width, fixed_count = (operands[7].shape[0], operands[0].shape[1], operands[5].shape[0])
    rows, fixed, specs = attention_specs(blocks, width, fixed_count)
    pairs = blocks * SPAN * (2 * SPAN + fixed_count)
    return pl.pallas_call(
        attention_back_kernel,
        grid=(blocks,),
        in_specs=specs + [rows],
        out_specs=[rows] * 5 + [fixed] * 2,
        out_shape=[jax.ShapeDtypeStruct((blocks * SPAN, width), NARROW)] * 5
        + [jax.ShapeDtypeStruct((fixed_count, width), WIDE)] * 2,
        scratch_shapes=[pltpu.VMEM((SPAN, width), WIDE)] * 5,
        cost_estimate=pl.CostEstimate(
            flops=40 * pairs * width,
            bytes_accessed=24 * blocks * SPAN * width,
            transcendentals=pairs * width // HD,
        ),
    )(*operands)


def on_device(
    tokens,
    segments,
    norm_gain,
    ffn_gain,
    memory_gain,
    memory_rates,
    persistent,
    w_qkv,
    w_out,
    w_value,
    w_feature,
    w_gate_up,
    w_down,
    out_grad,
):
    parts, ranks = (lax.axis_size("ctx"), lax.axis_size("tp"))
    part, rank = (lax.axis_index("ctx"), lax.axis_index("tp"))
    half_index = lax.axis_index("shard")
    first_half = half_index == 0
    odd_part = part % 2 == 1
    groups, local_len, width = tokens.shape
    blocks_each = local_len // SPAN
    reach = -(-LAGS // blocks_each)
    step = 6.0 / (SPAN + 8)
    scale = HD ** (-0.5)

    def joined(own, other, axis):
        return jnp.concatenate(either(first_half, own, other), axis=axis)

    pair_tokens = flipped(tokens, "ctx", 1)
    far_tokens = flipped(tokens, "ctx", 2)
    core, outer = (part % 2, part // 2)
    feature_half = pick(w_feature.reshape(2, -1, w_feature.shape[1]), core, 0)
    feature_half = flipped(feature_half, "shard", 1)
    feature_other = jnp.concatenate(
        either(core == 0, feature_half, flipped(feature_half, "ctx", 1)), axis=0
    )
    smalls = [norm_gain, ffn_gain, memory_gain, memory_rates, persistent]
    small_flat = jnp.concatenate([item.reshape(-1) for item in smalls])
    small_other = flipped(small_flat, "shard", 1)
    small_others = []
    start = 0
    for item in smalls:
        small_others.append(small_other[start : start + item.size].reshape(item.shape))
        start += item.size
    value_other = flipped(after(w_value, feature_half), "shard", 1)

    gain_in_wide = joined(norm_gain, small_others[0], 0).astype(WIDE)
    gain_ffn_wide = joined(ffn_gain, small_others[1], 0).astype(WIDE)
    gain_mem = joined(memory_gain, small_others[2], 1).astype(WIDE)
    rates = joined(memory_rates, small_others[3], 0)
    persist = joined(persistent, small_others[4], 1)
    feature_cols = joined(w_feature, feature_other, 0)
    value_cols = joined(w_value, value_other, 0)
    weights = {}
    local_width = w_qkv.shape[2]
    local_units = feature_cols.shape[1]
    local_heads = local_width // HD
    persist_count = persist.shape[0]

    def scattered(array):
        return lax.psum_scatter(
            array.astype(NARROW), "tp", scatter_dimension=0, tiled=True
        ).astype(WIDE)

    def collected(array):
        return lax.all_gather(array.astype(NARROW), "tp", axis=0, tiled=True)

    def summed_over_ranks(array, kind=WIDE):
        bit = 1
        while bit < ranks:
            array = array.astype(kind)
            array = array.astype(WIDE) + flipped(array, "tp", bit).astype(WIDE)
            bit *= 2
        return array

    own_units = lax.dynamic_slice_in_dim(rates.astype(WIDE), rank * local_units, local_units, 1)
    retain, moment = (own_units[0], own_units[1])
    decays = [jnp.ones_like(retain)]
    for lag in range(1, LAGS):
        decays.append(retain * decays[-1] + moment**lag)

    labels_all = segments.astype(WIDE).reshape(groups, blocks_each, SPAN) + 1.0
    lasts_all = labels_all[:, :, -1]
    late_lasts = after(lasts_all, far_tokens)
    far_lasts = flipped(late_lasts, "ctx", 2)
    lasts_around = jnp.stack(
        [lasts_all, flipped(late_lasts, "ctx", 1), far_lasts, flipped(far_lasts, "ctx", 1)]
    )

    def last_of(index):
        delta, place = divmod(index, blocks_each)
        source = part + delta
        found = pick(lasts_around, jnp.clip(source, 0, parts - 1) ^ part, 0)[:, place]
        return jnp.where(source >= 0, found, 0.0)

    before_all = jnp.stack([last_of(own - 1) for own in range(blocks_each)], axis=1)
    linked_all = []
    for own in range(blocks_each):
        for lag in range(LAGS):
            source = own - 1 - lag
            present = part + source // blocks_each >= 0
            linked_all.append(present & (last_of(source) == last_of(own - 1)))
    linked_all = jnp.stack(linked_all, axis=1).reshape(groups, blocks_each, LAGS)

    def place_of(own, lag):
        return divmod(own - 1 - lag, blocks_each)

    head_of = (jnp.arange(local_width)[:, None] // HD == jnp.arange(local_heads)).astype(WIDE)
    gain_flat = gain_mem.reshape(local_width)

    def head_mean(values):
        return exact_product(values, head_of) / HD

    def head_spread(values):
        return exact_product(values, head_of.T)

    count = groups
    rows = count * local_len
    blocks = count * blocks_each
    part_rows = rows // STREAMS
    part_blocks = blocks // STREAMS

    def own_rows(array):
        sub = array.shape[0] // ranks
        return lax.dynamic_slice_in_dim(array, rank * sub, sub, 0)

    class Stream:
        pass

    def linked(one, square, corner):
        spread = jnp.repeat(one.linked[:, :, LAGS - 2 :: -1], SPAN, axis=2)[:, :, None]
        square = jnp.where(spread, square, jnp.zeros_like(square))
        corner = jnp.where(
            one.linked[:, :, LAGS - 1, None, None], corner, jnp.zeros_like(corner)
        )
        return square, corner

    def packed(square, corner):
        wide = square.shape[-1]
        lanes = corner.transpose(2, 0, 1, 3).reshape(CORNER, -1)
        lanes = jnp.pad(lanes, ((0, 0), (0, wide - lanes.shape[1])))
        return jnp.concatenate([square.reshape(-1, wide), lanes], axis=0)

    def unpacked(array):
        square = array[:-CORNER].reshape(count, blocks_each, SPAN, -1)
        corner = array[-CORNER:, : blocks * CORNER]
        corner = corner.reshape(CORNER, count, blocks_each, CORNER).transpose(1, 2, 0, 3)
        return square, corner

    def begin(one, index):
        def mine(array):
            return array[index * count : (index + 1) * count]

        one.flat = mine(tokens).reshape(rows, width)
        one.upstream_low = mine(out_grad).reshape(rows, width)
        one.labels = mine(labels_all)
        one.lasts = mine(lasts_all)
        one.before = mine(before_all)
        one.linked = mine(linked_all)
        one.keeping = (one.lasts == one.before).astype(WIDE)[:, :, None, None]
        one.writing = (one.labels == one.lasts[:, :, None]).astype(WIDE)[..., None]
        one.reading = (one.labels == one.before[:, :, None]).astype(WIDE)

        def features_of(piece):
            low = norm_rows(piece.astype(WIDE), gain_in_wide)[0].astype(NARROW)
            return low, matmul(low.reshape(rows, width), feature_cols)

        def shaped(values):
            return values.reshape(count, blocks_each, SPAN, local_units)

        low, preact = features_of(mine(tokens))
        one.preact = lax.optimization_barrier(preact)
        one.input_low = low.reshape(rows, width)
        one.features = jax.nn.silu(one.preact).astype(NARROW)
        squares = jnp.sum(jnp.square(one.features.astype(WIDE)), axis=1)
        one.key_scale = lax.rsqrt(summed_over_ranks(squares) + EPSILON)
        far, pair, one.features, one.key_scale = lax.optimization_barrier(
            (mine(far_tokens), mine(pair_tokens), one.features, one.key_scale)
        )
        close = [pair, flipped(far, "ctx", 1)]
        one.around = {0: shaped(one.features)}
        for delta, piece in (
            (-1, jnp.where(odd_part, close[0], close[1])),
            (1, jnp.where(odd_part, close[1], close[0])),
            (2, far),
        ):
            one.around[delta] = shaped(jax.nn.silu(features_of(piece)[1]).astype(NARROW))
        one.around[-2] = one.around[2]
        one.targets = matmul(one.input_low, value_cols).reshape(
            count, blocks_each, SPAN, local_width
        )
        weighted = [(one.around[0].astype(WIDE) * decay).astype(NARROW) for decay in decays]
        products = []
        corners = []
        for own in range(blocks_each):
            row = []
            for lag in range(LAGS - 1, -1, -1):
                delta, place = place_of(own, lag)
                near, past = weighted[lag][:, own], one.around[delta][:, place]
                if lag == LAGS - 1:
                    near, past = near[:, :CORNER], past[:, SPAN - CORNER :]
                    corners.append(batched("sth,suh->stu", near, past))
                else:
                    row.append(batched("sth,suh->stu", near, past))
            products.append(jnp.concatenate(row, axis=2))
        one.products = packed(
            jnp.stack(products, axis=1).astype(NARROW), jnp.stack(corners, axis=1).astype(NARROW)
        )
        one.mixing = lax.psum(one.products, "tp")

    def span_of(own):
        start = (reach * blocks_each - LAGS + own) * SPAN
        return slice(start, start + LAGS * SPAN)

    def remember(one):
        square, corner = linked(one, *unpacked(one.mixing))
        corner = jnp.pad(
            corner, ((0, 0), (0, 0), (0, SPAN - CORNER), (SPAN - CORNER, 0))
        )
        one.mixing = jnp.concatenate([corner, square], axis=3)
        one.scales = one.key_scale.reshape(count, blocks_each, SPAN, 1)
        halos = [
            jnp.zeros((count, blocks_each * SPAN, local_width), NARROW) for _ in range(reach)
        ]
        pending = {}
        for turn in range(parts):
            for hop in range(1, reach + 1):
                if (turn - hop, hop) in pending:
                    halos[reach - hop] = halos[reach - hop] + pending[(turn - hop, hop)]
            known = jnp.concatenate(halos, axis=1)
            recalls = []
            errors = []
            for own in range(blocks_each):
                total = batched("stu,sud->std", one.mixing[:, own], known[:, span_of(own)])
                recall = -step * one.scales[:, own] * total
                error = one.writing[:, own] * (
                    one.keeping[:, own] * recall - one.targets[:, own]
                )
                recalls.append(recall)
                errors.append(error)
                known = jnp.concatenate(
                    [known, (one.scales[:, own] * error).astype(NARROW)], axis=1
                )
            for hop in range(1, reach + 1):
                if turn + hop < parts:
                    pending[(turn, hop)] = passed_along(
                        known[:, reach * blocks_each * SPAN :], "ctx", [(turn, turn + hop)]
                    )
        one.known = known
        one.recall = jnp.stack(recalls, 1)
        one.errors = jnp.stack(errors, 1)
        masked = (one.reading[..., None] * one.recall).reshape(rows, local_width)
        one.head_factor = head_spread(lax.rsqrt(head_mean(masked * masked) + EPSILON))
        one.head_unit = masked * one.head_factor
        retrieved = (one.head_unit * gain_flat).astype(NARROW)
        one.retrieved_full = lax.all_gather(retrieved, "tp", axis=1, tiled=True)

    def attend(one):
        def projected(values, weight):
            return matmul(values, weight).astype(NARROW)

        labels = one.labels.reshape(part_blocks, SPAN)
        reading = one.reading.reshape(part_blocks, SPAN)
        one.operands = (
            projected(one.input_low, query_w),
            projected(one.retrieved_full, key_w),
            projected(one.input_low, key_w),
            projected(one.retrieved_full, value_w),
            projected(one.input_low, value_w),
            fixed_keys,
            fixed_values,
            labels[:, :, None],
            labels[:, None, :],
            reading[:, None, :],
        )
        one.attended = attention(*one.operands)
        one.residual = own_rows(one.flat).astype(WIDE)
        one.branch = scattered(matmul(one.attended, weights["out"]))

    def middle(one):
        if one is not streams[0]:
            one.branch = after(one.branch, streams[0].mid_own)
        one.hidden = one.residual + one.branch
        normed_mid, one.unit_mid, one.factor_mid = norm_rows(one.hidden, gain_ffn_wide)
        one.mid_own = normed_mid.astype(NARROW)
        one.mid_low = collected(one.mid_own)

    def feed(one):
        gate = matmul(one.mid_low, weights["gate"])
        upper = matmul(one.mid_low, weights["up"])
        one.activ = (jax.nn.silu(gate) * upper).astype(NARROW)
        grad_act = by_rows(one.upstream_low, weights["down"])
        one.grad_gate = (grad_act * upper * silu_slope(gate)).astype(NARROW)
        one.grad_upper = (grad_act * jax.nn.silu(gate)).astype(NARROW)
        one.grad_mid = scattered(
            by_rows(one.grad_gate, weights["gate"]) + by_rows(one.grad_upper, weights["up"])
        )

    def middle_back(one):
        if one is not streams[0]:
            one.grad_mid = after(one.grad_mid, streams[0].grad_hidden)
        grad_mid = one.grad_mid
        one.grad_gain_ffn = jnp.sum(grad_mid * one.unit_mid, axis=0)
        upstream = own_rows(one.upstream_low).astype(WIDE)
        one.grad_hidden = upstream + norm_back(
            grad_mid, one.unit_mid, one.factor_mid, gain_ffn_wide
        )
        one.grad_mixed = collected(one.grad_hidden)

    def branch_out(one):
        activ = after(one.activ, whole.grad_retrieved)
        one.branch = scattered(matmul(activ, weights["down"]))

    def rank_major(array):
        array = array.reshape(STREAMS, ranks, -1, width)
        return array.transpose(1, 0, 2, 3).reshape(-1, width)

    def stream_major(array):
        array = array.reshape(ranks, STREAMS, -1, width)
        return array.transpose(1, 0, 2, 3).reshape(-1, width)

    def finish_output(one):
        own = jnp.concatenate([item.hidden + item.branch for item in streams], axis=0)
        one.output = collected(after(own, one.grad_mixing))

    def attend_back(one):
        grad_attended = by_rows(one.grad_mixed, weights["out"]).astype(NARROW)
        (
            one.grad_queries,
            one.key_memory,
            one.key_token,
            one.value_memory,
            one.value_token,
            one.key_fixed,
            one.value_fixed,
        ) = attention_back(*one.operands, grad_attended)
        partial = by_rows(one.key_memory, key_w) + by_rows(one.value_memory, value_w)
        one.partial = partial.astype(NARROW)
        one.grad_retrieved = lax.psum_scatter(one.partial, "tp", scatter_dimension=1, tiled=True)

    def heads_back(one):
        grad_heads = one.grad_retrieved.astype(WIDE)
        one.grad_gain_memory = jnp.sum(grad_heads * one.head_unit, axis=0)
        inner = grad_heads * gain_flat
        grad_masked = one.head_factor * (
            inner - one.head_unit * head_spread(head_mean(inner * one.head_unit))
        )
        one.grad_read = one.reading[..., None] * grad_masked.reshape(
            count, blocks_each, SPAN, local_width
        )

    def remember_back(one):
        later = [0.0] * blocks_each
        pending = {}
        for turn in range(parts):
            for hop in range(1, reach + 1):
                if (turn - hop, hop) in pending:
                    arrived = pending[(turn - hop, hop)].astype(WIDE)
                    for own in range(blocks_each):
                        later[own] = later[own] + arrived[:, own * SPAN : (own + 1) * SPAN]
            known = [0.0] * (reach * blocks_each) + later
            grad_errors = [None] * blocks_each
            grad_recalls = [None] * blocks_each
            raws = [None] * blocks_each
            for own in range(blocks_each - 1, -1, -1):
                grad_scaled = -step * known[reach * blocks_each + own]
                grad_error = one.scales[:, own] * grad_scaled
                grad_recall = (
                    one.grad_read[:, own] + one.writing[:, own] * one.keeping[:, own] * grad_error
                )
                grad_errors[own] = jnp.broadcast_to(grad_error, grad_recall.shape)
                grad_recalls[own] = grad_recall
                raws[own] = (one.scales[:, own] * grad_recall).astype(NARROW)
                carried = batched("stu,std->sud", one.mixing[:, own], raws[own])
                for index in range(LAGS):
                    place = reach * blocks_each - LAGS + own + index
                    known[place] = (
                        known[place] + carried[:, index * SPAN : (index + 1) * SPAN]
                    )
            for hop in range(1, reach + 1):
                place = parts - 1 - turn
                if place - hop >= 0:
                    start = (reach - hop) * blocks_each
                    sent = jnp.concatenate(known[start : start + blocks_each], axis=1)
                    pending[(turn, hop)] = passed_along(
                        sent.astype(NARROW), "ctx", [(place, place - hop)]
                    )
        grad_errors = jnp.stack(grad_errors, 1)
        grad_recalls = jnp.stack(grad_recalls, 1)
        one.grad_targets = (-one.writing * grad_errors).astype(NARROW).reshape(rows, local_width)
        scale_part = jnp.sum(grad_recalls * one.recall + one.errors * grad_errors, axis=3)
        one.scale_sum = summed_over_ranks(scale_part.reshape(rows))
        grad_mixing = []
        for own in range(blocks_each):
            grad_mixing.append(
                -step * batched("std,sud->stu", raws[own], one.known[:, span_of(own)])
            )
        grad_mixing = jnp.stack(grad_mixing, 1)
        square, corner = linked(
            one, grad_mixing[..., SPAN:], grad_mixing[:, :, :CORNER, SPAN - CORNER : SPAN]
        )
        grad_mixing = packed(square.astype(NARROW), corner.astype(NARROW))
        branches = [item.branch for item in streams]
        grad_mixing, branches = lax.optimization_barrier((grad_mixing, branches))
        for item, branch in zip(streams, branches):
            item.branch = branch
        one.packed_back = grad_mixing
        one.grad_mixing = lax.psum(grad_mixing, "tp")

    def features_back(one):
        square, corner = unpacked(one.grad_mixing)

        def column(own, lag):
            if lag == LAGS - 1:
                return corner[:, own]
            start = (LAGS - 2 - lag) * SPAN
            return square[:, own, :, start : start + SPAN]

        needed = {}
        for hop in range(1, reach + 1):
            sends = [(source, source - hop) for source in range(hop, parts)]
            for last_lag in (False, True):
                pairs = [
                    (own, lag)
                    for own in range(blocks_each)
                    for lag in range(LAGS)
                    if place_of(own, lag)[0] == -hop and (lag == LAGS - 1) == last_lag
                ]
                if not pairs:
                    continue
                moved = passed_along(
                    jnp.stack([column(own, lag) for own, lag in pairs], axis=1), "ctx", sends
                )
                for place, (own, lag) in enumerate(pairs):
                    needed[(hop * blocks_each + own, lag)] = moved[:, place]
        for own in range(blocks_each):
            for lag in range(LAGS):
                needed[(own, lag)] = column(own, lag)
        grad_features = []
        one.grad_decays = [0.0] * LAGS
        rest = SPAN - CORNER
        for own in range(blocks_each):
            total = 0.0
            for lag in range(LAGS):
                own_features = one.around[0][:, own].astype(WIDE)
                delta, place = place_of(own, lag)
                past = one.around[delta][:, place]
                later = own + 1 + lag
                delta, place = divmod(later, blocks_each)
                future = one.around[delta][:, place]
                if lag == LAGS - 1:
                    own_features, past, future = (
                        own_features[:, :CORNER],
                        past[:, rest:],
                        future[:, :CORNER],
                    )
                from_reads = batched("stu,suh->sth", needed[(own, lag)], past)
                one.grad_decays[lag] = one.grad_decays[lag] + jnp.sum(
                    own_features * from_reads, axis=(0, 1)
                )
                from_writes = batched("stu,sth->suh", needed[(later, lag)], future)
                if lag == LAGS - 1:
                    from_reads = jnp.pad(from_reads, ((0, 0), (0, rest), (0, 0)))
                    from_writes = jnp.pad(from_writes, ((0, 0), (rest, 0), (0, 0)))
                total = total + decays[lag] * (from_reads + from_writes)
            grad_features.append(total)
        grad_features = jnp.stack(grad_features, 1).reshape(rows, local_units)
        grad_features = grad_features - (one.key_scale * one.key_scale * one.scale_sum)[
            :, None
        ] * one.features.astype(WIDE)
        one.grad_pre = (grad_features * silu_slope(one.preact)).astype(NARROW)

    def inputs_back(one):
        one.grad_input = (one.early + by_rows(one.grad_pre, feature_cols)).astype(NARROW)

    def input_early(one):
        queries, keys, values, targets, _ = lax.optimization_barrier(
            (one.grad_queries, one.key_token, one.value_token, one.grad_targets, one.packed_back)
        )
        one.early = (
            by_rows(queries, query_w)
            + by_rows(keys, key_w)
            + by_rows(values, value_w)
            + by_rows(targets, value_cols)
        )

    def tokens_back(one):
        grad_input = one.grad_input
        _, unit_in, factor_in = norm_rows(one.residual, gain_in_wide)
        one.grad_gain_in = jnp.sum(grad_input * unit_in, axis=0)
        grad_own = one.grad_hidden + norm_back(grad_input, unit_in, factor_in, gain_in_wide)
        one.grad_tokens = stream_major(collected(grad_own)).astype(WIDE)

    whole = Stream()
    streams = [Stream() for _ in range(STREAMS)]

    def over(function):
        total = function(streams[0])
        for one in streams[1:]:
            total = total + function(one)
        return total

    def every(stage):
        for one in streams:
            stage(one)

    class Reduction:
        def __init__(self, array, by_row):
            array = array.astype(NARROW)
            *self.lead, self.high, self.wide = array.shape
            self.by_row = by_row
            self.axis = len(self.lead)
            if by_row:
                array = array.reshape(*self.lead, 2, 2, 2, self.high // 8, self.wide)
            else:
                array = array.reshape(2, 2, self.high // 4, self.wide)
            self.array = array
            self.exchange(core, self.axis + 1 if by_row else 0, "ctx", 1)

        def exchange(self, index, axis, over_axis, bit):
            own, other = (pick(self.array, place, axis) for place in (index, 1 - index))
            self.add(own, flipped(other, over_axis, bit))

        def add(self, own, arrived):
            self.array = (own.astype(WIDE) + arrived.astype(WIDE)).astype(NARROW)

        def across(self):
            if self.by_row:
                self.exchange(half_index, self.axis, "shard", 1)
                return
            half = self.wide // 2
            own, other = (
                lax.dynamic_slice_in_dim(self.array, place * half, half, 2)
                for place in (half_index, 1 - half_index)
            )
            self.add(own, flipped(other, "shard", 1))

        def apart(self):
            self.exchange(outer, self.axis if self.by_row else 0, "ctx", 2)

        def together(self):
            pair = either(outer == 0, self.array, flipped(self.array, "ctx", 2))
            self.array = jnp.stack(pair, axis=self.axis if self.by_row else 0)

        def result(self):
            pair = either(core == 0, self.array, flipped(self.array, "ctx", 1))
            array = jnp.stack(pair, axis=self.axis if self.by_row else 0).astype(WIDE)
            if self.by_row:
                return array.reshape(*self.lead, self.high // 2, self.wide)
            return array.reshape(self.high, self.wide // 2)

    def tied(one, names, *reductions):
        held = [getattr(one, name) for name in names]
        held, arrays = lax.optimization_barrier((held, [item.array for item in reductions]))
        for name, value in zip(names, held):
            setattr(one, name, value)
        for item, array in zip(reductions, arrays):
            item.array = array

    class Holder:
        def __init__(self, array):
            self.array = array

    def fetched(one, names, start, *arrays):
        holders = [Holder(flipped(after(item, start), "shard", 1)) for item in arrays]
        tied(one, names, *holders)
        return [holder.array for holder in holders]

    def merged(name):
        setattr(
            whole, name, jnp.concatenate([getattr(one, name) for one in streams], axis=0)
        )

    begin(whole, 0)
    (qkv_other,) = fetched(whole, ["mixing"], whole.products, w_qkv)
    qkv_cols = joined(w_qkv, qkv_other, 1)
    query_w = qkv_cols[0]
    key_w = qkv_cols[1]
    value_w = qkv_cols[2]
    fixed_keys = matmul(persist, key_w).astype(NARROW)
    fixed_values = matmul(persist, value_w).astype(NARROW)
    remember(whole)
    out_other, down_other = fetched(whole, ["retrieved_full"], whole.recall, w_out, w_down)
    weights["out"] = joined(w_out, out_other, 1)
    weights["down"] = joined(w_down, down_other, 1)
    for index, one in enumerate(streams):
        for name in ("flat", "upstream_low", "input_low", "retrieved_full", "labels", "reading"):
            array = getattr(whole, name)
            size = array.shape[0] // STREAMS
            setattr(one, name, array[index * size : (index + 1) * size])
        attend(one)
    first_stream, last_stream = streams[0], streams[-1]
    (gate_other,) = fetched(last_stream, ["branch"], first_stream.attended, w_gate_up[0])
    weights["gate"] = joined(w_gate_up[0], gate_other, 0)
    every(middle)
    (up_other,) = fetched(first_stream, ["mid_low"], first_stream.hidden, w_gate_up[1])
    weights["up"] = joined(w_gate_up[1], up_other, 0)
    first_stream.mid_low = after(first_stream.mid_low, last_stream.hidden)
    every(feed)
    first_stream.grad_mid = after(first_stream.grad_mid, last_stream.mid_low)
    feed_reductions = [
        Reduction(over(lambda one: over_rows(one.activ, one.upstream_low)), False),
        Reduction(
            jnp.stack(
                [
                    over(lambda one: over_rows(one.mid_low, one.grad_gate)).astype(NARROW),
                    over(lambda one: over_rows(one.mid_low, one.grad_upper)).astype(NARROW),
                ]
            ),
            True,
        ),
    ]
    every(middle_back)
    first_stream.grad_mixed = after(first_stream.grad_mixed, last_stream.grad_mid)
    for item in feed_reductions:
        item.across()
    attend_back(first_stream)
    tied(last_stream, ["grad_mixed"], *feed_reductions, Holder(first_stream.partial))
    attend_back(last_stream)
    for name in (
        "grad_retrieved",
        "grad_queries",
        "key_token",
        "value_token",
        "key_memory",
        "value_memory",
    ):
        merged(name)
    persist_wide = persist.astype(WIDE)
    key_fixed = over(lambda one: one.key_fixed)
    value_fixed = over(lambda one: one.value_fixed)
    grad_query_w = over_rows(whole.input_low, whole.grad_queries)
    grad_key_w = (
        over_rows(whole.input_low, whole.key_token)
        + over_rows(whole.retrieved_full, whole.key_memory)
        + exact_product(persist_wide.T, key_fixed)
    )
    grad_value_proj = (
        over_rows(whole.input_low, whole.value_token)
        + over_rows(whole.retrieved_full, whole.value_memory)
        + exact_product(persist_wide.T, value_fixed)
    )
    mix_reductions = [
        Reduction(over(lambda one: over_rows(one.attended, one.grad_mixed)), False),
        Reduction(
            jnp.stack(
                [item.astype(NARROW) for item in (grad_query_w, grad_key_w, grad_value_proj)]
            ),
            True,
        ),
    ]
    grad_persist = exact_product(key_fixed, key_w.astype(WIDE).T) + exact_product(
        value_fixed, value_w.astype(WIDE).T
    )
    for item in feed_reductions:
        item.apart()
    tied(whole, ["grad_retrieved"], *feed_reductions, *mix_reductions)
    every(branch_out)
    heads_back(whole)
    remember_back(whole)
    persist_sum = Holder(summed_over_ranks(after(grad_persist, whole.packed_back), NARROW))
    input_early(whole)
    grad_targets = after(whole.grad_targets, whole.packed_back)
    target_reduction = Reduction(over_rows(whole.input_low, grad_targets), True)
    for item in feed_reductions + mix_reductions:
        item.array = after(item.array, whole.packed_back)
    for item in feed_reductions:
        item.together()
    for item in mix_reductions:
        item.across()
    tied(
        whole,
        ["grad_mixing", "scale_sum", "early"],
        *feed_reductions,
        *mix_reductions,
        target_reduction,
        persist_sum,
    )
    finish_output(whole)
    features_back(whole)
    inputs_back(whole)
    grad_input, whole.output = lax.optimization_barrier(
        (rank_major(whole.grad_input), whole.output)
    )
    whole.grad_input = scattered(grad_input)
    merged("residual")
    merged("grad_hidden")

    grad_decays = whole.grad_decays
    grad_retain = 0.0
    grad_moment = 0.0
    retain_slope = jnp.zeros_like(retain)
    for lag in range(1, LAGS):
        retain_slope = retain * retain_slope + decays[lag - 1]
        moment_slope = 0.0
        for power in range(1, lag + 1):
            moment_slope = moment_slope + power * retain ** (lag - power) * moment ** (power - 1)
        grad_retain = grad_retain + retain_slope * grad_decays[lag]
        grad_moment = grad_moment + moment_slope * grad_decays[lag]
    grad_rates = jnp.stack([grad_retain, grad_moment])

    def summed(pieces):
        small = jnp.concatenate([piece.reshape(-1) for piece in pieces])
        for axis, bit in (("ctx", 1), ("shard", 1), ("ctx", 2)):
            small = small + flipped(small, axis, bit)
        return small

    small = Holder(summed([persist_sum.array, whole.grad_gain_memory, grad_rates]))
    feature_reduction = Reduction(over_rows(whole.input_low, whole.grad_pre), True)
    late_reductions = [feature_reduction, target_reduction]
    for item in mix_reductions:
        item.apart()
    for item in late_reductions:
        item.across()
    tied(whole, ["grad_input"], small, *mix_reductions, *late_reductions)
    tokens_back(whole)
    for item in mix_reductions:
        item.together()
    for item in late_reductions:
        item.apart()
        item.together()
    gains = summed([whole.grad_gain_in, over(lambda one: one.grad_gain_ffn)])
    gain_in_sum, gain_ffn_sum = summed_over_ranks(gains).reshape(2, width)
    cut = persist_sum.array.size
    middle_cut = cut + local_width
    grad_persist = small.array[:cut].reshape(persist_count, width)
    grad_gain_memory = small.array[cut:middle_cut].reshape(local_heads, HD)
    grad_rates = small.array[middle_cut:].reshape(2, local_units)
    grad_down, grad_gate_up = [item.result() for item in feed_reductions]
    grad_out_rows, grad_qkv = [item.result() for item in mix_reductions]
    grad_feature_w, grad_target_w = [item.result() for item in late_reductions]

    def own_half(array, axis):
        size = array.shape[axis] // 2
        return lax.dynamic_slice_in_dim(array, half_index * size, size, axis)

    return (
        stream_major(whole.output).reshape(tokens.shape),
        whole.grad_tokens.reshape(tokens.shape),
        own_half(gain_in_sum, 0),
        own_half(gain_ffn_sum, 0),
        own_half(grad_gain_memory, 1),
        own_half(grad_rates, 0),
        own_half(grad_persist, 1),
        grad_qkv,
        grad_out_rows,
        grad_target_w,
        grad_feature_w,
        grad_gate_up,
        grad_down,
    )


def solution(mesh):
    placed = (
        P("shard", "ctx", None),
        P("shard", "ctx"),
        P("shard"),
        P("shard"),
        P("tp", "shard"),
        P("shard", None),
        P(None, "shard"),
        P(None, "shard", "tp"),
        P("tp", "shard"),
        P("shard", "tp"),
        P("shard", "tp"),
        P(None, "shard", "tp"),
        P("tp", "shard"),
        P("shard", "ctx", None),
    )
    return jax.shard_map(
        on_device,
        mesh=mesh,
        in_specs=placed,
        out_specs=(
            P("shard", "ctx", None),
            P("shard", "ctx", None),
            P("shard"),
            P("shard"),
            P("tp", "shard"),
            P("shard", "tp"),
            P(None, "shard"),
            P(None, "shard", "tp"),
            P("tp", "shard"),
            P("shard", "tp"),
            P("shard", "tp"),
            P(None, "shard", "tp"),
            P("tp", "shard"),
        ),
        check_vma=False,
    )
```

```python
import jax
import jax.numpy as jnp
from jax import lax
from jax.experimental import pallas as pl
from jax.experimental.pallas import tpu as pltpu
from jax.sharding import PartitionSpec as P

HD = 96
SPAN = 256
LANES = 128
LIMIT = 800
LAGS = (LIMIT + SPAN - 2) // SPAN
CORNER = LIMIT - (LAGS - 1) * SPAN
STREAMS = 2


EPSILON = 1e-06
MASKED = -1e30
WIDE = jnp.float32
NARROW = jnp.bfloat16


def passed_along(value, axis, pairs):
    return lax.ppermute(value, axis, pairs)


def flipped(value, axis, bit):
    return lax.ppermute(value, axis, [(i, i ^ bit) for i in range(lax.axis_size(axis))])


def either(first, one, other):
    return jnp.where(first, one, other), jnp.where(first, other, one)


def pick(array, place, axis):
    return lax.dynamic_index_in_dim(array, place, axis, keepdims=False)


def after(value, *others):
    return lax.optimization_barrier((value, *others))[0]


def norm_rows(values, gain):
    factor = lax.rsqrt(jnp.mean(values * values, axis=-1, keepdims=True) + EPSILON)
    normed = values * factor
    return (normed * gain, normed, factor)


def norm_back(upstream, normed, factor, gain):
    inner = upstream * gain
    return factor * (inner - normed * jnp.mean(inner * normed, axis=-1, keepdims=True))


def silu_slope(values):
    sigmoid = jax.nn.sigmoid(values)
    return sigmoid * (1.0 + values * (1.0 - sigmoid))


def matmul(left, right):
    return jnp.dot(left, right, preferred_element_type=WIDE)


def over_rows(left, right):
    return lax.dot_general(left, right, (((0,), (0,)), ((), ())), preferred_element_type=WIDE)


def by_rows(left, right):
    return lax.dot_general(left, right, (((1,), (1,)), ((), ())), preferred_element_type=WIDE)


def exact_product(left, right):
    return jnp.dot(left, right, precision=lax.Precision.HIGHEST, preferred_element_type=WIDE)


def batched(spec, left, right):
    return jnp.einsum(spec, left, right, preferred_element_type=WIDE)


def windows(width):
    found = []
    for start in range(0, width, HD):
        low = start // LANES * LANES
        high = min(-(-(start + HD) // LANES) * LANES, width)
        found.append((low, high, start - low))
    return found


def masks_of(label_col, label_row, read_row):
    rows = lax.broadcasted_iota(jnp.int32, (SPAN, SPAN), 0)
    columns = lax.broadcasted_iota(jnp.int32, (SPAN, SPAN), 1)
    own = (rows >= columns) & (label_col == label_row)
    return own & (read_row > 0.5), own


def head_probs(query, keys, visible_memory, visible_own):
    scale = HD ** (-0.5)
    scores = [by_rows(query, key) * scale for key in keys]
    scores[1] = jnp.where(visible_memory, scores[1], MASKED)
    scores[2] = jnp.where(visible_own, scores[2], MASKED)
    highest = jnp.max(scores[0], axis=-1, keepdims=True)
    for item in scores[1:]:
        highest = jnp.maximum(highest, jnp.max(item, axis=-1, keepdims=True))
    raised = [jnp.exp(item - highest) for item in scores]
    totals = sum(jnp.sum(item, axis=-1, keepdims=True) for item in raised)
    inverse = 1.0 / totals
    return [item * inverse for item in raised]


def attention_kernel(
    query, key_memory, key_own, value_memory, value_own, key_fixed, value_fixed,
    label_col, label_row, read_row, out, total,
):
    visible_memory, visible_own = masks_of(label_col[0], label_row[0], read_row[0])
    total[...] = jnp.zeros_like(total)
    for low, high, offset in windows(query.shape[1]):
        lanes = lax.broadcasted_iota(jnp.int32, (SPAN, high - low), 1)
        inside = (lanes >= offset) & (lanes < offset + HD)
        mine = jnp.where(inside, query[:, low:high], jnp.zeros((), NARROW))
        keys = [item[:, low:high] for item in (key_fixed, key_memory, key_own)]
        values = [item[:, low:high] for item in (value_fixed, value_memory, value_own)]
        probs = head_probs(mine, keys, visible_memory, visible_own)
        result = sum(matmul(item.astype(NARROW), value) for item, value in zip(probs, values))
        total[:, low:high] += jnp.where(inside, result, 0.0)
    out[...] = total[...].astype(NARROW)


def attention_back_kernel(
    query, key_memory, key_own, value_memory, value_own, key_fixed, value_fixed,
    label_col, label_row, read_row, upstream,
    grad_query, grad_key_memory, grad_key_own, grad_value_memory, grad_value_own,
    grad_key_fixed, grad_value_fixed, *totals,
):
    scale = HD ** (-0.5)
    visible_memory, visible_own = masks_of(label_col[0], label_row[0], read_row[0])
    for total in totals:
        total[...] = jnp.zeros_like(total)

    @pl.when(pl.program_id(0) == 0)
    def _():
        grad_key_fixed[...] = jnp.zeros_like(grad_key_fixed)
        grad_value_fixed[...] = jnp.zeros_like(grad_value_fixed)

    key_sums = (grad_key_fixed, totals[1], totals[2])
    value_sums = (grad_value_fixed, totals[3], totals[4])
    for low, high, offset in windows(query.shape[1]):
        lanes = lax.broadcasted_iota(jnp.int32, (SPAN, high - low), 1)
        inside = (lanes >= offset) & (lanes < offset + HD)
        mine = jnp.where(inside, query[:, low:high], jnp.zeros((), NARROW))
        above = jnp.where(inside, upstream[:, low:high], jnp.zeros((), NARROW))
        keys = [item[:, low:high] for item in (key_fixed, key_memory, key_own)]
        values = [item[:, low:high] for item in (value_fixed, value_memory, value_own)]
        probs = head_probs(mine, keys, visible_memory, visible_own)
        grads = [by_rows(above, value) for value in values]
        inner = sum(
            jnp.sum(grad * item, axis=-1, keepdims=True) for grad, item in zip(grads, probs)
        )
        result = 0.0
        for index in range(3):
            slope = (probs[index] * (grads[index] - inner)).astype(NARROW)
            result = result + matmul(slope, keys[index])
            key_sums[index][:, low:high] += over_rows(slope, mine) * scale
            value_sums[index][:, low:high] += over_rows(probs[index].astype(NARROW), above)
        totals[0][:, low:high] += jnp.where(inside, result, 0.0) * scale
    places = (grad_query, grad_key_memory, grad_key_own, grad_value_memory, grad_value_own)
    for place, total in zip(places, totals):
        place[...] = total[...].astype(NARROW)


def attention_specs(blocks, width, fixed_count):
    rows = pl.BlockSpec((SPAN, width), lambda block: (block, 0))
    fixed = pl.BlockSpec((fixed_count, width), lambda block: (0, 0))
    col = pl.BlockSpec((1, SPAN, 1), lambda block: (block, 0, 0))
    row = pl.BlockSpec((1, 1, SPAN), lambda block: (block, 0, 0))
    return rows, fixed, [rows] * 5 + [fixed] * 2 + [col, row, row]


def attention(*operands):
    blocks, width, fixed_count = (operands[7].shape[0], operands[0].shape[1], operands[5].shape[0])
    rows, _, specs = attention_specs(blocks, width, fixed_count)
    pairs = blocks * SPAN * (2 * SPAN + fixed_count)
    return pl.pallas_call(
        attention_kernel,
        grid=(blocks,),
        in_specs=specs,
        out_specs=rows,
        out_shape=jax.ShapeDtypeStruct((blocks * SPAN, width), NARROW),
        scratch_shapes=[pltpu.VMEM((SPAN, width), WIDE)],
        cost_estimate=pl.CostEstimate(
            flops=16 * pairs * width,
            bytes_accessed=12 * blocks * SPAN * width,
            transcendentals=pairs * width // HD,
        ),
    )(*operands)


def attention_back(*operands):
    blocks, width, fixed_count = (operands[7].shape[0], operands[0].shape[1], operands[5].shape[0])
    rows, fixed, specs = attention_specs(blocks, width, fixed_count)
    pairs = blocks * SPAN * (2 * SPAN + fixed_count)
    return pl.pallas_call(
        attention_back_kernel,
        grid=(blocks,),
        in_specs=specs + [rows],
        out_specs=[rows] * 5 + [fixed] * 2,
        out_shape=[jax.ShapeDtypeStruct((blocks * SPAN, width), NARROW)] * 5
        + [jax.ShapeDtypeStruct((fixed_count, width), WIDE)] * 2,
        scratch_shapes=[pltpu.VMEM((SPAN, width), WIDE)] * 5,
        cost_estimate=pl.CostEstimate(
            flops=40 * pairs * width,
            bytes_accessed=24 * blocks * SPAN * width,
            transcendentals=pairs * width // HD,
        ),
    )(*operands)


def on_device(
    tokens,
    segments,
    norm_gain,
    ffn_gain,
    memory_gain,
    memory_rates,
    persistent,
    w_qkv,
    w_out,
    w_value,
    w_feature,
    w_gate_up,
    w_down,
    out_grad,
):
    parts, ranks = (lax.axis_size("ctx"), lax.axis_size("tp"))
    part, rank = (lax.axis_index("ctx"), lax.axis_index("tp"))
    half_index = lax.axis_index("shard")
    first_half = half_index == 0
    odd_part = part % 2 == 1
    groups, local_len, width = tokens.shape
    blocks_each = local_len // SPAN
    reach = -(-LAGS // blocks_each)
    step = 6.0 / (SPAN + 8)
    scale = HD ** (-0.5)

    def joined(own, other, axis):
        return jnp.concatenate(either(first_half, own, other), axis=axis)

    pair_tokens = flipped(tokens, "ctx", 1)
    far_tokens = flipped(tokens, "ctx", 2)
    core, outer = (part % 2, part // 2)
    feature_half = pick(w_feature.reshape(2, -1, w_feature.shape[1]), core, 0)
    feature_half = flipped(feature_half, "shard", 1)
    feature_other = jnp.concatenate(
        either(core == 0, feature_half, flipped(feature_half, "ctx", 1)), axis=0
    )
    smalls = [norm_gain, ffn_gain, memory_gain, memory_rates, persistent]
    small_flat = jnp.concatenate([item.reshape(-1) for item in smalls])
    small_other = flipped(small_flat, "shard", 1)
    small_others = []
    start = 0
    for item in smalls:
        small_others.append(small_other[start : start + item.size].reshape(item.shape))
        start += item.size
    value_other = flipped(after(w_value, feature_half), "shard", 1)

    gain_in_wide = joined(norm_gain, small_others[0], 0).astype(WIDE)
    gain_ffn_wide = joined(ffn_gain, small_others[1], 0).astype(WIDE)
    gain_mem = joined(memory_gain, small_others[2], 1).astype(WIDE)
    rates = joined(memory_rates, small_others[3], 0)
    persist = joined(persistent, small_others[4], 1)
    feature_cols = joined(w_feature, feature_other, 0)
    value_cols = joined(w_value, value_other, 0)
    weights = {}
    local_width = w_qkv.shape[2]
    local_units = feature_cols.shape[1]
    local_heads = local_width // HD
    persist_count = persist.shape[0]

    def scattered(array):
        return lax.psum_scatter(
            array.astype(NARROW), "tp", scatter_dimension=0, tiled=True
        ).astype(WIDE)

    def collected(array):
        return lax.all_gather(array.astype(NARROW), "tp", axis=0, tiled=True)

    def summed_over_ranks(array, kind=WIDE):
        bit = 1
        while bit < ranks:
            array = array.astype(kind)
            array = array.astype(WIDE) + flipped(array, "tp", bit).astype(WIDE)
            bit *= 2
        return array

    own_units = lax.dynamic_slice_in_dim(rates.astype(WIDE), rank * local_units, local_units, 1)
    retain, moment = (own_units[0], own_units[1])
    decays = [jnp.ones_like(retain)]
    for lag in range(1, LAGS):
        decays.append(retain * decays[-1] + moment**lag)

    labels_all = segments.astype(WIDE).reshape(groups, blocks_each, SPAN) + 1.0
    lasts_all = labels_all[:, :, -1]
    late_lasts = after(lasts_all, far_tokens)
    far_lasts = flipped(late_lasts, "ctx", 2)
    lasts_around = jnp.stack(
        [lasts_all, flipped(late_lasts, "ctx", 1), far_lasts, flipped(far_lasts, "ctx", 1)]
    )

    def last_of(index):
        delta, place = divmod(index, blocks_each)
        source = part + delta
        found = pick(lasts_around, jnp.clip(source, 0, parts - 1) ^ part, 0)[:, place]
        return jnp.where(source >= 0, found, 0.0)

    before_all = jnp.stack([last_of(own - 1) for own in range(blocks_each)], axis=1)
    linked_all = []
    for own in range(blocks_each):
        for lag in range(LAGS):
            source = own - 1 - lag
            present = part + source // blocks_each >= 0
            linked_all.append(present & (last_of(source) == last_of(own - 1)))
    linked_all = jnp.stack(linked_all, axis=1).reshape(groups, blocks_each, LAGS)

    def place_of(own, lag):
        return divmod(own - 1 - lag, blocks_each)

    head_of = (jnp.arange(local_width)[:, None] // HD == jnp.arange(local_heads)).astype(WIDE)
    gain_flat = gain_mem.reshape(local_width)

    def head_mean(values):
        return exact_product(values, head_of) / HD

    def head_spread(values):
        return exact_product(values, head_of.T)

    count = groups
    rows = count * local_len
    blocks = count * blocks_each
    part_rows = rows // STREAMS
    part_blocks = blocks // STREAMS

    def own_rows(array):
        sub = array.shape[0] // ranks
        return lax.dynamic_slice_in_dim(array, rank * sub, sub, 0)

    class Stream:
        pass

    def linked(one, square, corner):
        spread = jnp.repeat(one.linked[:, :, LAGS - 2 :: -1], SPAN, axis=2)[:, :, None]
        square = jnp.where(spread, square, jnp.zeros_like(square))
        corner = jnp.where(
            one.linked[:, :, LAGS - 1, None, None], corner, jnp.zeros_like(corner)
        )
        return square, corner

    def packed(square, corner):
        wide = square.shape[-1]
        lanes = corner.transpose(2, 0, 1, 3).reshape(CORNER, -1)
        lanes = jnp.pad(lanes, ((0, 0), (0, wide - lanes.shape[1])))
        return jnp.concatenate([square.reshape(-1, wide), lanes], axis=0)

    def unpacked(array):
        square = array[:-CORNER].reshape(count, blocks_each, SPAN, -1)
        corner = array[-CORNER:, : blocks * CORNER]
        corner = corner.reshape(CORNER, count, blocks_each, CORNER).transpose(1, 2, 0, 3)
        return square, corner

    def begin(one, index):
        def mine(array):
            return array[index * count : (index + 1) * count]

        one.flat = mine(tokens).reshape(rows, width)
        one.upstream_low = mine(out_grad).reshape(rows, width)
        one.labels = mine(labels_all)
        one.lasts = mine(lasts_all)
        one.before = mine(before_all)
        one.linked = mine(linked_all)
        one.keeping = (one.lasts == one.before).astype(WIDE)[:, :, None, None]
        one.writing = (one.labels == one.lasts[:, :, None]).astype(WIDE)[..., None]
        one.reading = (one.labels == one.before[:, :, None]).astype(WIDE)

        def features_of(piece):
            low = norm_rows(piece.astype(WIDE), gain_in_wide)[0].astype(NARROW)
            return low, matmul(low.reshape(rows, width), feature_cols)

        def shaped(values):
            return values.reshape(count, blocks_each, SPAN, local_units)

        low, preact = features_of(mine(tokens))
        one.preact = lax.optimization_barrier(preact)
        one.input_low = low.reshape(rows, width)
        one.features = jax.nn.silu(one.preact).astype(NARROW)
        squares = jnp.sum(jnp.square(one.features.astype(WIDE)), axis=1)
        one.key_scale = lax.rsqrt(summed_over_ranks(squares) + EPSILON)
        far, pair, one.features, one.key_scale = lax.optimization_barrier(
            (mine(far_tokens), mine(pair_tokens), one.features, one.key_scale)
        )
        close = [pair, flipped(far, "ctx", 1)]
        one.around = {0: shaped(one.features)}
        for delta, piece in (
            (-1, jnp.where(odd_part, close[0], close[1])),
            (1, jnp.where(odd_part, close[1], close[0])),
            (2, far),
        ):
            one.around[delta] = shaped(jax.nn.silu(features_of(piece)[1]).astype(NARROW))
        one.around[-2] = one.around[2]
        one.targets = matmul(one.input_low, value_cols).reshape(
            count, blocks_each, SPAN, local_width
        )
        weighted = [(one.around[0].astype(WIDE) * decay).astype(NARROW) for decay in decays]
        products = []
        corners = []
        for own in range(blocks_each):
            row = []
            for lag in range(LAGS - 1, -1, -1):
                delta, place = place_of(own, lag)
                near, past = weighted[lag][:, own], one.around[delta][:, place]
                if lag == LAGS - 1:
                    near, past = near[:, :CORNER], past[:, SPAN - CORNER :]
                    corners.append(batched("sth,suh->stu", near, past))
                else:
                    row.append(batched("sth,suh->stu", near, past))
            products.append(jnp.concatenate(row, axis=2))
        one.products = packed(
            jnp.stack(products, axis=1).astype(NARROW), jnp.stack(corners, axis=1).astype(NARROW)
        )
        one.mixing = lax.psum(one.products, "tp")

    def span_of(own):
        start = (reach * blocks_each - LAGS + own) * SPAN
        return slice(start, start + LAGS * SPAN)

    def remember(one):
        square, corner = linked(one, *unpacked(one.mixing))
        corner = jnp.pad(
            corner, ((0, 0), (0, 0), (0, SPAN - CORNER), (SPAN - CORNER, 0))
        )
        one.mixing = jnp.concatenate([corner, square], axis=3)
        one.scales = one.key_scale.reshape(count, blocks_each, SPAN, 1)
        halos = [
            jnp.zeros((count, blocks_each * SPAN, local_width), NARROW) for _ in range(reach)
        ]
        pending = {}
        for turn in range(parts):
            for hop in range(1, reach + 1):
                if (turn - hop, hop) in pending:
                    halos[reach - hop] = halos[reach - hop] + pending[(turn - hop, hop)]
            known = jnp.concatenate(halos, axis=1)
            recalls = []
            errors = []
            for own in range(blocks_each):
                total = batched("stu,sud->std", one.mixing[:, own], known[:, span_of(own)])
                recall = -step * one.scales[:, own] * total
                error = one.writing[:, own] * (
                    one.keeping[:, own] * recall - one.targets[:, own]
                )
                recalls.append(recall)
                errors.append(error)
                known = jnp.concatenate(
                    [known, (one.scales[:, own] * error).astype(NARROW)], axis=1
                )
            for hop in range(1, reach + 1):
                if turn + hop < parts:
                    pending[(turn, hop)] = passed_along(
                        known[:, reach * blocks_each * SPAN :], "ctx", [(turn, turn + hop)]
                    )
        one.known = known
        one.recall = jnp.stack(recalls, 1)
        one.errors = jnp.stack(errors, 1)
        masked = (one.reading[..., None] * one.recall).reshape(rows, local_width)
        one.head_factor = head_spread(lax.rsqrt(head_mean(masked * masked) + EPSILON))
        one.head_unit = masked * one.head_factor
        retrieved = (one.head_unit * gain_flat).astype(NARROW)
        one.retrieved_full = lax.all_gather(retrieved, "tp", axis=1, tiled=True)

    def attend(one):
        def projected(values, weight):
            return matmul(values, weight).astype(NARROW)

        labels = one.labels.reshape(part_blocks, SPAN)
        reading = one.reading.reshape(part_blocks, SPAN)
        one.operands = (
            projected(one.input_low, query_w),
            projected(one.retrieved_full, key_w),
            projected(one.input_low, key_w),
            projected(one.retrieved_full, value_w),
            projected(one.input_low, value_w),
            fixed_keys,
            fixed_values,
            labels[:, :, None],
            labels[:, None, :],
            reading[:, None, :],
        )
        one.attended = attention(*one.operands)
        one.residual = own_rows(one.flat).astype(WIDE)
        one.branch = scattered(matmul(one.attended, weights["out"]))

    def middle(one):
        if one is not streams[0]:
            one.branch = after(one.branch, streams[0].mid_own)
        one.hidden = one.residual + one.branch
        normed_mid, one.unit_mid, one.factor_mid = norm_rows(one.hidden, gain_ffn_wide)
        one.mid_own = normed_mid.astype(NARROW)
        one.mid_low = collected(one.mid_own)

    def feed(one):
        gate = matmul(one.mid_low, weights["gate"])
        upper = matmul(one.mid_low, weights["up"])
        one.activ = (jax.nn.silu(gate) * upper).astype(NARROW)
        grad_act = by_rows(one.upstream_low, weights["down"])
        one.grad_gate = (grad_act * upper * silu_slope(gate)).astype(NARROW)
        one.grad_upper = (grad_act * jax.nn.silu(gate)).astype(NARROW)
        one.grad_mid = scattered(
            by_rows(one.grad_gate, weights["gate"]) + by_rows(one.grad_upper, weights["up"])
        )

    def middle_back(one):
        if one is not streams[0]:
            one.grad_mid = after(one.grad_mid, streams[0].grad_hidden)
        grad_mid = one.grad_mid
        one.grad_gain_ffn = jnp.sum(grad_mid * one.unit_mid, axis=0)
        upstream = own_rows(one.upstream_low).astype(WIDE)
        one.grad_hidden = upstream + norm_back(
            grad_mid, one.unit_mid, one.factor_mid, gain_ffn_wide
        )
        one.grad_mixed = collected(one.grad_hidden)

    def branch_part(one):
        activ = after(one.activ, last_stream.partial)
        return matmul(activ, weights["down"]).astype(NARROW)

    def rank_major(array):
        array = array.reshape(STREAMS, ranks, -1, width)
        return array.transpose(1, 0, 2, 3).reshape(-1, width)

    def stream_major(array):
        array = array.reshape(ranks, STREAMS, -1, width)
        return array.transpose(1, 0, 2, 3).reshape(-1, width)

    def finish_output(one):
        own = jnp.concatenate([item.hidden + item.branch for item in streams], axis=0)
        one.output = collected(after(own, one.grad_mixing))

    def attend_back(one):
        grad_attended = by_rows(one.grad_mixed, weights["out"]).astype(NARROW)
        (
            one.grad_queries,
            one.key_memory,
            one.key_token,
            one.value_memory,
            one.value_token,
            one.key_fixed,
            one.value_fixed,
        ) = attention_back(*one.operands, grad_attended)
        partial = by_rows(one.key_memory, key_w) + by_rows(one.value_memory, value_w)
        one.partial = partial.astype(NARROW)
        one.grad_retrieved = lax.psum_scatter(one.partial, "tp", scatter_dimension=1, tiled=True)

    def heads_back(one):
        grad_heads = one.grad_retrieved.astype(WIDE)
        one.grad_gain_memory = jnp.sum(grad_heads * one.head_unit, axis=0)
        inner = grad_heads * gain_flat
        grad_masked = one.head_factor * (
            inner - one.head_unit * head_spread(head_mean(inner * one.head_unit))
        )
        one.grad_read = one.reading[..., None] * grad_masked.reshape(
            count, blocks_each, SPAN, local_width
        )

    def remember_back(one):
        later = [0.0] * blocks_each
        pending = {}
        branches = [item.branch for item in streams]
        for turn in range(parts):
            if turn == parts // 2:
                later, branches[0] = lax.optimization_barrier((later, branches[0]))
            for hop in range(1, reach + 1):
                if (turn - hop, hop) in pending:
                    arrived = pending[(turn - hop, hop)].astype(WIDE)
                    for own in range(blocks_each):
                        later[own] = later[own] + arrived[:, own * SPAN : (own + 1) * SPAN]
            known = [0.0] * (reach * blocks_each) + later
            grad_errors = [None] * blocks_each
            grad_recalls = [None] * blocks_each
            raws = [None] * blocks_each
            for own in range(blocks_each - 1, -1, -1):
                grad_scaled = -step * known[reach * blocks_each + own]
                grad_error = one.scales[:, own] * grad_scaled
                grad_recall = (
                    one.grad_read[:, own] + one.writing[:, own] * one.keeping[:, own] * grad_error
                )
                grad_errors[own] = jnp.broadcast_to(grad_error, grad_recall.shape)
                grad_recalls[own] = grad_recall
                raws[own] = (one.scales[:, own] * grad_recall).astype(NARROW)
                carried = batched("stu,std->sud", one.mixing[:, own], raws[own])
                for index in range(LAGS):
                    place = reach * blocks_each - LAGS + own + index
                    known[place] = (
                        known[place] + carried[:, index * SPAN : (index + 1) * SPAN]
                    )
            for hop in range(1, reach + 1):
                place = parts - 1 - turn
                if place - hop >= 0:
                    start = (reach - hop) * blocks_each
                    sent = jnp.concatenate(known[start : start + blocks_each], axis=1)
                    pending[(turn, hop)] = passed_along(
                        sent.astype(NARROW), "ctx", [(place, place - hop)]
                    )
        grad_errors = jnp.stack(grad_errors, 1)
        grad_recalls = jnp.stack(grad_recalls, 1)
        one.grad_targets = (-one.writing * grad_errors).astype(NARROW).reshape(rows, local_width)
        scale_part = jnp.sum(grad_recalls * one.recall + one.errors * grad_errors, axis=3)
        one.scale_sum = summed_over_ranks(scale_part.reshape(rows))
        grad_mixing = []
        for own in range(blocks_each):
            grad_mixing.append(
                -step * batched("std,sud->stu", raws[own], one.known[:, span_of(own)])
            )
        grad_mixing = jnp.stack(grad_mixing, 1)
        square, corner = linked(
            one, grad_mixing[..., SPAN:], grad_mixing[:, :, :CORNER, SPAN - CORNER : SPAN]
        )
        grad_mixing = packed(square.astype(NARROW), corner.astype(NARROW))
        grad_mixing, branches = lax.optimization_barrier((grad_mixing, branches))
        for item, branch in zip(streams, branches):
            item.branch = branch
        one.packed_back = grad_mixing
        one.grad_mixing = lax.psum(grad_mixing, "tp")

    def features_back(one):
        square, corner = unpacked(one.grad_mixing)

        def column(own, lag):
            if lag == LAGS - 1:
                return corner[:, own]
            start = (LAGS - 2 - lag) * SPAN
            return square[:, own, :, start : start + SPAN]

        needed = {}
        for hop in range(1, reach + 1):
            sends = [(source, source - hop) for source in range(hop, parts)]
            for last_lag in (False, True):
                pairs = [
                    (own, lag)
                    for own in range(blocks_each)
                    for lag in range(LAGS)
                    if place_of(own, lag)[0] == -hop and (lag == LAGS - 1) == last_lag
                ]
                if not pairs:
                    continue
                moved = passed_along(
                    jnp.stack([column(own, lag) for own, lag in pairs], axis=1), "ctx", sends
                )
                for place, (own, lag) in enumerate(pairs):
                    needed[(hop * blocks_each + own, lag)] = moved[:, place]
        for own in range(blocks_each):
            for lag in range(LAGS):
                needed[(own, lag)] = column(own, lag)
        grad_features = []
        one.grad_decays = [0.0] * LAGS
        rest = SPAN - CORNER
        for own in range(blocks_each):
            total = 0.0
            for lag in range(LAGS):
                own_features = one.around[0][:, own].astype(WIDE)
                delta, place = place_of(own, lag)
                past = one.around[delta][:, place]
                later = own + 1 + lag
                delta, place = divmod(later, blocks_each)
                future = one.around[delta][:, place]
                if lag == LAGS - 1:
                    own_features, past, future = (
                        own_features[:, :CORNER],
                        past[:, rest:],
                        future[:, :CORNER],
                    )
                from_reads = batched("stu,suh->sth", needed[(own, lag)], past)
                one.grad_decays[lag] = one.grad_decays[lag] + jnp.sum(
                    own_features * from_reads, axis=(0, 1)
                )
                from_writes = batched("stu,sth->suh", needed[(later, lag)], future)
                if lag == LAGS - 1:
                    from_reads = jnp.pad(from_reads, ((0, 0), (0, rest), (0, 0)))
                    from_writes = jnp.pad(from_writes, ((0, 0), (rest, 0), (0, 0)))
                total = total + decays[lag] * (from_reads + from_writes)
            if own == 0:
                total, one.output = lax.optimization_barrier((total, one.output))
            grad_features.append(total)
        grad_features = jnp.stack(grad_features, 1).reshape(rows, local_units)
        grad_features = grad_features - (one.key_scale * one.key_scale * one.scale_sum)[
            :, None
        ] * one.features.astype(WIDE)
        one.grad_pre = (grad_features * silu_slope(one.preact)).astype(NARROW)

    def inputs_back(one):
        one.grad_input = (one.early + by_rows(one.grad_pre, feature_cols)).astype(NARROW)

    def input_early(one):
        targets = after(one.grad_targets, one.packed_back)
        one.early = one.early + by_rows(targets, value_cols)

    def tokens_back(one):
        grad_input = one.grad_input
        _, unit_in, factor_in = norm_rows(one.residual, gain_in_wide)
        one.grad_gain_in = jnp.sum(grad_input * unit_in, axis=0)
        grad_own = one.grad_hidden + norm_back(grad_input, unit_in, factor_in, gain_in_wide)
        one.grad_tokens = stream_major(collected(grad_own)).astype(WIDE)

    whole = Stream()
    streams = [Stream() for _ in range(STREAMS)]

    def over(function):
        total = function(streams[0])
        for one in streams[1:]:
            total = total + function(one)
        return total

    def every(stage):
        for one in streams:
            stage(one)

    class Reduction:
        def __init__(self, array, by_row):
            array = array.astype(NARROW)
            *self.lead, self.high, self.wide = array.shape
            self.by_row = by_row
            self.axis = len(self.lead)
            if by_row:
                array = array.reshape(*self.lead, 2, 2, 2, self.high // 8, self.wide)
            else:
                array = array.reshape(2, 2, self.high // 4, self.wide)
            self.array = array
            self.exchange(core, self.axis + 1 if by_row else 0, "ctx", 1)

        def exchange(self, index, axis, over_axis, bit):
            own, other = (pick(self.array, place, axis) for place in (index, 1 - index))
            self.add(own, flipped(other, over_axis, bit))

        def add(self, own, arrived):
            self.array = (own.astype(WIDE) + arrived.astype(WIDE)).astype(NARROW)

        def across(self):
            if self.by_row:
                self.exchange(half_index, self.axis, "shard", 1)
                return
            half = self.wide // 2
            own, other = (
                lax.dynamic_slice_in_dim(self.array, place * half, half, 2)
                for place in (half_index, 1 - half_index)
            )
            self.add(own, flipped(other, "shard", 1))

        def apart(self):
            self.exchange(outer, self.axis if self.by_row else 0, "ctx", 2)

        def together(self):
            pair = either(outer == 0, self.array, flipped(self.array, "ctx", 2))
            self.array = jnp.stack(pair, axis=self.axis if self.by_row else 0)

        def result(self):
            pair = either(core == 0, self.array, flipped(self.array, "ctx", 1))
            array = jnp.stack(pair, axis=self.axis if self.by_row else 0).astype(WIDE)
            if self.by_row:
                return array.reshape(*self.lead, self.high // 2, self.wide)
            return array.reshape(self.high, self.wide // 2)

    def tied(one, names, *reductions):
        held = [getattr(one, name) for name in names]
        held, arrays = lax.optimization_barrier((held, [item.array for item in reductions]))
        for name, value in zip(names, held):
            setattr(one, name, value)
        for item, array in zip(reductions, arrays):
            item.array = array

    class Holder:
        def __init__(self, array):
            self.array = array

    def fetched(one, names, start, *arrays):
        holders = [Holder(flipped(after(item, start), "shard", 1)) for item in arrays]
        tied(one, names, *holders)
        return [holder.array for holder in holders]

    def merged(name):
        setattr(
            whole, name, jnp.concatenate([getattr(one, name) for one in streams], axis=0)
        )

    begin(whole, 0)
    qkv_fetch = Holder(flipped(after(w_qkv, whole.products), "shard", 1))
    next_features = Holder(whole.around[1])
    tied(whole, ["mixing"], qkv_fetch, next_features)
    qkv_other = qkv_fetch.array
    whole.around[1] = next_features.array
    qkv_cols = joined(w_qkv, qkv_other, 1)
    query_w = qkv_cols[0]
    key_w = qkv_cols[1]
    value_w = qkv_cols[2]
    fixed_keys = matmul(persist, key_w).astype(NARROW)
    fixed_values = matmul(persist, value_w).astype(NARROW)
    remember(whole)
    out_other, down_other = fetched(whole, ["retrieved_full"], whole.recall, w_out, w_down)
    weights["out"] = joined(w_out, out_other, 1)
    weights["down"] = joined(w_down, down_other, 1)
    for index, one in enumerate(streams):
        for name in ("flat", "upstream_low", "input_low", "retrieved_full", "labels", "reading"):
            array = getattr(whole, name)
            size = array.shape[0] // STREAMS
            setattr(one, name, array[index * size : (index + 1) * size])
        attend(one)
    first_stream, last_stream = streams[0], streams[-1]
    (gate_other,) = fetched(last_stream, ["branch"], first_stream.attended, w_gate_up[0])
    weights["gate"] = joined(w_gate_up[0], gate_other, 0)
    every(middle)
    (up_other,) = fetched(first_stream, ["mid_low"], first_stream.hidden, w_gate_up[1])
    weights["up"] = joined(w_gate_up[1], up_other, 0)
    first_stream.mid_low = after(first_stream.mid_low, last_stream.hidden)
    every(feed)
    first_stream.grad_mid = after(first_stream.grad_mid, last_stream.mid_low)
    feed_reductions = [
        Reduction(over(lambda one: over_rows(one.activ, one.upstream_low)), False),
        Reduction(
            jnp.stack(
                [
                    over(lambda one: over_rows(one.mid_low, one.grad_gate)).astype(NARROW),
                    over(lambda one: over_rows(one.mid_low, one.grad_upper)).astype(NARROW),
                ]
            ),
            True,
        ),
    ]
    every(middle_back)
    first_stream.grad_mixed = after(first_stream.grad_mixed, last_stream.grad_mid)
    for item in feed_reductions:
        item.across()
    attend_back(first_stream)
    tied(last_stream, ["grad_mixed"], *feed_reductions, Holder(first_stream.partial))
    attend_back(last_stream)
    for name in (
        "grad_retrieved",
        "grad_queries",
        "key_token",
        "value_token",
        "key_memory",
        "value_memory",
    ):
        merged(name)
    persist_wide = persist.astype(WIDE)
    key_fixed = over(lambda one: one.key_fixed)
    value_fixed = over(lambda one: one.value_fixed)
    grad_query_w = over_rows(whole.input_low, whole.grad_queries)
    grad_key_w = (
        over_rows(whole.input_low, whole.key_token)
        + over_rows(whole.retrieved_full, whole.key_memory)
        + exact_product(persist_wide.T, key_fixed)
    )
    grad_value_proj = (
        over_rows(whole.input_low, whole.value_token)
        + over_rows(whole.retrieved_full, whole.value_memory)
        + exact_product(persist_wide.T, value_fixed)
    )
    mix_reductions = [
        Reduction(over(lambda one: over_rows(one.attended, one.grad_mixed)), False),
        Reduction(
            jnp.stack(
                [item.astype(NARROW) for item in (grad_query_w, grad_key_w, grad_value_proj)]
            ),
            True,
        ),
    ]
    grad_persist = exact_product(key_fixed, key_w.astype(WIDE).T) + exact_product(
        value_fixed, value_w.astype(WIDE).T
    )
    for item in feed_reductions:
        item.apart()
    early = Holder(
        by_rows(whole.grad_queries, query_w)
        + by_rows(whole.key_token, key_w)
        + by_rows(whole.value_token, value_w)
    )
    branch_parts = [Holder(branch_part(one)) for one in streams]
    tied(
        whole,
        ["grad_retrieved"],
        *feed_reductions,
        *mix_reductions,
        early,
        *branch_parts,
    )
    whole.early = early.array
    for one, part_sum in zip(streams, branch_parts):
        one.branch = scattered(part_sum.array)
    heads_back(whole)
    remember_back(whole)
    persist_sum = Holder(summed_over_ranks(after(grad_persist, whole.packed_back), NARROW))
    input_early(whole)
    grad_targets = after(whole.grad_targets, whole.packed_back)
    target_reduction = Reduction(over_rows(whole.input_low, grad_targets), True)
    for item in mix_reductions:
        item.array = after(item.array, whole.packed_back)
        item.across()
    tied(
        whole,
        ["grad_mixing", "scale_sum", "early"],
        *mix_reductions,
        target_reduction,
        persist_sum,
    )
    finish_output(whole)
    features_back(whole)
    inputs_back(whole)
    whole.grad_input_low = rank_major(whole.grad_input)
    whole.grad_input = scattered(whole.grad_input_low)
    merged("residual")
    merged("grad_hidden")

    grad_decays = whole.grad_decays
    grad_retain = 0.0
    grad_moment = 0.0
    retain_slope = jnp.zeros_like(retain)
    for lag in range(1, LAGS):
        retain_slope = retain * retain_slope + decays[lag - 1]
        moment_slope = 0.0
        for power in range(1, lag + 1):
            moment_slope = moment_slope + power * retain ** (lag - power) * moment ** (power - 1)
        grad_retain = grad_retain + retain_slope * grad_decays[lag]
        grad_moment = grad_moment + moment_slope * grad_decays[lag]
    grad_rates = jnp.stack([grad_retain, grad_moment])

    def summed(pieces):
        small = jnp.concatenate([piece.reshape(-1) for piece in pieces])
        for axis, bit in (("ctx", 1), ("shard", 1), ("ctx", 2)):
            small = small + flipped(small, axis, bit)
        return small

    small = Holder(summed([persist_sum.array, whole.grad_gain_memory, grad_rates]))
    feature_reduction = Reduction(over_rows(whole.input_low, whole.grad_pre), True)
    late_reductions = [feature_reduction, target_reduction]
    for item in feed_reductions:
        item.array = after(item.array, whole.grad_input_low)
        item.together()
    for item in mix_reductions:
        item.apart()
    for item in late_reductions:
        item.across()
    tied(
        whole,
        ["grad_input"],
        small,
        *feed_reductions,
        *mix_reductions,
        *late_reductions,
    )
    tokens_back(whole)
    for item in mix_reductions:
        item.together()
    for item in late_reductions:
        item.apart()
        item.together()
    gains = summed([whole.grad_gain_in, over(lambda one: one.grad_gain_ffn)])
    gain_in_sum, gain_ffn_sum = summed_over_ranks(gains).reshape(2, width)
    cut = persist_sum.array.size
    middle_cut = cut + local_width
    grad_persist = small.array[:cut].reshape(persist_count, width)
    grad_gain_memory = small.array[cut:middle_cut].reshape(local_heads, HD)
    grad_rates = small.array[middle_cut:].reshape(2, local_units)
    grad_down, grad_gate_up = [item.result() for item in feed_reductions]
    grad_out_rows, grad_qkv = [item.result() for item in mix_reductions]
    grad_feature_w, grad_target_w = [item.result() for item in late_reductions]

    def own_half(array, axis):
        size = array.shape[axis] // 2
        return lax.dynamic_slice_in_dim(array, half_index * size, size, axis)

    return (
        stream_major(whole.output).reshape(tokens.shape),
        whole.grad_tokens.reshape(tokens.shape),
        own_half(gain_in_sum, 0),
        own_half(gain_ffn_sum, 0),
        own_half(grad_gain_memory, 1),
        own_half(grad_rates, 0),
        own_half(grad_persist, 1),
        grad_qkv,
        grad_out_rows,
        grad_target_w,
        grad_feature_w,
        grad_gate_up,
        grad_down,
    )


def solution(mesh):
    placed = (
        P("shard", "ctx", None),
        P("shard", "ctx"),
        P("shard"),
        P("shard"),
        P("tp", "shard"),
        P("shard", None),
        P(None, "shard"),
        P(None, "shard", "tp"),
        P("tp", "shard"),
        P("shard", "tp"),
        P("shard", "tp"),
        P(None, "shard", "tp"),
        P("tp", "shard"),
        P("shard", "ctx", None),
    )
    return jax.shard_map(
        on_device,
        mesh=mesh,
        in_specs=placed,
        out_specs=(
            P("shard", "ctx", None),
            P("shard", "ctx", None),
            P("shard"),
            P("shard"),
            P("tp", "shard"),
            P("shard", "tp"),
            P(None, "shard"),
            P(None, "shard", "tp"),
            P("tp", "shard"),
            P("shard", "tp"),
            P("shard", "tp"),
            P(None, "shard", "tp"),
            P("tp", "shard"),
        ),
        check_vma=False,
    )
```

```python
import jax
import jax.numpy as jnp
from jax import lax
from jax.experimental import pallas as pl
from jax.experimental.pallas import tpu as pltpu
from jax.sharding import PartitionSpec as P

HD = 96
SPAN = 256
LANES = 128
LIMIT = 800
LAGS = (LIMIT + SPAN - 2) // SPAN
CORNER = LIMIT - (LAGS - 1) * SPAN
STREAMS = 2


EPSILON = 1e-06
MASKED = -1e30
WIDE = jnp.float32
NARROW = jnp.bfloat16


def passed_along(value, axis, pairs):
    return lax.ppermute(value, axis, pairs)


def flipped(value, axis, bit):
    return lax.ppermute(value, axis, [(i, i ^ bit) for i in range(lax.axis_size(axis))])


def either(first, one, other):
    return jnp.where(first, one, other), jnp.where(first, other, one)


def pick(array, place, axis):
    return lax.dynamic_index_in_dim(array, place, axis, keepdims=False)


def after(value, *others):
    return lax.optimization_barrier((value, *others))[0]


def norm_rows(values, gain):
    factor = lax.rsqrt(jnp.mean(values * values, axis=-1, keepdims=True) + EPSILON)
    normed = values * factor
    return (normed * gain, normed, factor)


def norm_back(upstream, normed, factor, gain):
    inner = upstream * gain
    return factor * (inner - normed * jnp.mean(inner * normed, axis=-1, keepdims=True))


def silu_slope(values):
    sigmoid = jax.nn.sigmoid(values)
    return sigmoid * (1.0 + values * (1.0 - sigmoid))


def matmul(left, right):
    return jnp.dot(left, right, preferred_element_type=WIDE)


def over_rows(left, right):
    return lax.dot_general(left, right, (((0,), (0,)), ((), ())), preferred_element_type=WIDE)


def by_rows(left, right):
    return lax.dot_general(left, right, (((1,), (1,)), ((), ())), preferred_element_type=WIDE)


def exact_product(left, right):
    return jnp.dot(left, right, precision=lax.Precision.HIGHEST, preferred_element_type=WIDE)


def batched(spec, left, right):
    return jnp.einsum(spec, left, right, preferred_element_type=WIDE)


def windows(width):
    found = []
    for start in range(0, width, HD):
        low = start // LANES * LANES
        high = min(-(-(start + HD) // LANES) * LANES, width)
        found.append((low, high, start - low))
    return found


def masks_of(label_col, label_row, read_row):
    rows = lax.broadcasted_iota(jnp.int32, (SPAN, SPAN), 0)
    columns = lax.broadcasted_iota(jnp.int32, (SPAN, SPAN), 1)
    own = (rows >= columns) & (label_col == label_row)
    return own & (read_row > 0.5), own


def head_probs(query, keys, visible_memory, visible_own):
    scale = HD ** (-0.5)
    scores = [by_rows(query, key) * scale for key in keys]
    scores[1] = jnp.where(visible_memory, scores[1], MASKED)
    scores[2] = jnp.where(visible_own, scores[2], MASKED)
    highest = jnp.max(scores[0], axis=-1, keepdims=True)
    for item in scores[1:]:
        highest = jnp.maximum(highest, jnp.max(item, axis=-1, keepdims=True))
    raised = [jnp.exp(item - highest) for item in scores]
    totals = sum(jnp.sum(item, axis=-1, keepdims=True) for item in raised)
    inverse = 1.0 / totals
    return [item * inverse for item in raised]


def attention_kernel(
    query, key_memory, key_own, value_memory, value_own, key_fixed, value_fixed,
    label_col, label_row, read_row, out, total,
):
    visible_memory, visible_own = masks_of(label_col[0], label_row[0], read_row[0])
    total[...] = jnp.zeros_like(total)
    for low, high, offset in windows(query.shape[1]):
        lanes = lax.broadcasted_iota(jnp.int32, (SPAN, high - low), 1)
        inside = (lanes >= offset) & (lanes < offset + HD)
        mine = jnp.where(inside, query[:, low:high], jnp.zeros((), NARROW))
        keys = [item[:, low:high] for item in (key_fixed, key_memory, key_own)]
        values = [item[:, low:high] for item in (value_fixed, value_memory, value_own)]
        probs = head_probs(mine, keys, visible_memory, visible_own)
        result = sum(matmul(item.astype(NARROW), value) for item, value in zip(probs, values))
        total[:, low:high] += jnp.where(inside, result, 0.0)
    out[...] = total[...].astype(NARROW)


def attention_back_kernel(
    query, key_memory, key_own, value_memory, value_own, key_fixed, value_fixed,
    label_col, label_row, read_row, upstream,
    grad_query, grad_key_memory, grad_key_own, grad_value_memory, grad_value_own,
    grad_key_fixed, grad_value_fixed, *totals,
):
    scale = HD ** (-0.5)
    visible_memory, visible_own = masks_of(label_col[0], label_row[0], read_row[0])
    for total in totals:
        total[...] = jnp.zeros_like(total)

    @pl.when(pl.program_id(0) == 0)
    def _():
        grad_key_fixed[...] = jnp.zeros_like(grad_key_fixed)
        grad_value_fixed[...] = jnp.zeros_like(grad_value_fixed)

    key_sums = (grad_key_fixed, totals[1], totals[2])
    value_sums = (grad_value_fixed, totals[3], totals[4])
    for low, high, offset in windows(query.shape[1]):
        lanes = lax.broadcasted_iota(jnp.int32, (SPAN, high - low), 1)
        inside = (lanes >= offset) & (lanes < offset + HD)
        mine = jnp.where(inside, query[:, low:high], jnp.zeros((), NARROW))
        above = jnp.where(inside, upstream[:, low:high], jnp.zeros((), NARROW))
        keys = [item[:, low:high] for item in (key_fixed, key_memory, key_own)]
        values = [item[:, low:high] for item in (value_fixed, value_memory, value_own)]
        probs = head_probs(mine, keys, visible_memory, visible_own)
        grads = [by_rows(above, value) for value in values]
        inner = sum(
            jnp.sum(grad * item, axis=-1, keepdims=True) for grad, item in zip(grads, probs)
        )
        result = 0.0
        for index in range(3):
            slope = (probs[index] * (grads[index] - inner)).astype(NARROW)
            result = result + matmul(slope, keys[index])
            key_sums[index][:, low:high] += over_rows(slope, mine) * scale
            value_sums[index][:, low:high] += over_rows(probs[index].astype(NARROW), above)
        totals[0][:, low:high] += jnp.where(inside, result, 0.0) * scale
    places = (grad_query, grad_key_memory, grad_key_own, grad_value_memory, grad_value_own)
    for place, total in zip(places, totals):
        place[...] = total[...].astype(NARROW)


def attention_specs(blocks, width, fixed_count):
    rows = pl.BlockSpec((SPAN, width), lambda block: (block, 0))
    fixed = pl.BlockSpec((fixed_count, width), lambda block: (0, 0))
    col = pl.BlockSpec((1, SPAN, 1), lambda block: (block, 0, 0))
    row = pl.BlockSpec((1, 1, SPAN), lambda block: (block, 0, 0))
    return rows, fixed, [rows] * 5 + [fixed] * 2 + [col, row, row]


def attention(*operands):
    blocks, width, fixed_count = (operands[7].shape[0], operands[0].shape[1], operands[5].shape[0])
    rows, _, specs = attention_specs(blocks, width, fixed_count)
    pairs = blocks * SPAN * (2 * SPAN + fixed_count)
    return pl.pallas_call(
        attention_kernel,
        grid=(blocks,),
        in_specs=specs,
        out_specs=rows,
        out_shape=jax.ShapeDtypeStruct((blocks * SPAN, width), NARROW),
        scratch_shapes=[pltpu.VMEM((SPAN, width), WIDE)],
        cost_estimate=pl.CostEstimate(
            flops=16 * pairs * width,
            bytes_accessed=12 * blocks * SPAN * width,
            transcendentals=pairs * width // HD,
        ),
    )(*operands)


def attention_back(*operands):
    blocks, width, fixed_count = (operands[7].shape[0], operands[0].shape[1], operands[5].shape[0])
    rows, fixed, specs = attention_specs(blocks, width, fixed_count)
    pairs = blocks * SPAN * (2 * SPAN + fixed_count)
    return pl.pallas_call(
        attention_back_kernel,
        grid=(blocks,),
        in_specs=specs + [rows],
        out_specs=[rows] * 5 + [fixed] * 2,
        out_shape=[jax.ShapeDtypeStruct((blocks * SPAN, width), NARROW)] * 5
        + [jax.ShapeDtypeStruct((fixed_count, width), WIDE)] * 2,
        scratch_shapes=[pltpu.VMEM((SPAN, width), WIDE)] * 5,
        cost_estimate=pl.CostEstimate(
            flops=40 * pairs * width,
            bytes_accessed=24 * blocks * SPAN * width,
            transcendentals=pairs * width // HD,
        ),
    )(*operands)


def on_device(
    tokens,
    segments,
    norm_gain,
    ffn_gain,
    memory_gain,
    memory_rates,
    persistent,
    w_qkv,
    w_out,
    w_value,
    w_feature,
    w_gate_up,
    w_down,
    out_grad,
):
    parts, ranks = (lax.axis_size("ctx"), lax.axis_size("tp"))
    part, rank = (lax.axis_index("ctx"), lax.axis_index("tp"))
    half_index = lax.axis_index("shard")
    first_half = half_index == 0
    odd_part = part % 2 == 1
    groups, local_len, width = tokens.shape
    blocks_each = local_len // SPAN
    reach = -(-LAGS // blocks_each)
    step = 6.0 / (SPAN + 8)
    scale = HD ** (-0.5)

    def joined(own, other, axis):
        return jnp.concatenate(either(first_half, own, other), axis=axis)

    pair_tokens = flipped(tokens, "ctx", 1)
    far_tokens = flipped(tokens, "ctx", 2)
    core, outer = (part % 2, part // 2)
    feature_half = pick(w_feature.reshape(2, -1, w_feature.shape[1]), core, 0)
    feature_half = flipped(feature_half, "shard", 1)
    feature_other = jnp.concatenate(
        either(core == 0, feature_half, flipped(feature_half, "ctx", 1)), axis=0
    )
    smalls = [norm_gain, ffn_gain, memory_gain, memory_rates, persistent]
    small_flat = jnp.concatenate([item.reshape(-1) for item in smalls])
    small_other = flipped(small_flat, "shard", 1)
    small_others = []
    start = 0
    for item in smalls:
        small_others.append(small_other[start : start + item.size].reshape(item.shape))
        start += item.size
    value_other = flipped(after(w_value, feature_half), "shard", 1)

    gain_in_wide = joined(norm_gain, small_others[0], 0).astype(WIDE)
    gain_ffn_wide = joined(ffn_gain, small_others[1], 0).astype(WIDE)
    gain_mem = joined(memory_gain, small_others[2], 1).astype(WIDE)
    rates = joined(memory_rates, small_others[3], 0)
    persist = joined(persistent, small_others[4], 1)
    feature_cols = joined(w_feature, feature_other, 0)
    value_cols = joined(w_value, value_other, 0)
    weights = {}
    local_width = w_qkv.shape[2]
    local_units = feature_cols.shape[1]
    local_heads = local_width // HD
    persist_count = persist.shape[0]

    def scattered(array):
        return lax.psum_scatter(
            array.astype(NARROW), "tp", scatter_dimension=0, tiled=True
        ).astype(WIDE)

    def collected(array):
        return lax.all_gather(array.astype(NARROW), "tp", axis=0, tiled=True)

    def summed_over_ranks(array, kind=WIDE):
        bit = 1
        while bit < ranks:
            array = array.astype(kind)
            array = array.astype(WIDE) + flipped(array, "tp", bit).astype(WIDE)
            bit *= 2
        return array

    own_units = lax.dynamic_slice_in_dim(rates.astype(WIDE), rank * local_units, local_units, 1)
    retain, moment = (own_units[0], own_units[1])
    decays = [jnp.ones_like(retain)]
    for lag in range(1, LAGS):
        decays.append(retain * decays[-1] + moment**lag)

    labels_all = segments.astype(WIDE).reshape(groups, blocks_each, SPAN) + 1.0
    lasts_all = labels_all[:, :, -1]
    late_lasts = after(lasts_all, far_tokens)
    far_lasts = flipped(late_lasts, "ctx", 2)
    lasts_around = jnp.stack(
        [lasts_all, flipped(late_lasts, "ctx", 1), far_lasts, flipped(far_lasts, "ctx", 1)]
    )

    def last_of(index):
        delta, place = divmod(index, blocks_each)
        source = part + delta
        found = pick(lasts_around, jnp.clip(source, 0, parts - 1) ^ part, 0)[:, place]
        return jnp.where(source >= 0, found, 0.0)

    before_all = jnp.stack([last_of(own - 1) for own in range(blocks_each)], axis=1)
    linked_all = []
    for own in range(blocks_each):
        for lag in range(LAGS):
            source = own - 1 - lag
            present = part + source // blocks_each >= 0
            linked_all.append(present & (last_of(source) == last_of(own - 1)))
    linked_all = jnp.stack(linked_all, axis=1).reshape(groups, blocks_each, LAGS)

    def place_of(own, lag):
        return divmod(own - 1 - lag, blocks_each)

    head_of = (jnp.arange(local_width)[:, None] // HD == jnp.arange(local_heads)).astype(WIDE)
    gain_flat = gain_mem.reshape(local_width)

    def head_mean(values):
        return exact_product(values, head_of) / HD

    def head_spread(values):
        return exact_product(values, head_of.T)

    count = groups
    rows = count * local_len
    blocks = count * blocks_each
    part_rows = rows // STREAMS
    part_blocks = blocks // STREAMS

    def own_rows(array):
        sub = array.shape[0] // ranks
        return lax.dynamic_slice_in_dim(array, rank * sub, sub, 0)

    class Stream:
        pass

    def linked(one, square, corner):
        spread = jnp.repeat(one.linked[:, :, LAGS - 2 :: -1], SPAN, axis=2)[:, :, None]
        square = jnp.where(spread, square, jnp.zeros_like(square))
        corner = jnp.where(
            one.linked[:, :, LAGS - 1, None, None], corner, jnp.zeros_like(corner)
        )
        return square, corner

    def packed(square, corner):
        wide = square.shape[-1]
        lanes = corner.transpose(2, 0, 1, 3).reshape(CORNER, -1)
        lanes = jnp.pad(lanes, ((0, 0), (0, wide - lanes.shape[1])))
        return jnp.concatenate([square.reshape(-1, wide), lanes], axis=0)

    def unpacked(array):
        square = array[:-CORNER].reshape(count, blocks_each, SPAN, -1)
        corner = array[-CORNER:, : blocks * CORNER]
        corner = corner.reshape(CORNER, count, blocks_each, CORNER).transpose(1, 2, 0, 3)
        return square, corner

    def begin(one, index):
        def mine(array):
            return array[index * count : (index + 1) * count]

        one.flat = mine(tokens).reshape(rows, width)
        one.upstream_low = mine(out_grad).reshape(rows, width)
        one.labels = mine(labels_all)
        one.lasts = mine(lasts_all)
        one.before = mine(before_all)
        one.linked = mine(linked_all)
        one.keeping = (one.lasts == one.before).astype(WIDE)[:, :, None, None]
        one.writing = (one.labels == one.lasts[:, :, None]).astype(WIDE)[..., None]
        one.reading = (one.labels == one.before[:, :, None]).astype(WIDE)

        def features_of(piece):
            low = norm_rows(piece.astype(WIDE), gain_in_wide)[0].astype(NARROW)
            return low, matmul(low.reshape(rows, width), feature_cols)

        def shaped(values):
            return values.reshape(count, blocks_each, SPAN, local_units)

        low, preact = features_of(mine(tokens))
        one.preact = lax.optimization_barrier(preact)
        one.input_low = low.reshape(rows, width)
        one.features = jax.nn.silu(one.preact).astype(NARROW)
        squares = jnp.sum(jnp.square(one.features.astype(WIDE)), axis=1)
        one.key_scale = lax.rsqrt(summed_over_ranks(squares) + EPSILON)
        far, pair, one.features, one.key_scale = lax.optimization_barrier(
            (mine(far_tokens), mine(pair_tokens), one.features, one.key_scale)
        )
        close = [pair, flipped(far, "ctx", 1)]
        one.around = {0: shaped(one.features)}
        one.features_around = lambda piece: shaped(
            jax.nn.silu(features_of(piece)[1]).astype(NARROW)
        )
        one.next_piece = jnp.where(odd_part, close[1], close[0])
        one.around[-1] = one.features_around(jnp.where(odd_part, close[0], close[1]))
        one.around[2] = one.features_around(far)
        one.around[-2] = one.around[2]
        one.targets = matmul(one.input_low, value_cols).reshape(
            count, blocks_each, SPAN, local_width
        )
        weighted = [(one.around[0].astype(WIDE) * decay).astype(NARROW) for decay in decays]
        products = []
        corners = []
        for own in range(blocks_each):
            row = []
            for lag in range(LAGS - 1, -1, -1):
                delta, place = place_of(own, lag)
                near, past = weighted[lag][:, own], one.around[delta][:, place]
                if lag == LAGS - 1:
                    near, past = near[:, :CORNER], past[:, SPAN - CORNER :]
                    corners.append(batched("sth,suh->stu", near, past))
                else:
                    row.append(batched("sth,suh->stu", near, past))
            products.append(jnp.concatenate(row, axis=2))
        one.products = packed(
            jnp.stack(products, axis=1).astype(NARROW), jnp.stack(corners, axis=1).astype(NARROW)
        )
        one.mixing = lax.psum(one.products, "tp")

    def span_of(own):
        start = (reach * blocks_each - LAGS + own) * SPAN
        return slice(start, start + LAGS * SPAN)

    def remember(one):
        square, corner = linked(one, *unpacked(one.mixing))
        corner = jnp.pad(
            corner, ((0, 0), (0, 0), (0, SPAN - CORNER), (SPAN - CORNER, 0))
        )
        one.mixing = jnp.concatenate([corner, square], axis=3)
        one.scales = one.key_scale.reshape(count, blocks_each, SPAN, 1)
        halos = [
            jnp.zeros((count, blocks_each * SPAN, local_width), NARROW) for _ in range(reach)
        ]
        pending = {}
        for turn in range(parts):
            for hop in range(1, reach + 1):
                if (turn - hop, hop) in pending:
                    halos[reach - hop] = halos[reach - hop] + pending[(turn - hop, hop)]
            known = jnp.concatenate(halos, axis=1)
            recalls = []
            errors = []
            for own in range(blocks_each):
                total = batched("stu,sud->std", one.mixing[:, own], known[:, span_of(own)])
                recall = -step * one.scales[:, own] * total
                error = one.writing[:, own] * (
                    one.keeping[:, own] * recall - one.targets[:, own]
                )
                recalls.append(recall)
                errors.append(error)
                known = jnp.concatenate(
                    [known, (one.scales[:, own] * error).astype(NARROW)], axis=1
                )
            for hop in range(1, reach + 1):
                if turn + hop < parts:
                    pending[(turn, hop)] = passed_along(
                        known[:, reach * blocks_each * SPAN :], "ctx", [(turn, turn + hop)]
                    )
        one.known = known
        one.recall = jnp.stack(recalls, 1)
        one.errors = jnp.stack(errors, 1)
        masked = (one.reading[..., None] * one.recall).reshape(rows, local_width)
        one.head_factor = head_spread(lax.rsqrt(head_mean(masked * masked) + EPSILON))
        one.head_unit = masked * one.head_factor
        retrieved = (one.head_unit * gain_flat).astype(NARROW)
        one.retrieved_full = lax.all_gather(retrieved, "tp", axis=1, tiled=True)

    def attend(one):
        def projected(values, weight):
            return matmul(values, weight).astype(NARROW)

        labels = one.labels.reshape(part_blocks, SPAN)
        reading = one.reading.reshape(part_blocks, SPAN)
        one.operands = (
            projected(one.input_low, query_w),
            projected(one.retrieved_full, key_w),
            projected(one.input_low, key_w),
            projected(one.retrieved_full, value_w),
            projected(one.input_low, value_w),
            fixed_keys,
            fixed_values,
            labels[:, :, None],
            labels[:, None, :],
            reading[:, None, :],
        )
        one.attended = attention(*one.operands)
        one.residual = own_rows(one.flat).astype(WIDE)
        one.branch = scattered(matmul(one.attended, weights["out"]))

    def middle(one):
        if one is not streams[0]:
            one.branch = after(one.branch, streams[0].mid_own)
        one.hidden = one.residual + one.branch
        normed_mid, one.unit_mid, one.factor_mid = norm_rows(one.hidden, gain_ffn_wide)
        one.mid_own = normed_mid.astype(NARROW)
        one.mid_low = collected(one.mid_own)

    def feed(one):
        gate = matmul(one.mid_low, weights["gate"])
        upper = matmul(one.mid_low, weights["up"])
        one.activ = (jax.nn.silu(gate) * upper).astype(NARROW)
        grad_act = by_rows(one.upstream_low, weights["down"])
        one.grad_gate = (grad_act * upper * silu_slope(gate)).astype(NARROW)
        one.grad_upper = (grad_act * jax.nn.silu(gate)).astype(NARROW)
        one.grad_mid = scattered(
            by_rows(one.grad_gate, weights["gate"]) + by_rows(one.grad_upper, weights["up"])
        )

    def middle_back(one):
        if one is not streams[0]:
            one.grad_mid = after(one.grad_mid, streams[0].grad_hidden)
        grad_mid = one.grad_mid
        one.grad_gain_ffn = jnp.sum(grad_mid * one.unit_mid, axis=0)
        upstream = own_rows(one.upstream_low).astype(WIDE)
        one.grad_hidden = upstream + norm_back(
            grad_mid, one.unit_mid, one.factor_mid, gain_ffn_wide
        )
        one.grad_mixed = collected(one.grad_hidden)

    def branch_part(one):
        activ = after(one.activ, last_stream.partial)
        return matmul(activ, weights["down"]).astype(NARROW)

    def rank_major(array):
        array = array.reshape(STREAMS, ranks, -1, width)
        return array.transpose(1, 0, 2, 3).reshape(-1, width)

    def stream_major(array):
        array = array.reshape(ranks, STREAMS, -1, width)
        return array.transpose(1, 0, 2, 3).reshape(-1, width)

    def finish_output(one):
        own = jnp.concatenate([item.hidden + item.branch for item in streams], axis=0)
        one.output = collected(after(own, one.grad_mixing))

    def attend_back(one):
        grad_attended = by_rows(one.grad_mixed, weights["out"]).astype(NARROW)
        (
            one.grad_queries,
            one.key_memory,
            one.key_token,
            one.value_memory,
            one.value_token,
            one.key_fixed,
            one.value_fixed,
        ) = attention_back(*one.operands, grad_attended)
        partial = by_rows(one.key_memory, key_w) + by_rows(one.value_memory, value_w)
        one.partial = partial.astype(NARROW)
        one.grad_retrieved = lax.psum_scatter(one.partial, "tp", scatter_dimension=1, tiled=True)

    def heads_back(one):
        grad_heads = one.grad_retrieved.astype(WIDE)
        one.grad_gain_memory = jnp.sum(grad_heads * one.head_unit, axis=0)
        inner = grad_heads * gain_flat
        grad_masked = one.head_factor * (
            inner - one.head_unit * head_spread(head_mean(inner * one.head_unit))
        )
        one.grad_read = one.reading[..., None] * grad_masked.reshape(
            count, blocks_each, SPAN, local_width
        )

    def remember_back(one):
        later = [0.0] * blocks_each
        pending = {}
        for turn in range(parts):
            if turn == parts // 2:
                later, first_stream.branch = lax.optimization_barrier(
                    (later, first_stream.branch)
                )
            for hop in range(1, reach + 1):
                if (turn - hop, hop) in pending:
                    arrived = pending[(turn - hop, hop)].astype(WIDE)
                    for own in range(blocks_each):
                        later[own] = later[own] + arrived[:, own * SPAN : (own + 1) * SPAN]
            known = [0.0] * (reach * blocks_each) + later
            grad_errors = [None] * blocks_each
            grad_recalls = [None] * blocks_each
            raws = [None] * blocks_each
            for own in range(blocks_each - 1, -1, -1):
                grad_scaled = -step * known[reach * blocks_each + own]
                grad_error = one.scales[:, own] * grad_scaled
                grad_recall = (
                    one.grad_read[:, own] + one.writing[:, own] * one.keeping[:, own] * grad_error
                )
                grad_errors[own] = jnp.broadcast_to(grad_error, grad_recall.shape)
                grad_recalls[own] = grad_recall
                raws[own] = (one.scales[:, own] * grad_recall).astype(NARROW)
                carried = batched("stu,std->sud", one.mixing[:, own], raws[own])
                for index in range(LAGS):
                    place = reach * blocks_each - LAGS + own + index
                    known[place] = (
                        known[place] + carried[:, index * SPAN : (index + 1) * SPAN]
                    )
            for hop in range(1, reach + 1):
                place = parts - 1 - turn
                if place - hop >= 0:
                    start = (reach - hop) * blocks_each
                    sent = jnp.concatenate(known[start : start + blocks_each], axis=1)
                    pending[(turn, hop)] = passed_along(
                        sent.astype(NARROW), "ctx", [(place, place - hop)]
                    )
        grad_errors = jnp.stack(grad_errors, 1)
        grad_recalls = jnp.stack(grad_recalls, 1)
        one.grad_targets = (-one.writing * grad_errors).astype(NARROW).reshape(rows, local_width)
        scale_part = jnp.sum(grad_recalls * one.recall + one.errors * grad_errors, axis=3)
        one.scale_sum = summed_over_ranks(scale_part.reshape(rows))
        grad_mixing = []
        for own in range(blocks_each):
            grad_mixing.append(
                -step * batched("std,sud->stu", raws[own], one.known[:, span_of(own)])
            )
        grad_mixing = jnp.stack(grad_mixing, 1)
        square, corner = linked(
            one, grad_mixing[..., SPAN:], grad_mixing[:, :, :CORNER, SPAN - CORNER : SPAN]
        )
        grad_mixing = packed(square.astype(NARROW), corner.astype(NARROW))
        one.packed_back = grad_mixing
        one.grad_mixing = lax.psum(grad_mixing, "tp")

    def features_back(one):
        square, corner = unpacked(one.grad_mixing)

        def column(own, lag):
            if lag == LAGS - 1:
                return corner[:, own]
            start = (LAGS - 2 - lag) * SPAN
            return square[:, own, :, start : start + SPAN]

        needed = {}
        for hop in range(1, reach + 1):
            sends = [(source, source - hop) for source in range(hop, parts)]
            for last_lag in (False, True):
                pairs = [
                    (own, lag)
                    for own in range(blocks_each)
                    for lag in range(LAGS)
                    if place_of(own, lag)[0] == -hop and (lag == LAGS - 1) == last_lag
                ]
                if not pairs:
                    continue
                moved = passed_along(
                    jnp.stack([column(own, lag) for own, lag in pairs], axis=1), "ctx", sends
                )
                for place, (own, lag) in enumerate(pairs):
                    needed[(hop * blocks_each + own, lag)] = moved[:, place]
        for own in range(blocks_each):
            for lag in range(LAGS):
                needed[(own, lag)] = column(own, lag)
        grad_features = []
        one.grad_decays = [0.0] * LAGS
        rest = SPAN - CORNER
        for own in range(blocks_each):
            total = 0.0
            for lag in range(LAGS):
                own_features = one.around[0][:, own].astype(WIDE)
                delta, place = place_of(own, lag)
                past = one.around[delta][:, place]
                later = own + 1 + lag
                delta, place = divmod(later, blocks_each)
                future = one.around[delta][:, place]
                if lag == LAGS - 1:
                    own_features, past, future = (
                        own_features[:, :CORNER],
                        past[:, rest:],
                        future[:, :CORNER],
                    )
                from_reads = batched("stu,suh->sth", needed[(own, lag)], past)
                one.grad_decays[lag] = one.grad_decays[lag] + jnp.sum(
                    own_features * from_reads, axis=(0, 1)
                )
                from_writes = batched("stu,sth->suh", needed[(later, lag)], future)
                if lag == LAGS - 1:
                    from_reads = jnp.pad(from_reads, ((0, 0), (0, rest), (0, 0)))
                    from_writes = jnp.pad(from_writes, ((0, 0), (rest, 0), (0, 0)))
                total = total + decays[lag] * (from_reads + from_writes)
            grad_features.append(total)
        grad_features = jnp.stack(grad_features, 1).reshape(rows, local_units)
        grad_features = grad_features - (one.key_scale * one.key_scale * one.scale_sum)[
            :, None
        ] * one.features.astype(WIDE)
        one.grad_pre = (grad_features * silu_slope(one.preact)).astype(NARROW)

    def inputs_back(one):
        one.grad_input = (one.early + by_rows(one.grad_pre, feature_cols)).astype(NARROW)

    def input_early(one):
        targets = after(one.grad_targets, one.packed_back)
        one.early = one.early + by_rows(targets, value_cols)

    def tokens_back(one):
        grad_input = one.grad_input
        _, unit_in, factor_in = norm_rows(one.residual, gain_in_wide)
        one.grad_gain_in = jnp.sum(grad_input * unit_in, axis=0)
        grad_own = one.grad_hidden + norm_back(grad_input, unit_in, factor_in, gain_in_wide)
        one.grad_tokens = stream_major(collected(grad_own)).astype(WIDE)

    whole = Stream()
    streams = [Stream() for _ in range(STREAMS)]

    def over(function):
        total = function(streams[0])
        for one in streams[1:]:
            total = total + function(one)
        return total

    def every(stage):
        for one in streams:
            stage(one)

    class Reduction:
        def __init__(self, array, by_row):
            array = array.astype(NARROW)
            *self.lead, self.high, self.wide = array.shape
            self.by_row = by_row
            self.axis = len(self.lead)
            if by_row:
                array = array.reshape(*self.lead, 2, 2, 2, self.high // 8, self.wide)
            else:
                array = array.reshape(2, 2, self.high // 4, self.wide)
            self.array = array
            self.exchange(core, self.axis + 1 if by_row else 0, "ctx", 1)

        def exchange(self, index, axis, over_axis, bit):
            own, other = (pick(self.array, place, axis) for place in (index, 1 - index))
            self.add(own, flipped(other, over_axis, bit))

        def add(self, own, arrived):
            self.array = (own.astype(WIDE) + arrived.astype(WIDE)).astype(NARROW)

        def across(self):
            if self.by_row:
                self.exchange(half_index, self.axis, "shard", 1)
                return
            half = self.wide // 2
            own, other = (
                lax.dynamic_slice_in_dim(self.array, place * half, half, 2)
                for place in (half_index, 1 - half_index)
            )
            self.add(own, flipped(other, "shard", 1))

        def apart(self):
            self.exchange(outer, self.axis if self.by_row else 0, "ctx", 2)

        def together(self):
            pair = either(outer == 0, self.array, flipped(self.array, "ctx", 2))
            self.array = jnp.stack(pair, axis=self.axis if self.by_row else 0)

        def result(self):
            pair = either(core == 0, self.array, flipped(self.array, "ctx", 1))
            array = jnp.stack(pair, axis=self.axis if self.by_row else 0).astype(WIDE)
            if self.by_row:
                return array.reshape(*self.lead, self.high // 2, self.wide)
            return array.reshape(self.high, self.wide // 2)

    def tied(one, names, *reductions):
        held = [getattr(one, name) for name in names]
        held, arrays = lax.optimization_barrier((held, [item.array for item in reductions]))
        for name, value in zip(names, held):
            setattr(one, name, value)
        for item, array in zip(reductions, arrays):
            item.array = array

    class Holder:
        def __init__(self, array):
            self.array = array

    def fetched(one, names, start, *arrays):
        holders = [Holder(flipped(after(item, start), "shard", 1)) for item in arrays]
        tied(one, names, *holders)
        return [holder.array for holder in holders]

    def merged(name):
        setattr(
            whole, name, jnp.concatenate([getattr(one, name) for one in streams], axis=0)
        )

    begin(whole, 0)
    qkv_fetch = Holder(flipped(after(w_qkv, whole.products), "shard", 1))
    tied(whole, ["mixing"], qkv_fetch)
    qkv_other = qkv_fetch.array
    qkv_cols = joined(w_qkv, qkv_other, 1)
    query_w = qkv_cols[0]
    key_w = qkv_cols[1]
    value_w = qkv_cols[2]
    fixed_keys = matmul(persist, key_w).astype(NARROW)
    fixed_values = matmul(persist, value_w).astype(NARROW)
    remember(whole)
    next_features = Holder(whole.features_around(after(whole.next_piece, whole.recall)))
    tied(whole, ["retrieved_full"], next_features)
    whole.around[1] = next_features.array
    out_other, down_other = fetched(whole, ["retrieved_full"], whole.recall, w_out, w_down)
    weights["out"] = joined(w_out, out_other, 1)
    weights["down"] = joined(w_down, down_other, 1)
    for index, one in enumerate(streams):
        for name in ("flat", "upstream_low", "input_low", "retrieved_full", "labels", "reading"):
            array = getattr(whole, name)
            size = array.shape[0] // STREAMS
            setattr(one, name, array[index * size : (index + 1) * size])
        attend(one)
    first_stream, last_stream = streams[0], streams[-1]
    (gate_other,) = fetched(last_stream, ["branch"], first_stream.attended, w_gate_up[0])
    weights["gate"] = joined(w_gate_up[0], gate_other, 0)
    every(middle)
    (up_other,) = fetched(first_stream, ["mid_low"], first_stream.hidden, w_gate_up[1])
    weights["up"] = joined(w_gate_up[1], up_other, 0)
    first_stream.mid_low = after(first_stream.mid_low, last_stream.hidden)
    every(feed)
    first_stream.grad_mid = after(first_stream.grad_mid, last_stream.mid_low)
    feed_reductions = [
        Reduction(over(lambda one: over_rows(one.activ, one.upstream_low)), False),
        Reduction(
            jnp.stack(
                [
                    over(lambda one: over_rows(one.mid_low, one.grad_gate)).astype(NARROW),
                    over(lambda one: over_rows(one.mid_low, one.grad_upper)).astype(NARROW),
                ]
            ),
            True,
        ),
    ]
    every(middle_back)
    first_stream.grad_mixed = after(first_stream.grad_mixed, last_stream.grad_mid)
    for item in feed_reductions:
        item.across()
    attend_back(first_stream)
    tied(last_stream, ["grad_mixed"], *feed_reductions, Holder(first_stream.partial))
    attend_back(last_stream)
    for name in (
        "grad_retrieved",
        "grad_queries",
        "key_token",
        "value_token",
        "key_memory",
        "value_memory",
    ):
        merged(name)
    persist_wide = persist.astype(WIDE)
    key_fixed = over(lambda one: one.key_fixed)
    value_fixed = over(lambda one: one.value_fixed)
    grad_query_w = over_rows(whole.input_low, whole.grad_queries)
    grad_key_w = (
        over_rows(whole.input_low, whole.key_token)
        + over_rows(whole.retrieved_full, whole.key_memory)
        + exact_product(persist_wide.T, key_fixed)
    )
    grad_value_proj = (
        over_rows(whole.input_low, whole.value_token)
        + over_rows(whole.retrieved_full, whole.value_memory)
        + exact_product(persist_wide.T, value_fixed)
    )
    mix_reductions = [
        Reduction(over(lambda one: over_rows(one.attended, one.grad_mixed)), False),
        Reduction(
            jnp.stack(
                [item.astype(NARROW) for item in (grad_query_w, grad_key_w, grad_value_proj)]
            ),
            True,
        ),
    ]
    grad_persist = exact_product(key_fixed, key_w.astype(WIDE).T) + exact_product(
        value_fixed, value_w.astype(WIDE).T
    )
    for item in feed_reductions:
        item.apart()
    early = Holder(
        by_rows(whole.grad_queries, query_w)
        + by_rows(whole.key_token, key_w)
        + by_rows(whole.value_token, value_w)
    )
    branch_parts = [Holder(branch_part(one)) for one in streams]
    tied(
        whole,
        ["grad_retrieved"],
        *feed_reductions,
        *mix_reductions,
        early,
        *branch_parts,
    )
    whole.early = early.array
    first_stream.branch = scattered(branch_parts[0].array)
    heads_back(whole)
    remember_back(whole)
    last_branch = Holder(scattered(branch_parts[-1].array))
    persist_sum = Holder(summed_over_ranks(after(grad_persist, whole.packed_back), NARROW))
    input_early(whole)
    for item in mix_reductions:
        item.array = after(item.array, whole.packed_back)
        item.across()
    tied(
        whole,
        ["grad_mixing", "scale_sum", "early"],
        *mix_reductions,
        persist_sum,
        last_branch,
    )
    last_stream.branch = last_branch.array
    finish_output(whole)
    features_back(whole)
    inputs_back(whole)
    whole.grad_input_low, whole.output = lax.optimization_barrier(
        (rank_major(whole.grad_input), whole.output)
    )
    whole.grad_input = scattered(whole.grad_input_low)
    merged("residual")
    merged("grad_hidden")

    grad_decays = whole.grad_decays
    grad_retain = 0.0
    grad_moment = 0.0
    retain_slope = jnp.zeros_like(retain)
    for lag in range(1, LAGS):
        retain_slope = retain * retain_slope + decays[lag - 1]
        moment_slope = 0.0
        for power in range(1, lag + 1):
            moment_slope = moment_slope + power * retain ** (lag - power) * moment ** (power - 1)
        grad_retain = grad_retain + retain_slope * grad_decays[lag]
        grad_moment = grad_moment + moment_slope * grad_decays[lag]
    grad_rates = jnp.stack([grad_retain, grad_moment])

    def summed(pieces):
        small = jnp.concatenate([piece.reshape(-1) for piece in pieces])
        for axis, bit in (("ctx", 1), ("shard", 1), ("ctx", 2)):
            small = small + flipped(small, axis, bit)
        return small

    small = Holder(summed([persist_sum.array, whole.grad_gain_memory, grad_rates]))
    feature_reduction = Reduction(over_rows(whole.input_low, whole.grad_pre), True)
    grad_targets = after(whole.grad_targets, whole.grad_input_low)
    target_reduction = Reduction(over_rows(whole.input_low, grad_targets), True)
    late_reductions = [feature_reduction, target_reduction]
    for item in feed_reductions:
        item.array = after(item.array, whole.grad_input_low)
        item.together()
    for item in mix_reductions:
        item.apart()
    for item in late_reductions:
        item.across()
    tied(
        whole,
        ["grad_input"],
        small,
        *feed_reductions,
        *mix_reductions,
        *late_reductions,
    )
    tokens_back(whole)
    for item in mix_reductions:
        item.together()
    for item in late_reductions:
        item.apart()
        item.together()
    gains = summed([whole.grad_gain_in, over(lambda one: one.grad_gain_ffn)])
    gain_in_sum, gain_ffn_sum = summed_over_ranks(gains).reshape(2, width)
    cut = persist_sum.array.size
    middle_cut = cut + local_width
    grad_persist = small.array[:cut].reshape(persist_count, width)
    grad_gain_memory = small.array[cut:middle_cut].reshape(local_heads, HD)
    grad_rates = small.array[middle_cut:].reshape(2, local_units)
    grad_down, grad_gate_up = [item.result() for item in feed_reductions]
    grad_out_rows, grad_qkv = [item.result() for item in mix_reductions]
    grad_feature_w, grad_target_w = [item.result() for item in late_reductions]

    def own_half(array, axis):
        size = array.shape[axis] // 2
        return lax.dynamic_slice_in_dim(array, half_index * size, size, axis)

    return (
        stream_major(whole.output).reshape(tokens.shape),
        whole.grad_tokens.reshape(tokens.shape),
        own_half(gain_in_sum, 0),
        own_half(gain_ffn_sum, 0),
        own_half(grad_gain_memory, 1),
        own_half(grad_rates, 0),
        own_half(grad_persist, 1),
        grad_qkv,
        grad_out_rows,
        grad_target_w,
        grad_feature_w,
        grad_gate_up,
        grad_down,
    )


def solution(mesh):
    placed = (
        P("shard", "ctx", None),
        P("shard", "ctx"),
        P("shard"),
        P("shard"),
        P("tp", "shard"),
        P("shard", None),
        P(None, "shard"),
        P(None, "shard", "tp"),
        P("tp", "shard"),
        P("shard", "tp"),
        P("shard", "tp"),
        P(None, "shard", "tp"),
        P("tp", "shard"),
        P("shard", "ctx", None),
    )
    return jax.shard_map(
        on_device,
        mesh=mesh,
        in_specs=placed,
        out_specs=(
            P("shard", "ctx", None),
            P("shard", "ctx", None),
            P("shard"),
            P("shard"),
            P("tp", "shard"),
            P("shard", "tp"),
            P(None, "shard"),
            P(None, "shard", "tp"),
            P("tp", "shard"),
            P("shard", "tp"),
            P("shard", "tp"),
            P(None, "shard", "tp"),
            P("tp", "shard"),
        ),
        check_vma=False,
    )
```
